32 devices in a mesh: wide: 16 (over z, x, core), narrow: 2 (over y).
Axes of the slice: x: 2, y: 2, z: 4, core: 2. Of those that a mesh axis runs over, the one named last changes fastest.
Arguments:
- dosage: bfloat16 [2048, 32768], P(None, 'wide'), may hold values from -4 to 6, as said below
- annotations: int32 [128, 32768], P(None, 'wide'), may hold values from 0 to 1, as said below
- test_statistic_table: float32 [32768, 512], P('wide', 'narrow'), may hold values from 0 to 200
Outputs:
- ld_scores: float32 [128, 32768], P(None, ('wide', 'narrow'))
- fitted: float32 [32768, 512], P('wide', 'narrow')
The draws below stay inside these ranges and needn't reach their ends.
Inputs may be any that keep to these rules, and one draw needn't show every extreme that they name: `dosage`: dosages of each variant follow a correlated process along the variants. `annotations`: 1 where a variant belongs to an annotation.
All inputs are finite; a program needn't handle non-finite values.
Results may differ from the reference program's by a relative error of at most 0.0023.
Values may be sent and summed in bfloat16 or wider, within the bound.
No kernel may reach another device: no remote copies, remote signals or barrier semaphores. Data moves between devices by JAX's collectives and lax.ppermute only.
A program may use at most 128 MiB of HBM per device.

```python
import jax
import jax.numpy as jnp
from jax import lax

SAMPLES = 2048
HALF = 1024
ANNOT = 128
TRAITS = 512
LOCUS_COUNT = 32768


def shared_rates(key):
    ambient_seed, maximum_seed, elevated_random_stream = jax.random.split(jax.random.fold_in(key, 101), 3)
    typical_exchange_intensity = jnp.exp(jax.random.uniform(ambient_seed, (LOCUS_COUNT,), minval=jnp.log(0.1 / HALF), maxval=jnp.log(3.0 / HALF)))
    exchange_ceiling = jax.random.uniform(maximum_seed, (LOCUS_COUNT,)) < 4.0 / HALF
    elevated_exchange_profile = jax.random.uniform(elevated_random_stream, (LOCUS_COUNT,), minval=0.2, maxval=0.7)
    return typical_exchange_intensity + jnp.where(exchange_ceiling, elevated_exchange_profile, 0.0)


def shared_annotations(key):
    ambient_seed, key_mult, key_member = jax.random.split(jax.random.fold_in(key, 202), 3)
    base_level = jax.random.randint(ambient_seed, (ANNOT, 1), 40, 200)
    multiplier = jax.random.randint(key_mult, (ANNOT, LOCUS_COUNT // (2 * HALF)), 1, 4)
    thresh = jnp.repeat(multiplier, 2 * HALF, axis=1) * base_level
    uniform_draw = jax.random.randint(key_member, (ANNOT, LOCUS_COUNT), 0, 1024)
    return (uniform_draw < thresh).astype(jnp.int32)


def draw_annotations(key, part):
    return shared_annotations(key)


def draw_dosage(key, part):
    persist = jnp.exp(-shared_rates(key))
    keys = jax.random.split(jax.random.fold_in(key, 303), 6)
    fresh_noise_term = jax.random.normal(keys[0], (LOCUS_COUNT, SAMPLES))
    initial = jax.random.normal(keys[1], (SAMPLES,))

    def advance(state_now, inputs):
        factor, fresh = inputs
        following = factor * state_now + jnp.sqrt(1.0 - factor * factor) * fresh
        return (following, following)
    unused, latent = lax.scan(advance, initial, (persist, fresh_noise_term))
    latent = jnp.clip(latent, -5.0, 5.0)
    offset = jax.random.uniform(keys[4], (LOCUS_COUNT,), minval=0.2, maxval=1.8)
    scales = jnp.exp(jax.random.uniform(keys[5], (LOCUS_COUNT,), minval=jnp.log(0.2), maxval=jnp.log(0.6)))
    values = jnp.clip(offset[:, None] + scales[:, None] * latent, -4.0, 6.0)
    return values.T.astype(jnp.bfloat16)


def draw_test_statistic_table(key, part):
    decay = jnp.exp(-2.0 * shared_rates(key))
    member = shared_annotations(key).astype(jnp.float32).T
    member = member - jnp.mean(member, axis=0)[None, :]

    def carry_on(state_now, inputs):
        factor, fresh = inputs
        following = factor * state_now + fresh
        return (following, following)
    zeros_row = jnp.zeros((ANNOT,), jnp.float32)
    unused, forward = lax.scan(carry_on, zeros_row, (decay, member))
    next_decay = jnp.concatenate([decay[1:], jnp.zeros((1,), jnp.float32)])
    unused_back, backward = lax.scan(carry_on, zeros_row, (next_decay, member), reverse=True)
    proxy = forward + backward - member
    proxy = proxy / (jnp.std(proxy, axis=0)[None, :] + 0.001)
    keys = jax.random.split(jax.random.fold_in(key, 404), 6)
    effects = jax.random.normal(keys[0], (ANNOT, TRAITS)) / jnp.sqrt(float(ANNOT))
    signal = jnp.tanh(jnp.dot(proxy, effects, precision=lax.Precision.HIGHEST))
    position = jnp.arange(LOCUS_COUNT, dtype=jnp.float32) / LOCUS_COUNT
    row_scale = (1.0 + 2.0 * position) / 3.0 * jnp.exp(jax.random.uniform(keys[1], (LOCUS_COUNT,), minval=0.0, maxval=jnp.log(10.0)))
    col_scale = jnp.exp(jax.random.uniform(keys[2], (TRAITS,), minval=jnp.log(0.3), maxval=jnp.log(3.0)))
    gauss = jnp.clip(jax.random.normal(keys[5], (LOCUS_COUNT, TRAITS)), -4.0, 4.0)
    baseline = 0.3 + gauss * gauss
    values = row_scale[:, None] * col_scale[None, :] * baseline * (1.0 + 0.6 * signal) / 4.0
    return jnp.clip(values, 0.0, 200.0).astype(jnp.float32)


def setup_inputs(seed: int = 0) -> dict:
    key_of = jax.random.split(jax.random.key(seed), 4)
    dosage = draw_dosage(jax.random.fold_in(key_of[3], 71), 0)
    annotations = draw_annotations(jax.random.fold_in(key_of[3], 71), 0)
    test_statistic_table = draw_test_statistic_table(jax.random.fold_in(key_of[3], 71), 0)
    return {"dosage": dosage, "annotations": annotations, "test_statistic_table": test_statistic_table}


highest_precision = lax.Precision.HIGHEST

def band_weights(col_geno, row_geno, col_start, row_start, total_variants):
    products = lax.dot_general(col_geno.astype(jnp.float32), row_geno.astype(jnp.float32), (((0,), (0,)), ((), ())), preferred_element_type=jnp.float32)
    samples = row_geno.shape[0]
    correlation = products / samples
    squared = correlation * correlation
    adjusted = squared - (1.0 - squared) / (samples - 2)
    col_index = col_start + jnp.arange(col_geno.shape[1], dtype=jnp.int32)[:, None]
    row_index = row_start + jnp.arange(row_geno.shape[1], dtype=jnp.int32)[None, :]
    inside = (jnp.abs(row_index - col_index) <= HALF) & (col_index >= 0) & (col_index < total_variants)
    return jnp.where(inside, adjusted, 0.0).astype(jnp.bfloat16)

def reference(dosage, annotations, test_statistic_table):
    values = dosage.astype(jnp.float32)
    average = lax.optimization_barrier(jnp.mean(values, axis=0))
    centred_values = values - average[None, :]
    variance = lax.optimization_barrier(jnp.mean(centred_values * centred_values, axis=0))
    standard = (centred_values / jnp.sqrt(variance + 1e-05)[None, :]).astype(jnp.bfloat16)
    shares = lax.optimization_barrier(jnp.sum(annotations.astype(jnp.float32), axis=1)) / LOCUS_COUNT
    centred = (annotations.astype(jnp.float32) - shares[:, None]).astype(jnp.bfloat16)
    padded_geno = jnp.pad(standard, ((0, 0), (HALF, HALF)))
    padded_annot = jnp.pad(centred, ((0, 0), (HALF, HALF)))

    def strip_block(block):
        start = (block * HALF).astype(jnp.int32)
        own_rows = lax.dynamic_slice_in_dim(standard, start, HALF, 1)
        col_geno = lax.dynamic_slice_in_dim(padded_geno, start, 3 * HALF, 1)
        col_annot = lax.dynamic_slice_in_dim(padded_annot, start, 3 * HALF, 1)
        weights = band_weights(col_geno, own_rows, start - HALF, start, LOCUS_COUNT)
        return jnp.dot(col_annot.astype(jnp.float32), weights.astype(jnp.float32), preferred_element_type=jnp.float32)
    blocks = lax.map(strip_block, jnp.arange(LOCUS_COUNT // HALF, dtype=jnp.int32))
    scores = jnp.transpose(blocks, (1, 0, 2)).reshape(ANNOT, LOCUS_COUNT)
    score_mean = lax.optimization_barrier(jnp.sum(scores, axis=1)) / LOCUS_COUNT
    deviation = scores - score_mean[:, None]
    score_var = lax.optimization_barrier(jnp.sum(deviation * deviation, axis=1)) / LOCUS_COUNT
    ld_scores = deviation / jnp.sqrt(score_var + 1e-05)[:, None]
    chi_mean = lax.optimization_barrier(jnp.sum(test_statistic_table, axis=0)) / LOCUS_COUNT
    gram_matrix = jnp.dot(ld_scores.astype(jnp.float32), ld_scores.T.astype(jnp.float32), precision=highest_precision, preferred_element_type=jnp.float32) / LOCUS_COUNT
    projection = jnp.dot(ld_scores.astype(jnp.float32), (test_statistic_table - chi_mean[None, :]).astype(jnp.float32), precision=highest_precision, preferred_element_type=jnp.float32) / LOCUS_COUNT
    coefficient = jnp.linalg.solve(gram_matrix, projection)
    fitted = chi_mean[None, :] + jnp.dot(ld_scores.T.astype(jnp.float32), coefficient.astype(jnp.float32), precision=highest_precision, preferred_element_type=jnp.float32)
    return (ld_scores, fitted)
```

```python
import functools

import jax
import jax.numpy as jnp
from jax import lax
from jax.experimental import pallas as pl
from jax.experimental.pallas import tpu as pltpu
from jax.sharding import PartitionSpec as P

HALF = 1024
EPS = 1e-05
TILE = 256
ROWS = 256
PAD = 8

highest_precision = lax.Precision.HIGHEST
both = ("wide", "narrow")


def standardized(read, write, samples):
    def folded(values):
        return jnp.sum(values.reshape(-1, 8, values.shape[-1]), axis=0)

    def total(r, carry):
        return carry + folded(read(r).astype(jnp.float32))

    steps = samples // ROWS
    empty = jnp.zeros((8, TILE), jnp.float32)
    mean = jnp.sum(lax.fori_loop(0, steps, total, empty), axis=0, keepdims=True) / samples

    def spread(r, carry):
        away = read(r).astype(jnp.float32) - mean
        return carry + folded(away * away)

    variance = jnp.sum(lax.fori_loop(0, steps, spread, empty), axis=0, keepdims=True) / samples
    scale = 1.0 / jnp.sqrt(variance + EPS)

    def store(r, carry):
        write(r, ((read(r).astype(jnp.float32) - mean) * scale).astype(jnp.bfloat16))
        return carry

    lax.fori_loop(0, steps, store, 0)


def adjusted(products, samples):
    correlation = products * (1.0 / samples)
    squared = correlation * correlation
    return squared - (1.0 - squared) * (1.0 / (samples - 2))


def tile_iota(axis):
    return lax.broadcasted_iota(jnp.int32, (TILE, TILE), axis)


def rows_at(r):
    return pl.ds(pl.multiple_of(r * ROWS, ROWS), ROWS)


def cols_at(c):
    return pl.ds(pl.multiple_of(c * TILE, TILE), TILE)


def strip_kernel(n_ref, dosage_ref, annot_ref, sums_ref, own_ref, geno, turned):
    samples, strip = dosage_ref.shape
    tiles = strip // TILE
    mine = tiles // 2
    n = n_ref[0]

    def standardize(c, carry):
        def write(r, value):
            geno[c, rows_at(r), :] = value

        standardized(lambda r: dosage_ref[rows_at(r), cols_at(c)], write, samples)
        return carry

    lax.fori_loop(0, tiles, standardize, 0)
    sums_ref[...] = jnp.zeros_like(sums_ref)

    def own(t, carry):
        column = n * mine + t
        own_ref[t] = geno[column]
        turned[...] = geno[column].T
        annot = annot_ref[:, cols_at(column)]
        for y in range(mine):
            products = jnp.dot(turned[...], geno[n * mine + y], preferred_element_type=jnp.float32)
            weights = adjusted(products, samples).astype(jnp.bfloat16)
            sums_ref[:, y * TILE : (y + 1) * TILE] += jnp.dot(
                annot, weights, preferred_element_type=jnp.float32
            )
        return carry

    lax.fori_loop(0, mine, own, 0)
    sign = 1 - 2 * n
    offset = tile_iota(0) - tile_iota(1)

    def other(t, carry):
        column = (1 - n) * mine + t
        turned[...] = geno[column].T
        annot = annot_ref[:, cols_at(column)]
        for y in range(mine):

            @pl.when(sign * (t - y) <= 0)
            def _(y=y):
                products = jnp.dot(
                    turned[...], geno[n * mine + y], preferred_element_type=jnp.float32
                )
                inside = sign * (offset + (t - y) * TILE) <= 0
                weights = jnp.where(inside, adjusted(products, samples), 0.0).astype(jnp.bfloat16)
                sums_ref[:, y * TILE : (y + 1) * TILE] += jnp.dot(
                    annot, weights, preferred_element_type=jnp.float32
                )

        return carry

    lax.fori_loop(0, mine, other, 0)


def strip_sums(n, dosage, annot):
    samples, strip = dosage.shape
    mine = strip // (2 * TILE)
    return pl.pallas_call(
        strip_kernel,
        out_shape=(
            jax.ShapeDtypeStruct((annot.shape[0], strip // 2), jnp.float32),
            jax.ShapeDtypeStruct((mine, samples, TILE), jnp.bfloat16),
        ),
        in_specs=[
            pl.BlockSpec(memory_space=pltpu.SMEM),
            pl.BlockSpec(memory_space=pltpu.VMEM),
            pl.BlockSpec(memory_space=pltpu.VMEM),
        ],
        out_specs=(
            pl.BlockSpec(memory_space=pltpu.VMEM),
            pl.BlockSpec(memory_space=pltpu.VMEM),
        ),
        scratch_shapes=[
            pltpu.VMEM((2 * mine, samples, TILE), jnp.bfloat16),
            pltpu.VMEM((TILE, samples), jnp.bfloat16),
        ],
        cost_estimate=pl.CostEstimate(
            flops=2 * samples * strip * strip // 2,
            bytes_accessed=2 * samples * strip * 3 // 2,
            transcendentals=0,
        ),
        name="strip_sums",
    )(n, dosage, annot)


def rim_kernel(order, n_ref, arrived_ref, own_ref, annot_ref, sums_in, sums_ref, back_ref, geno, turned):
    samples = geno.shape[0]
    mine = own_ref.shape[0]
    n = n_ref[0]

    def write(r, value):
        geno[rows_at(r), :] = value

    standardized(lambda r: arrived_ref[rows_at(r), :], write, samples)
    turned[...] = geno[...].T
    arrived_annot = arrived_ref[samples:, :]
    sums_ref[...] = sums_in[...]
    back_ref[...] = jnp.zeros_like(back_ref)
    sign = 1 - 2 * n
    base = (1 - n) * (mine - 1 - order) + n * order
    offset = tile_iota(1) - tile_iota(0)
    for y in range(mine):
        covered = jnp.where(n == 0, y <= base, (y >= base) & (y < mine // 2))

        @pl.when(covered)
        def _(y=y):
            products = jnp.dot(turned[...], own_ref[y], preferred_element_type=jnp.float32)
            inside = sign * (offset + (y - base) * TILE) <= 0
            weights = jnp.where(inside, adjusted(products, samples), 0.0).astype(jnp.bfloat16)
            sums_ref[:, y * TILE : (y + 1) * TILE] += jnp.dot(
                arrived_annot, weights, preferred_element_type=jnp.float32
            )
            back_ref[...] += lax.dot_general(
                annot_ref[:, cols_at(n * mine + y)],
                weights,
                (((1,), (1,)), ((), ())),
                preferred_element_type=jnp.float32,
            )


def rim_sums(order, n, arrived, own, annot, sums):
    mine, samples, _ = own.shape
    return pl.pallas_call(
        functools.partial(rim_kernel, order),
        out_shape=(
            jax.ShapeDtypeStruct(sums.shape, jnp.float32),
            jax.ShapeDtypeStruct((sums.shape[0], TILE), jnp.float32),
        ),
        in_specs=[pl.BlockSpec(memory_space=pltpu.SMEM)]
        + [pl.BlockSpec(memory_space=pltpu.VMEM)] * 4,
        out_specs=(
            pl.BlockSpec(memory_space=pltpu.VMEM),
            pl.BlockSpec(memory_space=pltpu.VMEM),
        ),
        scratch_shapes=[
            pltpu.VMEM((samples, TILE), jnp.bfloat16),
            pltpu.VMEM((TILE, samples), jnp.bfloat16),
        ],
        input_output_aliases={4: 0},
        cost_estimate=pl.CostEstimate(
            flops=2 * samples * TILE * mine * TILE,
            bytes_accessed=2 * samples * TILE * (mine + 1),
            transcendentals=0,
        ),
        name="rim_sums",
    )(n, arrived, own, annot, sums)


def flipped(value, axis, bit):
    length = lax.axis_size(axis)
    return lax.ppermute(value, axis, [(i, i ^ bit) for i in range(length)])


def wide_bits():
    length = lax.axis_size("wide")
    bits = []
    bit = 1
    while bit < length:
        bits.append(bit)
        bit *= 2
    return bits


def wide_sum(value):
    for bit in wide_bits():
        value = value + flipped(value, "wide", bit)
    return value


def split_wide_sum(value):
    half = value.shape[0] // 2
    low = lax.axis_index("wide") % 2
    kept = lax.dynamic_slice_in_dim(value, low * half, half, 0)
    given = lax.dynamic_slice_in_dim(value, (1 - low) * half, half, 0)
    kept = kept + flipped(given, "wide", 1)
    for bit in wide_bits()[1:]:
        kept = kept + flipped(kept, "wide", bit)
    other = flipped(kept, "wide", 1)
    return jnp.where(
        low == 0, jnp.concatenate([kept, other], 0), jnp.concatenate([other, kept], 0)
    )


def shards(dosage, annotations, test_statistic_table):
    samples, strip = dosage.shape
    annots = annotations.shape[0]
    traits = test_statistic_table.shape[1]
    wide = lax.axis_size("wide")
    total_variants = wide * strip
    w = lax.axis_index("wide")
    n = lax.axis_index("narrow")
    block = strip // 2
    n_array = jnp.reshape(n, (1,)).astype(jnp.int32)

    annot = jnp.concatenate(
        [
            annotations.astype(jnp.bfloat16),
            jnp.ones((1, strip), jnp.bfloat16),
            jnp.zeros((PAD - 1, strip), jnp.bfloat16),
        ],
        axis=0,
    )
    rim_pairs = []
    for i in range(wide - 1):
        rim_pairs += [(2 * i, 2 * i + 2), (2 * i + 3, 2 * i + 1)]
    back_pairs = []
    for i in range(wide - 1):
        back_pairs += [(2 * i + 1, 2 * i + 2), (2 * i + 2, 2 * i + 1)]
    arrived = []
    for order in range(2):
        start = jnp.where(n == 0, strip - (order + 1) * TILE, order * TILE)
        outgoing = jnp.concatenate(
            [
                lax.dynamic_slice_in_dim(dosage, start, TILE, 1),
                lax.dynamic_slice_in_dim(annot, start, TILE, 1),
            ],
            axis=0,
        )
        arrived.append(lax.ppermute(outgoing, both, rim_pairs))

    chi = test_statistic_table
    chi_own = lax.dynamic_slice_in_dim(chi, n * block, block, 0)
    chi_other = flipped(lax.dynamic_slice_in_dim(chi, (1 - n) * block, block, 0), "narrow", 1)

    counts = jnp.sum(annotations, axis=1).astype(jnp.float32)
    chi_local = jnp.sum(chi, axis=0)
    early = wide_sum(jnp.concatenate([counts, chi_local]))
    shares = early[:annots] / total_variants
    chi_mean = early[annots:] / total_variants
    chi_mean_other = flipped(chi_mean, "narrow", 1)

    sums, own = strip_sums(n_array, dosage, annot)
    back = []
    for order in range(2):
        sums, part = rim_sums(order, n_array, arrived[order], own, annot, sums)
        back.append(lax.ppermute(part, both, back_pairs))
    empty = jnp.zeros((annot.shape[0], block - 2 * TILE), jnp.float32)
    sums = sums + jnp.where(
        n == 0,
        jnp.concatenate([back[0], back[1], empty], axis=1),
        jnp.concatenate([empty, back[1], back[0]], axis=1),
    )

    high = lax.reduce_precision(1.0 - shares, 8, 7)[:, None]
    low = lax.reduce_precision(0.0 - shares, 8, 7)[:, None]
    members = sums[:annots]
    scores = high * members + low * (sums[annots : annots + 1] - members)

    block_mean = jnp.mean(scores, axis=1)
    deviation = scores - block_mean[:, None]
    cross = lax.dot_general(
        deviation,
        deviation,
        (((1,), (1,)), ((), ())),
        precision=highest_precision,
        preferred_element_type=jnp.float32,
    )
    proj_own = jnp.dot(
        scores, chi_own - chi_mean[None, :], precision=highest_precision,
        preferred_element_type=jnp.float32,
    )
    proj_other = jnp.dot(
        scores, chi_other - chi_mean_other[None, :], precision=highest_precision,
        preferred_element_type=jnp.float32,
    )
    blocks = 2 * wide
    slots = jnp.where(
        jnp.arange(blocks)[:, None] == 2 * w + n, block_mean[None, :], 0.0
    )
    payload = jnp.concatenate([cross, slots], axis=0)
    payload = payload + flipped(payload, "narrow", 1)
    payload = split_wide_sum(payload)
    projection = proj_own + flipped(proj_other, "narrow", 1)
    projection = split_wide_sum(projection)
    scores_other = flipped(scores, "narrow", 1)

    means = payload[annots:]
    score_mean = jnp.mean(means, axis=0)
    between = means - score_mean[None, :]
    covariance = (
        payload[:annots]
        + block
        * lax.dot_general(
            between,
            between,
            (((0,), (0,)), ((), ())),
            precision=highest_precision,
            preferred_element_type=jnp.float32,
        )
    ) / total_variants
    spread = jnp.sqrt(jnp.diagonal(covariance) + EPS)
    gram_matrix = covariance / (spread[:, None] * spread[None, :])
    projection = projection / total_variants / spread[:, None]
    factor = jnp.linalg.cholesky(gram_matrix)
    coefficient = jax.scipy.linalg.cho_solve((factor, True), projection)
    own_scores = (scores - score_mean[:, None]) / spread[:, None]
    other_scores = (scores_other - score_mean[:, None]) / spread[:, None]

    def fit(values):
        return chi_mean[None, :] + lax.dot_general(
            values,
            coefficient,
            (((0,), (0,)), ((), ())),
            precision=highest_precision,
            preferred_element_type=jnp.float32,
        )

    first = fit(jnp.where(n == 0, own_scores, other_scores))
    second = fit(jnp.where(n == 0, other_scores, own_scores))
    return (own_scores, jnp.concatenate([first, second], axis=0))


def solution(mesh):
    in_specs = (P(None, "wide"), P(None, "wide"), P("wide", "narrow"))
    out_specs = (P(None, both), P("wide", "narrow"))
    return jax.shard_map(shards, mesh=mesh, in_specs=in_specs, out_specs=out_specs, check_vma=False)
```

```python
import functools

import jax
import jax.numpy as jnp
from jax import lax
from jax.experimental import pallas as pl
from jax.experimental.pallas import tpu as pltpu
from jax.sharding import PartitionSpec as P

HALF = 1024
EPS = 1e-05
TILE = 256
LANES = 128
ROWS = 256
PAD = 8
VMEM_LIMIT = 36 * 1024 * 1024

highest_precision = lax.Precision.HIGHEST
both = ("wide", "narrow")
in_vmem = pl.BlockSpec(memory_space=pltpu.VMEM)
in_smem = pl.BlockSpec(memory_space=pltpu.SMEM)


def cols_at(c):
    return pl.ds(pl.multiple_of(c * TILE, TILE), TILE)


def standardized(read, write, wide_values, samples):
    steps = samples // ROWS
    empty = jnp.zeros((4 * PAD, TILE), jnp.float32)

    def folded(values):
        return jnp.sum(values.reshape(-1, 4 * PAD, TILE), axis=0)

    def rows_at(r):
        return pl.ds(pl.multiple_of(r * ROWS, ROWS), ROWS)

    def total(r, carry):
        values = read(rows_at(r)).astype(jnp.float32)
        wide_values[rows_at(r), :] = values
        return carry + folded(values)

    mean = jnp.sum(lax.fori_loop(0, steps, total, empty), axis=0, keepdims=True) / samples

    def squares(r, carry):
        away = wide_values[rows_at(r), :] - mean
        return carry + folded(away * away)

    variance = jnp.sum(lax.fori_loop(0, steps, squares, empty), axis=0, keepdims=True) / samples
    scale = 1.0 / jnp.sqrt(variance + EPS)

    def store(r, carry):
        write(rows_at(r), ((wide_values[rows_at(r), :] - mean) * scale).astype(jnp.bfloat16))
        return carry

    lax.fori_loop(0, steps, store, 0)


def into(geno, tile):
    def write(rows, value):
        geno[2 * tile, rows, :] = value[:, :LANES]
        geno[2 * tile + 1, rows, :] = value[:, LANES:]

    return write


def columns_of(geno, tile):
    return jnp.concatenate([geno[2 * tile], geno[2 * tile + 1]], axis=1)


def rows_of(turned, tile):
    return jnp.concatenate([turned[tile, k] for k in range(turned.shape[1])], axis=1)


def band_weights(rows, columns, inside=None):
    samples = rows.shape[1]
    products = jnp.dot(rows, columns, preferred_element_type=jnp.float32)
    unit = 1.0 / (samples - 2)
    weights = products * products * ((1.0 + unit) / (samples * samples)) - unit
    if inside is not None:
        weights = jnp.where(inside, weights, 0.0)
    return weights.astype(jnp.bfloat16)


def along_rows(annot, weights):
    return jnp.dot(annot, weights, preferred_element_type=jnp.float32)


def along_columns(annot, weights):
    return lax.dot_general(
        annot, weights, (((1,), (1,)), ((), ())), preferred_element_type=jnp.float32
    )


def tile_offset():
    shape = (TILE, TILE)
    return lax.broadcasted_iota(jnp.int32, shape, 0) - lax.broadcasted_iota(jnp.int32, shape, 1)


def sizes(dosage):
    samples, strip = dosage.shape
    return samples, strip, strip // (2 * TILE)


def outgoing_kernel(n_ref, dosage_ref, annot_ref, out_ref):
    samples = dosage_ref.shape[0]
    annots = annot_ref.shape[0]
    out_ref[:samples, :] = dosage_ref[...]
    out_ref[samples : samples + annots, :] = (
        annot_ref[...].astype(jnp.float32).astype(jnp.bfloat16)
    )
    row = lax.broadcasted_iota(jnp.int32, (PAD, TILE), 0)
    out_ref[samples + annots :, :] = jnp.where(row == 0, 1.0, 0.0).astype(jnp.bfloat16)


def outgoing_columns(order, n, dosage, annotations):
    samples, strip, _ = sizes(dosage)
    annots = annotations.shape[0]
    last = strip // TILE - 1
    rows = samples + annots + PAD

    def picked(i, n_ref):
        return (0, (1 - n_ref[0]) * (last - order) + n_ref[0] * order)

    return pl.pallas_call(
        outgoing_kernel,
        out_shape=jax.ShapeDtypeStruct((rows, TILE), jnp.bfloat16),
        grid_spec=pltpu.PrefetchScalarGridSpec(
            num_scalar_prefetch=1,
            grid=(1,),
            in_specs=[
                pl.BlockSpec((samples, TILE), picked),
                pl.BlockSpec((annots, TILE), picked),
            ],
            out_specs=pl.BlockSpec((rows, TILE), lambda i, n_ref: (0, 0)),
        ),
        compiler_params=pltpu.CompilerParams(vmem_limit_bytes=VMEM_LIMIT),
        cost_estimate=pl.CostEstimate(flops=0, bytes_accessed=4 * rows * TILE, transcendentals=0),
        name="outgoing",
    )(n, dosage, annotations)


def own_kernel(n_ref, dosage_ref, annot_ref, sums_ref, turned_ref, geno, wide_values):
    samples, block = dosage_ref.shape
    mine = block // TILE
    n = n_ref[0]

    def standardize(t, carry):
        standardized(lambda rows: dosage_ref[rows, cols_at(t)], into(geno, t), wide_values, samples)
        for k in range(samples // LANES):
            for part in range(2):
                turned_ref[t, k, part * LANES : (part + 1) * LANES, :] = geno[
                    2 * t + part, k * LANES : (k + 1) * LANES, :
                ].T
        return carry

    lax.fori_loop(0, mine, standardize, 0)
    sums_ref[...] = jnp.zeros_like(sums_ref)
    for y in range(mine):
        for x in range(y + 1):
            weights = band_weights(rows_of(turned_ref, x), columns_of(geno, y))
            sums_ref[:, y * TILE : (y + 1) * TILE] += along_rows(
                annot_ref[:, cols_at(n * mine + x)], weights
            )
            if x < y:
                sums_ref[:, x * TILE : (x + 1) * TILE] += along_columns(
                    annot_ref[:, cols_at(n * mine + y)], weights
                )


def other_kernel(n_ref, dosage_ref, annot_ref, turned_ref, sums_in, sums_ref, geno, wide_values):
    samples, block = dosage_ref.shape
    mine = block // TILE
    n = n_ref[0]

    def standardize(t, carry):
        standardized(lambda rows: dosage_ref[rows, cols_at(t)], into(geno, t), wide_values, samples)
        return carry

    lax.fori_loop(0, mine, standardize, 0)
    sums_ref[...] = sums_in[...]
    inside = (1 - 2 * n) * tile_offset() >= 0
    for high in range(mine):
        for low in range(high + 1):
            theirs = low + n * (high - low)
            ours = high - n * (high - low)
            weights = band_weights(
                rows_of(turned_ref, ours),
                columns_of(geno, theirs),
                inside if low == high else None,
            )
            sums_ref[:, cols_at(ours)] += along_columns(
                annot_ref[:, cols_at((1 - n) * mine + theirs)], weights
            )


def strip_sums(n, dosage, annot):
    samples, strip, mine = sizes(dosage)
    block = strip // 2
    work = 2 * samples * TILE * TILE * mine * (mine + 1) // 2
    sums_type = jax.ShapeDtypeStruct((annot.shape[0], block), jnp.float32)
    turned_type = jax.ShapeDtypeStruct((mine, samples // LANES, TILE, LANES), jnp.bfloat16)
    annot_spec = pl.BlockSpec(annot.shape, lambda i, n_ref: (0, 0))
    sums_spec = pl.BlockSpec(sums_type.shape, lambda i, n_ref: (0, 0))
    turned_spec = pl.BlockSpec(turned_type.shape, lambda i, n_ref: (0, 0, 0, 0))
    scratch = [
        pltpu.VMEM((2 * mine, samples, LANES), jnp.bfloat16),
        pltpu.VMEM((samples, TILE), jnp.float32),
    ]
    cost = pl.CostEstimate(flops=work, bytes_accessed=4 * samples * block, transcendentals=0)
    params = pltpu.CompilerParams(vmem_limit_bytes=VMEM_LIMIT)
    sums, turned = pl.pallas_call(
        own_kernel,
        out_shape=(sums_type, turned_type),
        grid_spec=pltpu.PrefetchScalarGridSpec(
            num_scalar_prefetch=1,
            grid=(1,),
            in_specs=[
                pl.BlockSpec((samples, block), lambda i, n_ref: (0, n_ref[0])),
                annot_spec,
            ],
            out_specs=(sums_spec, turned_spec),
            scratch_shapes=scratch,
        ),
        compiler_params=params,
        cost_estimate=cost,
        name="own_sums",
    )(n, dosage, annot)
    sums = pl.pallas_call(
        other_kernel,
        out_shape=sums_type,
        grid_spec=pltpu.PrefetchScalarGridSpec(
            num_scalar_prefetch=1,
            grid=(1,),
            in_specs=[
                pl.BlockSpec((samples, block), lambda i, n_ref: (0, 1 - n_ref[0])),
                annot_spec,
                turned_spec,
                sums_spec,
            ],
            out_specs=sums_spec,
            scratch_shapes=scratch,
        ),
        compiler_params=params,
        cost_estimate=cost,
        name="other_sums",
    )(n, dosage, annot, turned, sums)
    return sums, turned


def rim_kernel(order, n_ref, arrived_ref, turned_ref, annot_ref, sums_in, sums_ref, back_ref, geno, wide_values):
    mine = turned_ref.shape[0]
    samples = geno.shape[1]
    n = n_ref[0]
    standardized(lambda rows: arrived_ref[rows, :], into(geno, 0), wide_values, samples)
    arrived_annot = arrived_ref[samples:, :]
    sums_ref[...] = sums_in[...]
    back_ref[...] = jnp.zeros_like(back_ref)

    def add(y, inside=None):
        weights = band_weights(rows_of(turned_ref, y), columns_of(geno, 0), inside)
        sums_ref[:, cols_at(y)] += along_columns(arrived_annot, weights)
        back_ref[...] += along_rows(annot_ref[:, cols_at(n * mine + y)], weights)

    low, high = order, mine - 1 - order
    add((1 - n) * high + n * low, (1 - 2 * n) * tile_offset() <= 0)
    for y in range(mine):
        first, second = y < high, low < y < mine // 2
        if first or second:

            @pl.when(True if first and second else (n == 0 if first else n == 1))
            def _(y=y):
                add(y)


def rim_sums(order, n, arrived, turned, annot, sums):
    mine, chunks, _, _ = turned.shape
    samples = chunks * LANES
    return pl.pallas_call(
        functools.partial(rim_kernel, order),
        out_shape=(
            jax.ShapeDtypeStruct(sums.shape, jnp.float32),
            jax.ShapeDtypeStruct((sums.shape[0], TILE), jnp.float32),
        ),
        in_specs=[in_smem] + [in_vmem] * 4,
        out_specs=(in_vmem, in_vmem),
        scratch_shapes=[
            pltpu.VMEM((2, samples, LANES), jnp.bfloat16),
            pltpu.VMEM((samples, TILE), jnp.float32),
        ],
        compiler_params=pltpu.CompilerParams(vmem_limit_bytes=VMEM_LIMIT),
        cost_estimate=pl.CostEstimate(
            flops=2 * samples * TILE * mine * TILE,
            bytes_accessed=2 * samples * TILE * (mine + 1),
            transcendentals=0,
        ),
        name="rim_sums",
    )(n, arrived, turned, annot, sums)


def inverse_kernel(divisor, payload_ref, inverse_ref, moments_ref):
    size = payload_ref.shape[1]
    slots = payload_ref.shape[0] - size
    means = payload_ref[size:, :]
    mean = jnp.sum(means, axis=0, keepdims=True) / slots
    between = means - mean
    covariance = (
        payload_ref[:size, :]
        + lax.dot_general(
            between,
            between,
            (((0,), (0,)), ((), ())),
            precision=highest_precision,
            preferred_element_type=jnp.float32,
        )
        * (divisor // slots)
    ) / divisor
    row = lax.broadcasted_iota(jnp.int32, (size, size), 0)
    lane = lax.broadcasted_iota(jnp.int32, (size, size), 1)
    diagonal = jnp.where(row == lane, covariance, 0.0)
    across = 1.0 / jnp.sqrt(jnp.sum(diagonal, axis=0, keepdims=True) + EPS)
    down = 1.0 / jnp.sqrt(jnp.sum(diagonal, axis=1, keepdims=True) + EPS)
    mean_down = jnp.sum(jnp.where(row == lane, jnp.broadcast_to(mean, (size, size)), 0.0), axis=1, keepdims=True)
    moments_ref[...] = jnp.where(lane == 0, mean_down, down)
    gram = covariance * down * across
    groups = [gram[PAD * g : PAD * (g + 1), :] for g in range(size // PAD)]
    one_lane = lax.broadcasted_iota(jnp.int32, (1, size), 1)
    eight = lax.broadcasted_iota(jnp.int32, (PAD, size), 0)
    for k in range(0, size, 2):
        g, i = divmod(k, PAD)
        first, second = groups[g][i : i + 1, :], groups[g][i + 1 : i + 2, :]
        a = first[:, k : k + 1]
        b = first[:, k + 1 : k + 2]
        c = second[:, k + 1 : k + 2]
        scale = 1.0 / (a * c - b * b)
        first = first - jnp.where(one_lane == k, 1.0, 0.0)
        second = second - jnp.where(one_lane == k + 1, 1.0, 0.0)
        left = (c * first - b * second) * scale
        right = (a * second - b * first) * scale
        for h in range(size // PAD):
            old = groups[h]
            new = old - old[:, k : k + 1] * left - old[:, k + 1 : k + 2] * right
            if h == g:
                new = new + jnp.where(eight == i, left, 0.0) + jnp.where(eight == i + 1, right, 0.0)
            groups[h] = new
    swept = jnp.concatenate(groups, axis=0)
    inverse = jnp.where(row == lane, 2.0, 0.0) - swept
    inverse_ref[...] = inverse * down * across / divisor


def gram_inverse(divisor, payload):
    size = payload.shape[1]
    square = jax.ShapeDtypeStruct((size, size), jnp.float32)
    return pl.pallas_call(
        functools.partial(inverse_kernel, divisor),
        out_shape=(square, square),
        in_specs=[in_vmem],
        out_specs=(in_vmem, in_vmem),
        compiler_params=pltpu.CompilerParams(vmem_limit_bytes=VMEM_LIMIT),
        cost_estimate=pl.CostEstimate(flops=20_000_000_000, bytes_accessed=4 * size * size, transcendentals=0),
        name="gram_inverse",
    )(payload)


def fit_kernel(divisor, n_ref, inverse_ref, moments_ref, proj_ref, scores_ref, other_ref, own_ref, fitted_ref):
    annots, block = scores_ref.shape
    n = n_ref[0]
    mean = moments_ref[:, 0:1]
    chi_mean = proj_ref[annots : annots + 1, :] / divisor
    projection = proj_ref[:annots, :] - mean * proj_ref[annots : annots + 1, :]
    coefficient = jnp.dot(
        inverse_ref[...], projection, precision=highest_precision, preferred_element_type=jnp.float32
    )

    def fit(values, place):
        fitted = lax.dot_general(
            values,
            coefficient,
            (((0,), (0,)), ((), ())),
            precision=highest_precision,
            preferred_element_type=jnp.float32,
        )
        fitted_ref[pl.ds(pl.multiple_of(place * block, block), block), :] = chi_mean + fitted

    centred = scores_ref[...] - mean
    own_ref[...] = centred * moments_ref[:, 1:2]
    fit(centred, n)
    fit(other_ref[...] - mean, 1 - n)


def fitted_values(divisor, n, inverse, moments, projection, scores, scores_other):
    annots, block = scores.shape
    traits = projection.shape[1]
    return pl.pallas_call(
        functools.partial(fit_kernel, divisor),
        out_shape=(
            jax.ShapeDtypeStruct((annots, block), jnp.float32),
            jax.ShapeDtypeStruct((2 * block, traits), jnp.float32),
        ),
        in_specs=[in_smem] + [in_vmem] * 5,
        out_specs=(in_vmem, in_vmem),
        compiler_params=pltpu.CompilerParams(vmem_limit_bytes=VMEM_LIMIT),
        cost_estimate=pl.CostEstimate(
            flops=4 * annots * block * traits, bytes_accessed=8 * block * traits, transcendentals=0
        ),
        name="fitted_values",
    )(n, inverse, moments, projection, scores, scores_other)


def flipped(value, axis, bit):
    length = lax.axis_size(axis)
    return lax.ppermute(value, axis, [(i, i ^ bit) for i in range(length)])


def wide_bits():
    length = lax.axis_size("wide")
    bits = []
    bit = 1
    while bit < length:
        bits.append(bit)
        bit *= 2
    return bits


def wide_sum(value):
    for bit in wide_bits():
        value = value + flipped(value, "wide", bit)
    return value


def split_wide_sum(value):
    half = value.shape[0] // 2
    low = lax.axis_index("wide") % 2
    kept = lax.dynamic_slice_in_dim(value, low * half, half, 0)
    given = lax.dynamic_slice_in_dim(value, (1 - low) * half, half, 0)
    kept = kept + flipped(given, "wide", 1)
    for bit in wide_bits()[1:]:
        kept = kept + flipped(kept, "wide", bit)
    other = flipped(kept, "wide", 1)
    return jnp.where(
        low == 0, jnp.concatenate([kept, other], 0), jnp.concatenate([other, kept], 0)
    )


def shards(dosage, annotations, test_statistic_table):
    samples, strip = dosage.shape
    annots = annotations.shape[0]
    wide = lax.axis_size("wide")
    total_variants = wide * strip
    w = lax.axis_index("wide")
    n = lax.axis_index("narrow")
    block = strip // 2
    n_array = jnp.reshape(n, (1,)).astype(jnp.int32)

    annot = jnp.concatenate(
        [
            annotations.astype(jnp.bfloat16),
            jnp.ones((1, strip), jnp.bfloat16),
            jnp.zeros((PAD - 1, strip), jnp.bfloat16),
        ],
        axis=0,
    )
    rim_pairs = []
    back_pairs = []
    for i in range(wide - 1):
        rim_pairs += [(2 * i, 2 * i + 2), (2 * i + 3, 2 * i + 1)]
        back_pairs += [(2 * i + 1, 2 * i + 2), (2 * i + 2, 2 * i + 1)]
    outgoing = [outgoing_columns(order, n_array, dosage, annotations) for order in range(2)]
    arrived = [lax.ppermute(value, both, rim_pairs) for value in outgoing]

    chi = test_statistic_table
    chi_own = lax.dynamic_slice_in_dim(chi, n * block, block, 0)
    chi_other = flipped(lax.dynamic_slice_in_dim(chi, (1 - n) * block, block, 0), "narrow", 1)

    counts = jnp.sum(annotations, axis=1).astype(jnp.float32)
    shares = wide_sum(counts) / total_variants

    sums, turned = strip_sums(n_array, dosage, annot)
    back = []
    for order in range(2):
        sums, part = rim_sums(order, n_array, arrived[order], turned, annot, sums)
        back.append(lax.ppermute(part, both, back_pairs))
    empty = jnp.zeros((annot.shape[0], block - 2 * TILE), jnp.float32)
    sums = sums + jnp.where(
        n == 0,
        jnp.concatenate([back[0], back[1], empty], axis=1),
        jnp.concatenate([empty, back[1], back[0]], axis=1),
    )

    high = lax.reduce_precision(1.0 - shares, 8, 7)[:, None]
    low = lax.reduce_precision(0.0 - shares, 8, 7)[:, None]
    members = sums[:annots]
    scores = high * members + low * (sums[annots : annots + 1] - members)

    block_mean = jnp.mean(scores, axis=1)
    deviation = scores - block_mean[:, None]
    cross = lax.dot_general(
        deviation,
        deviation,
        (((1,), (1,)), ((), ())),
        precision=highest_precision,
        preferred_element_type=jnp.float32,
    )
    blocks = 2 * wide
    slots = jnp.where(jnp.arange(blocks)[:, None] == 2 * w + n, block_mean[None, :], 0.0)
    payload = jnp.concatenate([cross, slots], axis=0)
    payload = payload + flipped(payload, "narrow", 1)
    payload = split_wide_sum(payload)

    extended = jnp.concatenate(
        [scores, jnp.ones((1, block), jnp.float32), jnp.zeros((2 * PAD - 1, block), jnp.float32)], axis=0
    )
    proj_own, proj_other = (
        jnp.dot(
            extended, values, precision=highest_precision, preferred_element_type=jnp.float32
        )
        for values in (chi_own, chi_other)
    )
    projection = proj_own + flipped(proj_other, "narrow", 1)
    projection = split_wide_sum(projection)
    scores_other = flipped(scores, "narrow", 1)

    inverse, moments = gram_inverse(total_variants, payload)
    return fitted_values(
        total_variants, n_array, inverse, moments, projection, scores, scores_other
    )


def solution(mesh):
    in_specs = (P(None, "wide"), P(None, "wide"), P("wide", "narrow"))
    out_specs = (P(None, both), P("wide", "narrow"))
    return jax.shard_map(shards, mesh=mesh, in_specs=in_specs, out_specs=out_specs, check_vma=False)
```

```python
import functools

import jax
import jax.numpy as jnp
from jax import lax
from jax.experimental import pallas as pl
from jax.experimental.pallas import tpu as pltpu
from jax.sharding import PartitionSpec as P


EPS = 1e-05
TILE = 256
LANES = 128
ROWS = 256
PAD = 8
PIVOTS = 4
VMEM_LIMIT = 36 * 1024 * 1024

highest_precision = lax.Precision.HIGHEST
both = ("wide", "narrow")
in_vmem = pl.BlockSpec(memory_space=pltpu.VMEM)
in_place = pl.BlockSpec(memory_space=pl.ANY)
in_smem = pl.BlockSpec(memory_space=pltpu.SMEM)


def cols_at(c):
    return pl.ds(pl.multiple_of(c * TILE, TILE), TILE)


def standardized(read, write, wide_values, samples):
    steps = samples // ROWS
    empty = jnp.zeros((4 * PAD, TILE), jnp.float32)

    def folded(values):
        return jnp.sum(values.reshape(-1, 4 * PAD, TILE), axis=0)

    def rows_at(r):
        return pl.ds(pl.multiple_of(r * ROWS, ROWS), ROWS)

    def total(r, carry):
        values = read(rows_at(r)).astype(jnp.float32)
        wide_values[rows_at(r), :] = values
        return carry + folded(values)

    mean = jnp.sum(lax.fori_loop(0, steps, total, empty), axis=0, keepdims=True) / samples

    def squares(r, carry):
        away = wide_values[rows_at(r), :] - mean
        return carry + folded(away * away)

    variance = jnp.sum(lax.fori_loop(0, steps, squares, empty), axis=0, keepdims=True) / samples
    scale = 1.0 / jnp.sqrt(variance + EPS)

    def store(r, carry):
        write(rows_at(r), ((wide_values[rows_at(r), :] - mean) * scale).astype(jnp.bfloat16))
        return carry

    lax.fori_loop(0, steps, store, 0)


def into(geno, tile):
    def write(rows, value):
        geno[2 * tile, rows, :] = value[:, :LANES]
        geno[2 * tile + 1, rows, :] = value[:, LANES:]

    return write


def columns_of(geno, tile):
    return jnp.concatenate([geno[2 * tile], geno[2 * tile + 1]], axis=1)


def rows_of(turned, tile):
    return jnp.concatenate([turned[tile, k] for k in range(turned.shape[1])], axis=1)


def band_weights(rows, columns, inside=None):
    samples = rows.shape[1]
    products = jnp.dot(rows, columns, preferred_element_type=jnp.float32)
    unit = 1.0 / (samples - 2)
    weights = products * products * ((1.0 + unit) / (samples * samples)) - unit
    if inside is not None:
        weights = jnp.where(inside, weights, 0.0)
    return weights.astype(jnp.bfloat16)


def along_rows(annot, weights):
    return jnp.dot(annot, weights, preferred_element_type=jnp.float32)


def along_columns(annot, weights):
    return lax.dot_general(
        annot, weights, (((1,), (1,)), ((), ())), preferred_element_type=jnp.float32
    )


def tile_offset():
    shape = (TILE, TILE)
    return lax.broadcasted_iota(jnp.int32, shape, 0) - lax.broadcasted_iota(jnp.int32, shape, 1)


def sizes(dosage):
    samples, strip = dosage.shape
    return samples, strip, strip // (2 * TILE)


def outgoing_kernel(order, n_ref, dosage_ref, annot_ref, out_ref, given_annot, arrived):
    samples, strip = dosage_ref.shape
    annots = annot_ref.shape[0]
    n = n_ref[0]
    column = cols_at((1 - n) * (strip // TILE - 1 - order) + n * order)
    copies = [
        pltpu.make_async_copy(dosage_ref.at[:, column], out_ref.at[:samples, :], arrived.at[0]),
        pltpu.make_async_copy(annot_ref.at[:, column], given_annot, arrived.at[1]),
    ]
    for copy in copies:
        copy.start()
    row = lax.broadcasted_iota(jnp.int32, (PAD, TILE), 0)
    out_ref[samples + annots :, :] = jnp.where(row == 0, 1.0, 0.0).astype(jnp.bfloat16)
    copies[1].wait()
    out_ref[samples : samples + annots, :] = given_annot[...].astype(jnp.float32).astype(jnp.bfloat16)
    copies[0].wait()


def outgoing_columns(order, n, dosage, annotations):
    samples, _, _ = sizes(dosage)
    annots = annotations.shape[0]
    rows = samples + annots + PAD
    return pl.pallas_call(
        functools.partial(outgoing_kernel, order),
        out_shape=jax.ShapeDtypeStruct((rows, TILE), jnp.bfloat16),
        in_specs=[in_smem, in_place, in_place],
        out_specs=in_vmem,
        scratch_shapes=[pltpu.VMEM((annots, TILE), jnp.int32), pltpu.SemaphoreType.DMA((2,))],
        cost_estimate=pl.CostEstimate(flops=0, bytes_accessed=4 * rows * TILE, transcendentals=0),
        name="outgoing",
    )(n, dosage, annotations)


def strip_kernel(
    n_ref, dosage_ref, annot_ref, sums_ref, turned_ref, given, geno, turned, wide_values, came, went
):
    samples, strip = dosage_ref.shape
    tiles = strip // TILE
    mine = tiles // 2
    n = n_ref[0]

    def column(t):
        owner = n if t < mine else 1 - n
        return owner * mine + t % mine

    arrivals = [
        pltpu.make_async_copy(dosage_ref.at[:, cols_at(column(t))], given.at[t], came.at[t])
        for t in range(tiles)
    ]
    departures = [
        pltpu.make_async_copy(turned.at[t], turned_ref.at[t], went.at[t]) for t in range(mine)
    ]
    for copy in arrivals:
        copy.start()
    sums_ref[...] = jnp.zeros_like(sums_ref)
    for t in range(tiles):
        arrivals[t].wait()
        standardized(lambda rows: given[t, rows, :], into(geno, t), wide_values, samples)
        if t < mine:
            for k in range(samples // LANES):
                for part in range(2):
                    turned[t, k, part * LANES : (part + 1) * LANES, :] = geno[
                        2 * t + part, k * LANES : (k + 1) * LANES, :
                    ].T
            departures[t].start()
    for y in range(mine):
        for x in range(y + 1):
            weights = band_weights(rows_of(turned, x), columns_of(geno, y))
            sums_ref[:, y * TILE : (y + 1) * TILE] += along_rows(
                annot_ref[:, cols_at(column(x))], weights
            )
            if x < y:
                sums_ref[:, x * TILE : (x + 1) * TILE] += along_columns(
                    annot_ref[:, cols_at(column(y))], weights
                )
    inside = (1 - 2 * n) * tile_offset() >= 0
    for high in range(mine):
        for low in range(high + 1):
            theirs = low + n * (high - low)
            ours = high - n * (high - low)
            columns = jnp.concatenate(
                [geno[2 * (mine + theirs)], geno[2 * (mine + theirs) + 1]], axis=1
            )
            weights = band_weights(
                rows_of(turned, ours), columns, inside if low == high else None
            )
            sums_ref[:, cols_at(ours)] += along_columns(
                annot_ref[:, cols_at((1 - n) * mine + theirs)], weights
            )
    for copy in departures:
        copy.wait()


def strip_sums(n, dosage, annot):
    samples, strip, mine = sizes(dosage)
    block = strip // 2
    chunks = samples // LANES
    return pl.pallas_call(
        strip_kernel,
        out_shape=(
            jax.ShapeDtypeStruct((annot.shape[0], block), jnp.float32),
            jax.ShapeDtypeStruct((mine, chunks, TILE, LANES), jnp.bfloat16),
        ),
        in_specs=[in_smem, in_place, in_vmem],
        out_specs=(in_vmem, in_place),
        scratch_shapes=[
            pltpu.VMEM((2 * mine, samples, TILE), jnp.bfloat16),
            pltpu.VMEM((4 * mine, samples, LANES), jnp.bfloat16),
            pltpu.VMEM((mine, chunks, TILE, LANES), jnp.bfloat16),
            pltpu.VMEM((samples, TILE), jnp.float32),
            pltpu.SemaphoreType.DMA((2 * mine,)),
            pltpu.SemaphoreType.DMA((mine,)),
        ],
        cost_estimate=pl.CostEstimate(
            flops=2 * samples * block * strip,
            bytes_accessed=3 * samples * strip,
            transcendentals=0,
        ),
        name="strip_sums",
    )(n, dosage, annot)


def rim_kernel(
    order, n_ref, arrived_ref, turned_ref, annot_ref, sums_in, sums_ref, back_ref,
    geno, turned, wide_values, came,
):
    mine = turned_ref.shape[0]
    samples = geno.shape[1]
    n = n_ref[0]
    arrivals = [
        pltpu.make_async_copy(turned_ref.at[t], turned.at[t], came.at[t]) for t in range(mine)
    ]
    for copy in arrivals:
        copy.start()
    standardized(lambda rows: arrived_ref[rows, :], into(geno, 0), wide_values, samples)
    arrived_annot = arrived_ref[samples:, :]
    sums_ref[...] = sums_in[...]
    back_ref[...] = jnp.zeros_like(back_ref)
    for copy in arrivals:
        copy.wait()

    def add(y, inside=None):
        weights = band_weights(rows_of(turned, y), columns_of(geno, 0), inside)
        sums_ref[:, cols_at(y)] += along_columns(arrived_annot, weights)
        back_ref[...] += along_rows(annot_ref[:, cols_at(n * mine + y)], weights)

    low, high = order, mine - 1 - order
    add((1 - n) * high + n * low, (1 - 2 * n) * tile_offset() <= 0)
    for y in range(mine):
        first, second = y < high, low < y < mine // 2
        if first or second:

            @pl.when(True if first and second else (n == 0 if first else n == 1))
            def _(y=y):
                add(y)


def rim_sums(order, n, arrived, turned, annot, sums):
    mine, chunks, _, _ = turned.shape
    samples = chunks * LANES
    return pl.pallas_call(
        functools.partial(rim_kernel, order),
        out_shape=(
            jax.ShapeDtypeStruct(sums.shape, jnp.float32),
            jax.ShapeDtypeStruct((sums.shape[0], TILE), jnp.float32),
        ),
        in_specs=[in_smem, in_vmem, in_place, in_vmem, in_vmem],
        out_specs=(in_vmem, in_vmem),
        scratch_shapes=[
            pltpu.VMEM((2, samples, LANES), jnp.bfloat16),
            pltpu.VMEM(turned.shape, jnp.bfloat16),
            pltpu.VMEM((samples, TILE), jnp.float32),
            pltpu.SemaphoreType.DMA((mine,)),
        ],
        cost_estimate=pl.CostEstimate(
            flops=2 * samples * TILE * mine * TILE,
            bytes_accessed=2 * samples * TILE * (mine + 1),
            transcendentals=0,
        ),
        name="rim_sums",
    )(n, arrived, turned, annot, sums)


def eye(size):
    shape = (size, size)
    return lax.broadcasted_iota(jnp.int32, shape, 0) == lax.broadcasted_iota(jnp.int32, shape, 1)


def upright(row):
    size = row.shape[1]
    return jnp.sum(jnp.where(eye(size), jnp.broadcast_to(row, (size, size)), 0.0), axis=1, keepdims=True)


def moments_kernel(total_variants, place_ref, counts_ref, sums_ref, first_ref, second_ref, scores_ref, payload_ref, whole):
    annots = counts_ref.shape[1]
    block = sums_ref.shape[1]
    mine = block // TILE
    n, slot = place_ref[0], place_ref[1]
    whole[...] = sums_ref[...]
    for order, back_ref in enumerate((first_ref, second_ref)):
        whole[:, cols_at((1 - n) * order + n * (mine - 1 - order))] += back_ref[...]
    shares = upright(counts_ref[...]) / total_variants
    high = (1.0 - shares).astype(jnp.bfloat16).astype(jnp.float32)
    low = (0.0 - shares).astype(jnp.bfloat16).astype(jnp.float32)
    members = whole[:annots, :]
    scores = high * members + low * (whole[annots : annots + 1, :] - members)
    scores_ref[:annots, :] = scores
    row = lax.broadcasted_iota(jnp.int32, (2 * PAD, block), 0)
    scores_ref[annots:, :] = jnp.where(row == 0, 1.0, 0.0)
    mean = jnp.sum(scores, axis=1, keepdims=True) / block
    deviation = scores - mean
    payload_ref[:annots, :] = lax.dot_general(
        deviation,
        deviation,
        (((1,), (1,)), ((), ())),
        precision=highest_precision,
        preferred_element_type=jnp.float32,
    )
    mean_row = jnp.sum(
        jnp.where(eye(annots), jnp.broadcast_to(mean, (annots, annots)), 0.0), axis=0, keepdims=True
    )
    slots = payload_ref.shape[0] - annots
    at = lax.broadcasted_iota(jnp.int32, (slots, annots), 0)
    payload_ref[annots:, :] = jnp.where(at == slot, mean_row, 0.0)


def moments_of(total_variants, slots, place, counts, sums, back):
    annots = counts.shape[0]
    block = sums.shape[1]
    return pl.pallas_call(
        functools.partial(moments_kernel, total_variants),
        out_shape=(
            jax.ShapeDtypeStruct((annots + 2 * PAD, block), jnp.float32),
            jax.ShapeDtypeStruct((annots + slots, annots), jnp.float32),
        ),
        in_specs=[in_smem] + [in_vmem] * 4,
        out_specs=(in_vmem, in_vmem),
        scratch_shapes=[pltpu.VMEM(sums.shape, jnp.float32)],
        compiler_params=pltpu.CompilerParams(vmem_limit_bytes=VMEM_LIMIT),
        cost_estimate=pl.CostEstimate(
            flops=12 * annots * annots * block, bytes_accessed=12 * annots * block, transcendentals=0
        ),
        name="moments",
    )(place, counts.reshape(1, annots), sums, *back)


def inverse_kernel(divisor, payload_ref, inverse_ref, moments_ref):
    size = payload_ref.shape[1]
    slots = payload_ref.shape[0] - size
    means = payload_ref[size:, :]
    mean = jnp.sum(means, axis=0, keepdims=True) / slots
    between = means - mean
    covariance = (
        payload_ref[:size, :]
        + lax.dot_general(
            between,
            between,
            (((0,), (0,)), ((), ())),
            precision=highest_precision,
            preferred_element_type=jnp.float32,
        )
        * (divisor // slots)
    ) / divisor
    row = lax.broadcasted_iota(jnp.int32, (size, size), 0)
    lane = lax.broadcasted_iota(jnp.int32, (size, size), 1)
    diagonal = jnp.where(row == lane, covariance, 0.0)
    across = 1.0 / jnp.sqrt(jnp.sum(diagonal, axis=0, keepdims=True) + EPS)
    down = 1.0 / jnp.sqrt(jnp.sum(diagonal, axis=1, keepdims=True) + EPS)
    mean_down = jnp.sum(jnp.where(row == lane, jnp.broadcast_to(mean, (size, size)), 0.0), axis=1, keepdims=True)
    moments_ref[...] = jnp.where(lane == 0, mean_down, down)
    gram = covariance * down * across
    groups = [gram[PAD * g : PAD * (g + 1), :] for g in range(size // PAD)]
    lane_of = lax.broadcasted_iota(jnp.int32, (1, size), 1)
    row_of = lax.broadcasted_iota(jnp.int32, (PAD, size), 0)

    def pair_inverse(a, b, c):
        scale = 1.0 / (a * c - b * b)
        return c * scale, -b * scale, a * scale

    for k in range(0, size, PIVOTS):
        g, i = divmod(k, PAD)
        spread = [
            [jnp.broadcast_to(old[:, k + j : k + j + 1], (PAD, size)) for j in range(PIVOTS)]
            for old in groups
        ]
        m = [[spread[g][c][i + r : i + r + 1, :] for c in range(PIVOTS)] for r in range(PIVOTS)]
        rows = [
            groups[g][i + j : i + j + 1, :] - jnp.where(lane_of == k + j, 1.0, 0.0)
            for j in range(PIVOTS)
        ]
        a, b, c = pair_inverse(m[0][0], m[0][1], m[1][1])
        u = a * rows[0] + b * rows[1], b * rows[0] + c * rows[1]
        v = [(a * m[0][j] + b * m[1][j], b * m[0][j] + c * m[1][j]) for j in (2, 3)]
        rest = [rows[j] - m[0][j] * u[0] - m[1][j] * u[1] for j in (2, 3)]
        d, e, f = pair_inverse(
            m[2][2] - m[0][2] * v[0][0] - m[1][2] * v[0][1],
            m[2][3] - m[0][2] * v[1][0] - m[1][2] * v[1][1],
            m[3][3] - m[0][3] * v[1][0] - m[1][3] * v[1][1],
        )
        third = d * rest[0] + e * rest[1]
        fourth = e * rest[0] + f * rest[1]
        solved = [
            u[0] - v[0][0] * third - v[1][0] * fourth,
            u[1] - v[0][1] * third - v[1][1] * fourth,
            third,
            fourth,
        ]
        solved = [jnp.broadcast_to(value, (PAD, size)) for value in solved]
        for h, old in enumerate(groups):
            for j in range(PIVOTS):
                old = old - spread[h][j] * solved[j]
                if h == g:
                    old = old + jnp.where(row_of == i + j, solved[j], 0.0)
            groups[h] = old
    swept = jnp.concatenate(groups, axis=0)
    inverse = jnp.where(row == lane, 2.0, 0.0) - swept
    inverse_ref[...] = inverse * down * across / divisor


def gram_inverse(divisor, payload):
    size = payload.shape[1]
    square = jax.ShapeDtypeStruct((size, size), jnp.float32)
    return pl.pallas_call(
        functools.partial(inverse_kernel, divisor),
        out_shape=(square, square),
        in_specs=[in_vmem],
        out_specs=(in_vmem, in_vmem),
        compiler_params=pltpu.CompilerParams(vmem_limit_bytes=VMEM_LIMIT),
        cost_estimate=pl.CostEstimate(flops=20_000_000_000, bytes_accessed=4 * size * size, transcendentals=0),
        name="gram_inverse",
    )(payload)


def halves(value):
    upper = value.astype(jnp.bfloat16)
    return upper, (value - upper.astype(jnp.float32)).astype(jnp.bfloat16)


def fit_kernel(divisor, n_ref, inverse_ref, moments_ref, proj_ref, scores_ref, other_ref, own_ref, fitted_ref):
    annots = own_ref.shape[0]
    block = scores_ref.shape[1]
    n = n_ref[0]
    mean = moments_ref[:, 0:1]
    sums = proj_ref[annots : annots + 1, :]
    coefficient = jnp.dot(
        inverse_ref[...],
        proj_ref[:annots, :] - mean * sums,
        precision=highest_precision,
        preferred_element_type=jnp.float32,
    )
    upper, lower = halves(coefficient)
    right = jnp.concatenate([upper, upper, lower], axis=0)

    def fit(values, place):
        upper, lower = halves(values)
        fitted = lax.dot_general(
            jnp.concatenate([upper, lower, upper], axis=0),
            right,
            (((0,), (0,)), ((), ())),
            preferred_element_type=jnp.float32,
        )
        rows = pl.ds(pl.multiple_of(place * block, block), block)
        fitted_ref[rows, :] = sums / divisor + fitted

    centred = scores_ref[:annots, :] - mean
    own_ref[...] = centred * moments_ref[:, 1:2]
    fit(centred, n)
    fit(other_ref[...] - mean, 1 - n)


def fitted_values(divisor, n, inverse, moments, projection, scores, scores_other):
    annots, block = scores_other.shape
    traits = projection.shape[1]
    return pl.pallas_call(
        functools.partial(fit_kernel, divisor),
        out_shape=(
            jax.ShapeDtypeStruct((annots, block), jnp.float32),
            jax.ShapeDtypeStruct((2 * block, traits), jnp.float32),
        ),
        in_specs=[in_smem] + [in_vmem] * 5,
        out_specs=(in_vmem, in_vmem),
        compiler_params=pltpu.CompilerParams(vmem_limit_bytes=VMEM_LIMIT),
        cost_estimate=pl.CostEstimate(
            flops=4 * annots * block * traits, bytes_accessed=8 * block * traits, transcendentals=0
        ),
        name="fitted_values",
    )(n, inverse, moments, projection, scores, scores_other)


def flipped(value, axis, bit):
    length = lax.axis_size(axis)
    return lax.ppermute(value, axis, [(i, i ^ bit) for i in range(length)])


def wide_bits():
    length = lax.axis_size("wide")
    bits = []
    bit = 1
    while bit < length:
        bits.append(bit)
        bit *= 2
    return bits


def wide_sum(value):
    for bit in wide_bits():
        value = value + flipped(value, "wide", bit)
    return value


def split_wide_sum(value):
    half = value.shape[0] // 2
    low = lax.axis_index("wide") % 2
    kept = lax.dynamic_slice_in_dim(value, low * half, half, 0)
    given = lax.dynamic_slice_in_dim(value, (1 - low) * half, half, 0)
    kept = kept + flipped(given, "wide", 1)
    for bit in wide_bits()[1:]:
        kept = kept + flipped(kept, "wide", bit)
    other = flipped(kept, "wide", 1)
    return jnp.where(
        low == 0, jnp.concatenate([kept, other], 0), jnp.concatenate([other, kept], 0)
    )


def whole_step(dosage, annotations, test_statistic_table):
    _, strip = dosage.shape
    annots = annotations.shape[0]
    wide = lax.axis_size("wide")
    total_variants = wide * strip
    w = lax.axis_index("wide")
    n = lax.axis_index("narrow")
    block = strip // 2
    n_array = jnp.reshape(n, (1,)).astype(jnp.int32)

    annot = jnp.concatenate(
        [
            annotations.astype(jnp.bfloat16),
            jnp.ones((1, strip), jnp.bfloat16),
            jnp.zeros((PAD - 1, strip), jnp.bfloat16),
        ],
        axis=0,
    )
    rim_pairs = []
    back_pairs = []
    for i in range(wide - 1):
        rim_pairs += [(2 * i, 2 * i + 2), (2 * i + 3, 2 * i + 1)]
        back_pairs += [(2 * i + 1, 2 * i + 2), (2 * i + 2, 2 * i + 1)]
    arrived = []
    for order in range(2):
        outgoing = outgoing_columns(order, n_array, dosage, annotations)
        arrived.append(lax.ppermute(outgoing, both, rim_pairs))
    annotations, chi, _ = lax.optimization_barrier((annotations, test_statistic_table, outgoing))

    chi_own = lax.dynamic_slice_in_dim(chi, n * block, block, 0)
    chi_other = flipped(lax.dynamic_slice_in_dim(chi, (1 - n) * block, block, 0), "narrow", 1)
    counts = wide_sum(jnp.sum(annotations, axis=1).astype(jnp.float32))

    sums, turned = strip_sums(n_array, dosage, annot)
    back = []
    for order in range(2):
        sums, part = rim_sums(order, n_array, arrived[order], turned, annot, sums)
        back.append(lax.ppermute(part, both, back_pairs))

    place = jnp.stack([n, 2 * w + n]).astype(jnp.int32)
    extended, payload = moments_of(total_variants, 2 * wide, place, counts, sums, back)
    scores = extended[:annots]
    payload = payload + flipped(payload, "narrow", 1)
    payload = split_wide_sum(payload)
    proj_own, proj_other = (
        jnp.dot(
            extended, values, precision=lax.Precision.HIGH, preferred_element_type=jnp.float32
        )
        for values in (chi_own, chi_other)
    )
    projection = proj_own + flipped(proj_other, "narrow", 1)
    projection = split_wide_sum(projection)
    scores_other = flipped(scores, "narrow", 1)

    inverse, moments = gram_inverse(total_variants, payload)
    return fitted_values(
        total_variants, n_array, inverse, moments, projection, extended, scores_other
    )


def solution(mesh):
    in_specs = (P(None, "wide"), P(None, "wide"), P("wide", "narrow"))
    out_specs = (P(None, both), P("wide", "narrow"))
    return jax.shard_map(whole_step, mesh=mesh, in_specs=in_specs, out_specs=out_specs, check_vma=False)
```

```python
import functools

import jax
import jax.numpy as jnp
from jax import lax
from jax.experimental import pallas as pl
from jax.experimental.pallas import tpu as pltpu
from jax.sharding import PartitionSpec as P


EPS = 1e-05
TILE = 256
LANES = 128
ROWS = 256
PAD = 8
PIVOTS = 4
VMEM_LIMIT = 36 * 1024 * 1024

highest_precision = lax.Precision.HIGHEST
both = ("wide", "narrow")
in_vmem = pl.BlockSpec(memory_space=pltpu.VMEM)
in_place = pl.BlockSpec(memory_space=pltpu.HBM)
in_smem = pl.BlockSpec(memory_space=pltpu.SMEM)


def cols_at(c):
    return pl.ds(pl.multiple_of(c * TILE, TILE), TILE)


def standardized(read, write, wide_values, samples):
    steps = samples // ROWS
    empty = jnp.zeros((4 * PAD, TILE), jnp.float32)
    pivot = read(pl.ds(0, 2 * PAD)).astype(jnp.float32)[:1, :]

    def folded(values):
        return jnp.sum(values.reshape(-1, 4 * PAD, TILE), axis=0)

    def rows_at(r):
        return pl.ds(pl.multiple_of(r * ROWS, ROWS), ROWS)

    def total(r, carry):
        values = read(rows_at(r)).astype(jnp.float32) - pivot
        wide_values[rows_at(r), :] = values
        return carry[0] + folded(values), carry[1] + folded(values * values)

    first, second = (
        jnp.sum(value, axis=0, keepdims=True) / samples
        for value in lax.fori_loop(0, steps, total, (empty, empty))
    )
    variance = jnp.maximum(second - first * first, 0.0)
    scale = 1.0 / jnp.sqrt(variance + EPS)

    def store(r, carry):
        write(rows_at(r), ((wide_values[rows_at(r), :] - first) * scale).astype(jnp.bfloat16))
        return carry

    lax.fori_loop(0, steps, store, 0)


def into(geno, tile):
    def write(rows, value):
        geno[2 * tile, rows, :] = value[:, :LANES]
        geno[2 * tile + 1, rows, :] = value[:, LANES:]

    return write


def columns_of(geno, tile):
    return jnp.concatenate([geno[2 * tile], geno[2 * tile + 1]], axis=1)


def rows_of(turned, tile):
    return jnp.concatenate([turned[tile, k] for k in range(turned.shape[1])], axis=1)


def band_weights(rows, columns, inside=None):
    samples = rows.shape[1]
    products = jnp.dot(rows, columns, preferred_element_type=jnp.float32)
    unit = 1.0 / (samples - 2)
    weights = products * products * ((1.0 + unit) / (samples * samples)) - unit
    if inside is not None:
        weights = jnp.where(inside, weights, 0.0)
    return weights.astype(jnp.bfloat16)


def along_rows(annot, weights):
    return jnp.dot(annot, weights, preferred_element_type=jnp.float32)


def along_columns(annot, weights):
    return lax.dot_general(
        annot, weights, (((1,), (1,)), ((), ())), preferred_element_type=jnp.float32
    )


def tile_offset():
    shape = (TILE, TILE)
    return lax.broadcasted_iota(jnp.int32, shape, 0) - lax.broadcasted_iota(jnp.int32, shape, 1)


def sizes(dosage):
    samples, strip = dosage.shape
    return samples, strip, strip // (2 * TILE)


def prepare_kernel(
    n_ref, dosage_ref, annot_ref, chi_ref, out_ref, annot_out_ref, counts_ref, chi_out_ref, given_annot, came
):
    samples, strip = dosage_ref.shape
    annots = annot_ref.shape[0]
    block = strip // 2
    width = out_ref.shape[1]
    n = n_ref[0]
    column = pl.ds(pl.multiple_of((1 - n) * (strip - width), width), width)
    rows = pl.ds(pl.multiple_of((1 - n) * block, block), block)
    copies = [
        pltpu.make_async_copy(annot_ref, given_annot, came.at[0]),
        pltpu.make_async_copy(dosage_ref.at[:, column], out_ref.at[:samples, :], came.at[1]),
        pltpu.make_async_copy(chi_ref.at[rows, :], chi_out_ref, came.at[2]),
    ]
    for copy in copies:
        copy.start()
    row = lax.broadcasted_iota(jnp.int32, (PAD, strip), 0)
    annot_out_ref[annots:, :] = jnp.where(row == 0, 1.0, 0.0).astype(jnp.bfloat16)
    copies[0].wait()
    members = given_annot[...].astype(jnp.float32)
    annot_out_ref[:annots, :] = members.astype(jnp.bfloat16)
    counts = jnp.sum(members, axis=1, keepdims=True)
    counts_ref[...] = lying(counts)
    out_ref[samples:, :] = annot_out_ref[:, column]
    for copy in copies[1:]:
        copy.wait()


def prepared(n, dosage, annotations, chi):
    samples, strip, _ = sizes(dosage)
    annots = annotations.shape[0]
    rows = annots + PAD
    width = strip // 4
    return pl.pallas_call(
        prepare_kernel,
        out_shape=(
            jax.ShapeDtypeStruct((samples + rows, width), jnp.bfloat16),
            jax.ShapeDtypeStruct((rows, strip), jnp.bfloat16),
            jax.ShapeDtypeStruct((1, annots), jnp.float32),
            jax.ShapeDtypeStruct((strip // 2, chi.shape[1]), jnp.float32),
        ),
        in_specs=[in_smem, in_place, in_place, in_place],
        out_specs=(in_vmem,) * 4,
        scratch_shapes=[pltpu.VMEM(annotations.shape, jnp.int32), pltpu.SemaphoreType.DMA((3,))],
        cost_estimate=pl.CostEstimate(
            flops=0, bytes_accessed=4 * samples * width + 8 * strip * annots, transcendentals=0
        ),
        name="prepare",
    )(n, dosage, annotations, chi)


def own_kernel(n_ref, dosage_ref, annot_ref, sums_ref, turned_ref, given, geno, turned, wide_values, came, went):
    samples, strip = dosage_ref.shape
    mine = strip // (2 * TILE)
    n = n_ref[0]
    arrivals = [
        pltpu.make_async_copy(dosage_ref.at[:, cols_at(n * mine + t)], given.at[t], came.at[t])
        for t in range(mine)
    ]
    departures = [
        pltpu.make_async_copy(turned.at[t], turned_ref.at[t], went.at[t]) for t in range(mine)
    ]
    for copy in arrivals:
        copy.start()
    sums_ref[...] = jnp.zeros_like(sums_ref)
    for t in range(mine):
        arrivals[t].wait()
        standardized(lambda rows: given[t, rows, :], into(geno, t), wide_values, samples)
        for k in range(samples // LANES):
            for part in range(2):
                turned[t, k, part * LANES : (part + 1) * LANES, :] = geno[
                    2 * t + part, k * LANES : (k + 1) * LANES, :
                ].T
        departures[t].start()
    for y in range(mine):
        for x in range(y + 1):
            weights = band_weights(rows_of(turned, x), columns_of(geno, y))
            sums_ref[:, y * TILE : (y + 1) * TILE] += along_rows(
                annot_ref[:, cols_at(n * mine + x)], weights
            )
            if x < y:
                sums_ref[:, x * TILE : (x + 1) * TILE] += along_columns(
                    annot_ref[:, cols_at(n * mine + y)], weights
                )
    for copy in departures:
        copy.wait()


def other_kernel(
    n_ref, dosage_ref, annot_ref, turned_ref, sums_in, sums_ref, given, geno, turned, wide_values, came, back
):
    samples, strip = dosage_ref.shape
    mine = strip // (2 * TILE)
    n = n_ref[0]
    arrivals = [
        pltpu.make_async_copy(dosage_ref.at[:, cols_at((1 - n) * mine + t)], given.at[t], came.at[t])
        for t in range(mine)
    ]
    returns = [
        pltpu.make_async_copy(turned_ref.at[t], turned.at[t], back.at[t]) for t in range(mine)
    ]
    for copy in arrivals + returns:
        copy.start()
    sums_ref[...] = sums_in[...]
    for t in range(mine):
        arrivals[t].wait()
        standardized(lambda rows: given[t, rows, :], into(geno, t), wide_values, samples)
    for copy in returns:
        copy.wait()
    inside = (1 - 2 * n) * tile_offset() >= 0
    for high in range(mine):
        for low in range(high + 1):
            theirs = low + n * (high - low)
            ours = high - n * (high - low)
            weights = band_weights(
                rows_of(turned, ours), columns_of(geno, theirs), inside if low == high else None
            )
            sums_ref[:, cols_at(ours)] += along_columns(
                annot_ref[:, cols_at((1 - n) * mine + theirs)], weights
            )


def own_sums(n, dosage, annot):
    samples, strip, mine = sizes(dosage)
    chunks = samples // LANES
    turned = (mine, chunks, TILE, LANES)
    return pl.pallas_call(
        own_kernel,
        out_shape=(
            jax.ShapeDtypeStruct((annot.shape[0], strip // 2), jnp.float32),
            jax.ShapeDtypeStruct(turned, jnp.bfloat16),
        ),
        in_specs=[in_smem, in_place, in_vmem],
        out_specs=(in_vmem, in_place),
        scratch_shapes=strip_scratch(dosage),
        cost_estimate=strip_cost(dosage),
        name="own_sums",
    )(n, dosage, annot)


def other_sums(n, dosage, annot, turned, sums):
    return pl.pallas_call(
        other_kernel,
        out_shape=jax.ShapeDtypeStruct(sums.shape, jnp.float32),
        in_specs=[in_smem, in_place, in_vmem, in_place, in_vmem],
        out_specs=in_vmem,
        scratch_shapes=strip_scratch(dosage),
        cost_estimate=strip_cost(dosage),
        name="other_sums",
    )(n, dosage, annot, turned, sums)


def strip_scratch(dosage):
    samples, _, mine = sizes(dosage)
    return [
        pltpu.VMEM((mine, samples, TILE), jnp.bfloat16),
        pltpu.VMEM((2 * mine, samples, LANES), jnp.bfloat16),
        pltpu.VMEM((mine, samples // LANES, TILE, LANES), jnp.bfloat16),
        pltpu.VMEM((samples, TILE), jnp.float32),
        pltpu.SemaphoreType.DMA((mine,)),
        pltpu.SemaphoreType.DMA((mine,)),
    ]


def strip_cost(dosage):
    samples, strip, _ = sizes(dosage)
    return pl.CostEstimate(
        flops=samples * strip * strip // 2, bytes_accessed=2 * samples * strip, transcendentals=0
    )


def rim_kernel(
    n_ref, arrived_ref, turned_ref, annot_ref, sums_in, sums_ref, back_ref,
    given, geno, turned, wide_values, came, back,
):
    mine = turned_ref.shape[0]
    samples = geno.shape[1]
    width = mine // 2
    n = n_ref[0]
    arrivals = [
        pltpu.make_async_copy(
            arrived_ref.at[:, c * TILE : (c + 1) * TILE], given.at[c], came.at[c]
        )
        for c in range(width)
    ]
    returns = [
        pltpu.make_async_copy(turned_ref.at[t], turned.at[t], back.at[t]) for t in range(mine)
    ]
    for copy in arrivals + returns:
        copy.start()
    sums_ref[...] = sums_in[...]
    back_ref[...] = jnp.zeros_like(back_ref)
    for c in range(width):
        arrivals[c].wait()
        standardized(lambda rows: given[c, rows, :], into(geno, c), wide_values, samples)
    for copy in returns:
        copy.wait()

    def add(c, y, inside=None):
        weights = band_weights(rows_of(turned, y), columns_of(geno, c), inside)
        sums_ref[:, cols_at(y)] += along_columns(given[c, samples:, :], weights)
        back_ref[:, c * TILE : (c + 1) * TILE] += along_rows(
            annot_ref[:, cols_at(n * mine + y)], weights
        )

    diagonal = (1 - 2 * n) * tile_offset() <= 0
    for c in range(width):
        add(c, c + (1 - n) * width, diagonal)
        for y in range(mine):
            first, second = y < c + width, c < y < width
            if first or second:

                @pl.when(True if first and second else (n == 0 if first else n == 1))
                def _(c=c, y=y):
                    add(c, y)


def rim_sums(n, arrived, turned, annot, sums):
    mine, chunks, _, _ = turned.shape
    samples = chunks * LANES
    width = mine // 2
    return pl.pallas_call(
        rim_kernel,
        out_shape=(
            jax.ShapeDtypeStruct(sums.shape, jnp.float32),
            jax.ShapeDtypeStruct((sums.shape[0], width * TILE), jnp.float32),
        ),
        in_specs=[in_smem, in_place, in_place, in_vmem, in_vmem],
        out_specs=(in_vmem, in_vmem),
        scratch_shapes=[
            pltpu.VMEM((width, arrived.shape[0], TILE), jnp.bfloat16),
            pltpu.VMEM((2 * width, samples, LANES), jnp.bfloat16),
            pltpu.VMEM(turned.shape, jnp.bfloat16),
            pltpu.VMEM((samples, TILE), jnp.float32),
            pltpu.SemaphoreType.DMA((width,)),
            pltpu.SemaphoreType.DMA((mine,)),
        ],
        cost_estimate=pl.CostEstimate(
            flops=2 * samples * width * TILE * mine * TILE,
            bytes_accessed=2 * samples * TILE * (mine + width),
            transcendentals=0,
        ),
        name="rim_sums",
    )(n, arrived, turned, annot, sums)


def eye(size):
    shape = (size, size)
    return lax.broadcasted_iota(jnp.int32, shape, 0) == lax.broadcasted_iota(jnp.int32, shape, 1)


def upright(row):
    size = row.shape[1]
    return jnp.sum(jnp.where(eye(size), jnp.broadcast_to(row, (size, size)), 0.0), axis=1, keepdims=True)


def lying(column):
    size = column.shape[0]
    return jnp.sum(
        jnp.where(eye(size), jnp.broadcast_to(column, (size, size)), 0.0), axis=0, keepdims=True
    )


def moments_kernel(total_variants, place_ref, counts_ref, sums_ref, back_ref, scores_ref, payload_ref, whole):
    annots = counts_ref.shape[1]
    block = sums_ref.shape[1]
    width = back_ref.shape[1]
    n, slot = place_ref[0], place_ref[1]
    whole[...] = sums_ref[...]
    whole[:, pl.ds(pl.multiple_of(n * (block - width), width), width)] += back_ref[...]
    shares = upright(counts_ref[...]) / total_variants
    high = (1.0 - shares).astype(jnp.bfloat16).astype(jnp.float32)
    low = (0.0 - shares).astype(jnp.bfloat16).astype(jnp.float32)
    members = whole[:annots, :]
    scores = high * members + low * (whole[annots : annots + 1, :] - members)
    scores_ref[:annots, :] = scores
    row = lax.broadcasted_iota(jnp.int32, (2 * PAD, block), 0)
    scores_ref[annots:, :] = jnp.where(row == 0, 1.0, 0.0)
    mean = jnp.sum(scores, axis=1, keepdims=True) / block
    deviation = scores - mean
    payload_ref[:annots, :] = lax.dot_general(
        deviation,
        deviation,
        (((1,), (1,)), ((), ())),
        precision=highest_precision,
        preferred_element_type=jnp.float32,
    )
    slots = payload_ref.shape[0] - annots
    at = lax.broadcasted_iota(jnp.int32, (slots, annots), 0)
    payload_ref[annots:, :] = jnp.where(at == slot, lying(mean), 0.0)


def moments_of(total_variants, slots, place, counts, sums, back):
    annots = counts.shape[1]
    block = sums.shape[1]
    return pl.pallas_call(
        functools.partial(moments_kernel, total_variants),
        out_shape=(
            jax.ShapeDtypeStruct((annots + 2 * PAD, block), jnp.float32),
            jax.ShapeDtypeStruct((annots + slots, annots), jnp.float32),
        ),
        in_specs=[in_smem] + [in_vmem] * 3,
        out_specs=(in_vmem, in_vmem),
        scratch_shapes=[pltpu.VMEM(sums.shape, jnp.float32)],
        cost_estimate=pl.CostEstimate(
            flops=12 * annots * annots * block, bytes_accessed=12 * annots * block, transcendentals=0
        ),
        name="moments",
    )(place, counts, sums, back)


def inverse_kernel(divisor, payload_ref, inverse_ref, moments_ref):
    size = payload_ref.shape[1]
    slots = payload_ref.shape[0] - size
    means = payload_ref[size:, :]
    mean = jnp.sum(means, axis=0, keepdims=True) / slots
    between = means - mean
    covariance = (
        payload_ref[:size, :]
        + lax.dot_general(
            between,
            between,
            (((0,), (0,)), ((), ())),
            precision=highest_precision,
            preferred_element_type=jnp.float32,
        )
        * (divisor // slots)
    ) / divisor
    row = lax.broadcasted_iota(jnp.int32, (size, size), 0)
    lane = lax.broadcasted_iota(jnp.int32, (size, size), 1)
    diagonal = jnp.where(row == lane, covariance, 0.0)
    across = 1.0 / jnp.sqrt(jnp.sum(diagonal, axis=0, keepdims=True) + EPS)
    down = 1.0 / jnp.sqrt(jnp.sum(diagonal, axis=1, keepdims=True) + EPS)
    mean_down = jnp.sum(jnp.where(row == lane, jnp.broadcast_to(mean, (size, size)), 0.0), axis=1, keepdims=True)
    moments_ref[...] = jnp.where(lane == 0, mean_down, down)
    gram = covariance * down * across
    groups = [gram[PAD * g : PAD * (g + 1), :] for g in range(size // PAD)]
    lane_of = lax.broadcasted_iota(jnp.int32, (1, size), 1)
    row_of = lax.broadcasted_iota(jnp.int32, (PAD, size), 0)

    def pair_inverse(a, b, c):
        scale = 1.0 / (a * c - b * b)
        return c * scale, -b * scale, a * scale

    for k in range(0, size, PIVOTS):
        g, i = divmod(k, PAD)
        spread = [
            [jnp.broadcast_to(old[:, k + j : k + j + 1], (PAD, size)) for j in range(PIVOTS)]
            for old in groups
        ]
        m = [[spread[g][c][i + r : i + r + 1, :] for c in range(PIVOTS)] for r in range(PIVOTS)]
        rows = [
            groups[g][i + j : i + j + 1, :] - jnp.where(lane_of == k + j, 1.0, 0.0)
            for j in range(PIVOTS)
        ]
        a, b, c = pair_inverse(m[0][0], m[0][1], m[1][1])
        u = a * rows[0] + b * rows[1], b * rows[0] + c * rows[1]
        v = [(a * m[0][j] + b * m[1][j], b * m[0][j] + c * m[1][j]) for j in (2, 3)]
        rest = [rows[j] - m[0][j] * u[0] - m[1][j] * u[1] for j in (2, 3)]
        d, e, f = pair_inverse(
            m[2][2] - m[0][2] * v[0][0] - m[1][2] * v[0][1],
            m[2][3] - m[0][2] * v[1][0] - m[1][2] * v[1][1],
            m[3][3] - m[0][3] * v[1][0] - m[1][3] * v[1][1],
        )
        third = d * rest[0] + e * rest[1]
        fourth = e * rest[0] + f * rest[1]
        solved = [
            u[0] - v[0][0] * third - v[1][0] * fourth,
            u[1] - v[0][1] * third - v[1][1] * fourth,
            third,
            fourth,
        ]
        solved = [jnp.broadcast_to(value, (PAD, size)) for value in solved]
        for h, old in enumerate(groups):
            for j in range(PIVOTS):
                old = old - spread[h][j] * solved[j]
                if h == g:
                    old = old + jnp.where(row_of == i + j, solved[j], 0.0)
            groups[h] = old
    swept = jnp.concatenate(groups, axis=0)
    inverse = jnp.where(row == lane, 2.0, 0.0) - swept
    inverse_ref[...] = inverse * down * across / divisor


def gram_inverse(divisor, payload):
    size = payload.shape[1]
    square = jax.ShapeDtypeStruct((size, size), jnp.float32)
    return pl.pallas_call(
        functools.partial(inverse_kernel, divisor),
        out_shape=(square, square),
        in_specs=[in_vmem],
        out_specs=(in_vmem, in_vmem),
        compiler_params=pltpu.CompilerParams(vmem_limit_bytes=VMEM_LIMIT),
        cost_estimate=pl.CostEstimate(flops=20_000_000_000, bytes_accessed=4 * size * size, transcendentals=0),
        name="gram_inverse",
    )(payload)


def halves(value):
    upper = value.astype(jnp.bfloat16)
    return upper, (value - upper.astype(jnp.float32)).astype(jnp.bfloat16)


def fit_kernel(divisor, n_ref, inverse_ref, moments_ref, proj_ref, scores_ref, other_ref, own_ref, fitted_ref):
    annots = own_ref.shape[0]
    block = scores_ref.shape[1]
    n = n_ref[0]
    mean = moments_ref[:, 0:1]
    sums = proj_ref[annots : annots + 1, :]
    coefficient = jnp.dot(
        inverse_ref[...],
        proj_ref[:annots, :] - mean * sums,
        precision=highest_precision,
        preferred_element_type=jnp.float32,
    )
    upper, lower = halves(coefficient)
    right = jnp.concatenate([upper, upper, lower], axis=0)

    def fit(values, place):
        upper, lower = halves(values)
        fitted = lax.dot_general(
            jnp.concatenate([upper, lower, upper], axis=0),
            right,
            (((0,), (0,)), ((), ())),
            preferred_element_type=jnp.float32,
        )
        rows = pl.ds(pl.multiple_of(place * block, block), block)
        fitted_ref[rows, :] = sums / divisor + fitted

    centred = scores_ref[:annots, :] - mean
    own_ref[...] = centred * moments_ref[:, 1:2]
    fit(centred, n)
    fit(other_ref[...] - mean, 1 - n)


def fitted_values(divisor, n, inverse, moments, projection, scores, scores_other):
    annots, block = scores_other.shape
    traits = projection.shape[1]
    return pl.pallas_call(
        functools.partial(fit_kernel, divisor),
        out_shape=(
            jax.ShapeDtypeStruct((annots, block), jnp.float32),
            jax.ShapeDtypeStruct((2 * block, traits), jnp.float32),
        ),
        in_specs=[in_smem] + [in_vmem] * 5,
        out_specs=(in_vmem, in_vmem),
        compiler_params=pltpu.CompilerParams(vmem_limit_bytes=VMEM_LIMIT),
        cost_estimate=pl.CostEstimate(
            flops=4 * annots * block * traits, bytes_accessed=8 * block * traits, transcendentals=0
        ),
        name="fitted_values",
    )(n, inverse, moments, projection, scores, scores_other)


def flipped(value, axis, bit):
    length = lax.axis_size(axis)
    return lax.ppermute(value, axis, [(i, i ^ bit) for i in range(length)])


def wide_bits():
    length = lax.axis_size("wide")
    bits = []
    bit = 1
    while bit < length:
        bits.append(bit)
        bit *= 2
    return bits


def wide_sum(value):
    for bit in wide_bits():
        value = value + flipped(value, "wide", bit)
    return value


def split(value):
    half = value.shape[0] // 2
    low = lax.axis_index("wide") % 2
    kept = lax.dynamic_slice_in_dim(value, low * half, half, 0)
    given = lax.dynamic_slice_in_dim(value, (1 - low) * half, half, 0)
    return kept + flipped(given, "wide", 1)


def long_sum(value):
    for bit in wide_bits()[1:]:
        value = value + flipped(value, "wide", bit)
    return value


def joined(kept):
    low = lax.axis_index("wide") % 2
    other = flipped(kept, "wide", 1)
    return jnp.where(
        low == 0, jnp.concatenate([kept, other], 0), jnp.concatenate([other, kept], 0)
    )


def whole_step(dosage, annotations, test_statistic_table):
    _, strip = dosage.shape
    annots = annotations.shape[0]
    wide = lax.axis_size("wide")
    total_variants = wide * strip
    w = lax.axis_index("wide")
    n = lax.axis_index("narrow")
    block = strip // 2
    n_array = jnp.reshape(n, (1,)).astype(jnp.int32)

    rim_pairs = []
    back_pairs = []
    for i in range(wide - 1):
        rim_pairs += [(2 * i, 2 * i + 2), (2 * i + 3, 2 * i + 1)]
        back_pairs += [(2 * i + 1, 2 * i + 2), (2 * i + 2, 2 * i + 1)]
    chi = test_statistic_table
    outgoing, annot, counts, chi_given = prepared(n_array, dosage, annotations, chi)
    arrived = lax.ppermute(outgoing, both, rim_pairs)
    chi_other = flipped(chi_given, "narrow", 1)
    counts = wide_sum(counts)
    sums, turned = own_sums(n_array, dosage, annot)
    sums = other_sums(n_array, dosage, annot, turned, sums)
    sums, back = rim_sums(n_array, arrived, turned, annot, sums)
    back = lax.ppermute(back, both, back_pairs)

    place = jnp.stack([n, 2 * w + n]).astype(jnp.int32)
    extended, payload = moments_of(total_variants, 2 * wide, place, counts, sums, back)
    scores = extended[:annots]
    payload = split(payload)
    payload = payload + flipped(payload, "narrow", 1)
    payload = joined(long_sum(payload))

    chi_own = lax.dynamic_slice_in_dim(chi, n * block, block, 0)
    halves_of = [
        jnp.dot(
            extended, values, precision=lax.Precision.HIGH, preferred_element_type=jnp.float32
        )
        for values in (chi_other, chi_own)
    ]
    projection = split(jnp.concatenate(halves_of, axis=1))
    traits = chi.shape[1]
    projection = projection[:, traits:] + flipped(projection[:, :traits], "narrow", 1)
    projection = joined(long_sum(projection))
    scores_other = flipped(scores, "narrow", 1)

    inverse, moments = gram_inverse(total_variants, payload)
    return fitted_values(
        total_variants, n_array, inverse, moments, projection, extended, scores_other
    )


def solution(mesh):
    in_specs = (P(None, "wide"), P(None, "wide"), P("wide", "narrow"))
    out_specs = (P(None, both), P("wide", "narrow"))
    return jax.shard_map(whole_step, mesh=mesh, in_specs=in_specs, out_specs=out_specs, check_vma=False)
```

```python
import functools

import jax
import jax.numpy as jnp
from jax import lax
from jax.experimental import pallas as pl
from jax.experimental.pallas import tpu as pltpu
from jax.sharding import PartitionSpec as P


EPS = 1e-05
TILE = 256
LANES = 128
ROWS = 256
PAD = 8
PIVOTS = 4
VMEM_LIMIT = 36 * 1024 * 1024
WHOLE_VMEM = 67043328

highest_precision = lax.Precision.HIGHEST
both = ("wide", "narrow")
in_vmem = pl.BlockSpec(memory_space=pltpu.VMEM)
in_place = pl.BlockSpec(memory_space=pl.ANY)
in_smem = pl.BlockSpec(memory_space=pltpu.SMEM)


def cols_at(c):
    return pl.ds(pl.multiple_of(c * TILE, TILE), TILE)


def standardized(read, write, wide_values, samples):
    steps = samples // ROWS
    empty = jnp.zeros((4 * PAD, TILE), jnp.float32)
    pivot = read(pl.ds(0, 2 * PAD)).astype(jnp.float32)[:1, :]

    def folded(values):
        return jnp.sum(values.reshape(-1, 4 * PAD, TILE), axis=0)

    def rows_at(r):
        return pl.ds(pl.multiple_of(r * ROWS, ROWS), ROWS)

    def total(r, carry):
        values = read(rows_at(r)).astype(jnp.float32) - pivot
        wide_values[rows_at(r), :] = values
        return carry[0] + folded(values), carry[1] + folded(values * values)

    first, second = (
        jnp.sum(value, axis=0, keepdims=True) / samples
        for value in lax.fori_loop(0, steps, total, (empty, empty))
    )
    variance = jnp.maximum(second - first * first, 0.0)
    scale = 1.0 / jnp.sqrt(variance + EPS)

    def store(r, carry):
        write(rows_at(r), ((wide_values[rows_at(r), :] - first) * scale).astype(jnp.bfloat16))
        return carry

    lax.fori_loop(0, steps, store, 0)


def into(geno, tile):
    def write(rows, value):
        geno[2 * tile, rows, :] = value[:, :LANES]
        geno[2 * tile + 1, rows, :] = value[:, LANES:]

    return write


def columns_of(geno, tile):
    return jnp.concatenate([geno[2 * tile], geno[2 * tile + 1]], axis=1)


def rows_of(turned, tile):
    return jnp.concatenate([turned[tile, k] for k in range(turned.shape[1])], axis=1)


def band_weights(rows, columns, inside=None):
    samples = rows.shape[1]
    products = jnp.dot(rows, columns, preferred_element_type=jnp.float32)
    unit = 1.0 / (samples - 2)
    weights = products * products * ((1.0 + unit) / (samples * samples)) - unit
    if inside is not None:
        weights = jnp.where(inside, weights, 0.0)
    return weights.astype(jnp.bfloat16)


def along_rows(annot, weights):
    return jnp.dot(annot, weights, preferred_element_type=jnp.float32)


def along_columns(annot, weights):
    return lax.dot_general(
        annot, weights, (((1,), (1,)), ((), ())), preferred_element_type=jnp.float32
    )


def tile_offset():
    shape = (TILE, TILE)
    return lax.broadcasted_iota(jnp.int32, shape, 0) - lax.broadcasted_iota(jnp.int32, shape, 1)


def sizes(dosage):
    samples, strip = dosage.shape
    return samples, strip, strip // (2 * TILE)


def prepare_kernel(
    n_ref, dosage_ref, annot_ref, chi_ref, out_ref, annot_out_ref, counts_ref, chi_out_ref, given_annot, came
):
    samples, strip = dosage_ref.shape
    annots = annot_ref.shape[0]
    block = strip // 2
    width = out_ref.shape[1]
    n = n_ref[0]
    column = pl.ds(pl.multiple_of((1 - n) * (strip - width), width), width)
    rows = pl.ds(pl.multiple_of((1 - n) * block, block), block)
    copies = [
        pltpu.make_async_copy(annot_ref, given_annot, came.at[0]),
        pltpu.make_async_copy(dosage_ref.at[:, column], out_ref.at[:samples, :], came.at[1]),
        pltpu.make_async_copy(chi_ref.at[rows, :], chi_out_ref, came.at[2]),
    ]
    for copy in copies:
        copy.start()
    row = lax.broadcasted_iota(jnp.int32, (PAD, strip), 0)
    annot_out_ref[annots:, :] = jnp.where(row == 0, 1.0, 0.0).astype(jnp.bfloat16)
    copies[0].wait()
    members = given_annot[...].astype(jnp.float32)
    annot_out_ref[:annots, :] = members.astype(jnp.bfloat16)
    counts = jnp.sum(members, axis=1, keepdims=True)
    counts_ref[...] = lying(counts)
    out_ref[samples:, :] = annot_out_ref[:, column]
    for copy in copies[1:]:
        copy.wait()


def prepared(n, dosage, annotations, chi):
    samples, strip, _ = sizes(dosage)
    annots = annotations.shape[0]
    rows = annots + PAD
    width = strip // 4
    return pl.pallas_call(
        prepare_kernel,
        out_shape=(
            jax.ShapeDtypeStruct((samples + rows, width), jnp.bfloat16),
            jax.ShapeDtypeStruct((rows, strip), jnp.bfloat16),
            jax.ShapeDtypeStruct((1, annots), jnp.float32),
            jax.ShapeDtypeStruct((strip // 2, chi.shape[1]), jnp.float32),
        ),
        in_specs=[in_smem, in_place, in_place, in_place],
        out_specs=(in_vmem,) * 4,
        scratch_shapes=[pltpu.VMEM(annotations.shape, jnp.int32), pltpu.SemaphoreType.DMA((3,))],
        cost_estimate=pl.CostEstimate(
            flops=0, bytes_accessed=4 * samples * width + 8 * strip * annots, transcendentals=0
        ),
        name="prepare",
    )(n, dosage, annotations, chi)


def own_kernel(n_ref, dosage_ref, annot_ref, sums_ref, turned_ref, given, geno, turned, wide_values, came, went):
    samples, strip = dosage_ref.shape
    mine = strip // (2 * TILE)
    n = n_ref[0]
    arrivals = [
        pltpu.make_async_copy(dosage_ref.at[:, cols_at(n * mine + t)], given.at[t], came.at[t])
        for t in range(mine)
    ]
    departures = [
        pltpu.make_async_copy(turned.at[t], turned_ref.at[t], went.at[t]) for t in range(mine)
    ]
    arrivals[0].start()
    sums_ref[...] = jnp.zeros_like(sums_ref)
    for t in range(mine):
        arrivals[t].wait()
        if t + 1 < mine:
            arrivals[t + 1].start()
        standardized(lambda rows: given[t, rows, :], into(geno, t), wide_values, samples)
        for k in range(samples // LANES):
            for part in range(2):
                turned[t, k, part * LANES : (part + 1) * LANES, :] = geno[
                    2 * t + part, k * LANES : (k + 1) * LANES, :
                ].T
        departures[t].start()
    for y in range(mine):
        for x in range(y + 1):
            weights = band_weights(rows_of(turned, x), columns_of(geno, y))
            sums_ref[:, y * TILE : (y + 1) * TILE] += along_rows(
                annot_ref[:, cols_at(n * mine + x)], weights
            )
            if x < y:
                sums_ref[:, x * TILE : (x + 1) * TILE] += along_columns(
                    annot_ref[:, cols_at(n * mine + y)], weights
                )
    for copy in departures:
        copy.wait()


def other_kernel(
    slots, n_ref, dosage_ref, annot_ref, turned_ref, sums_in, sums_ref,
    given, geno, turned, wide_values, came, back,
):
    samples, strip = dosage_ref.shape
    mine = strip // (2 * TILE)
    n = n_ref[0]

    def nearest(s):
        return (1 - n) * s + n * (mine - 1 - s)

    arrivals = [
        pltpu.make_async_copy(
            dosage_ref.at[:, cols_at((1 - n) * mine + nearest(s))], given.at[s], came.at[s]
        )
        for s in slots
    ]
    returns = [
        pltpu.make_async_copy(turned_ref.at[nearest(h)], turned.at[h], back.at[h])
        for h in range(slots[0], mine)
    ]
    arrivals[0].start()
    sums_ref[...] = sums_in[...]
    for i, s in enumerate(slots):
        arrivals[i].wait()
        for copy in [*arrivals, *returns][i + 1 : i + 2] if i + 1 < len(slots) else returns:
            copy.start()
        standardized(lambda rows: given[s, rows, :], into(geno, s), wide_values, samples)
    for copy in returns:
        copy.wait()
    inside = (1 - 2 * n) * tile_offset() >= 0
    for s in slots:
        for h in range(s, mine):
            weights = band_weights(
                rows_of(turned, h), columns_of(geno, s), inside if h == s else None
            )
            sums_ref[:, cols_at(nearest(h))] += along_columns(
                annot_ref[:, cols_at((1 - n) * mine + nearest(s))], weights
            )


def own_sums(n, dosage, annot):
    samples, strip, mine = sizes(dosage)
    chunks = samples // LANES
    turned = (mine, chunks, TILE, LANES)
    return pl.pallas_call(
        own_kernel,
        out_shape=(
            jax.ShapeDtypeStruct((annot.shape[0], strip // 2), jnp.float32),
            jax.ShapeDtypeStruct(turned, jnp.bfloat16),
        ),
        in_specs=[in_smem, in_place, in_vmem],
        out_specs=(in_vmem, in_place),
        scratch_shapes=strip_scratch(dosage),
        cost_estimate=strip_cost(dosage),
        name="own_sums",
    )(n, dosage, annot)


def other_sums(slots, n, dosage, annot, turned, sums):
    return pl.pallas_call(
        functools.partial(other_kernel, slots),
        out_shape=jax.ShapeDtypeStruct(sums.shape, jnp.float32),
        in_specs=[in_smem, in_place, in_vmem, in_place, in_vmem],
        out_specs=in_vmem,
        scratch_shapes=strip_scratch(dosage),
        cost_estimate=strip_cost(dosage),
        compiler_params=pltpu.CompilerParams(vmem_limit_bytes=WHOLE_VMEM),
        name="other_sums",
    )(n, dosage, annot, turned, sums)


def strip_scratch(dosage):
    samples, _, mine = sizes(dosage)
    return [
        pltpu.VMEM((mine, samples, TILE), jnp.bfloat16),
        pltpu.VMEM((2 * mine, samples, LANES), jnp.bfloat16),
        pltpu.VMEM((mine, samples // LANES, TILE, LANES), jnp.bfloat16),
        pltpu.VMEM((samples, TILE), jnp.float32),
        pltpu.SemaphoreType.DMA((mine,)),
        pltpu.SemaphoreType.DMA((mine,)),
    ]


def strip_cost(dosage):
    samples, strip, _ = sizes(dosage)
    return pl.CostEstimate(
        flops=samples * strip * strip // 2, bytes_accessed=2 * samples * strip, transcendentals=0
    )


def rim_kernel(
    n_ref, arrived_ref, turned_ref, annot_ref, sums_in, sums_ref, back_ref,
    given, geno, turned, wide_values, came, back,
):
    mine = turned_ref.shape[0]
    samples = geno.shape[1]
    width = mine // 2
    n = n_ref[0]
    arrivals = [
        pltpu.make_async_copy(
            arrived_ref.at[:, c * TILE : (c + 1) * TILE], given.at[c], came.at[c]
        )
        for c in range(width)
    ]
    returns = [
        pltpu.make_async_copy(turned_ref.at[t], turned.at[t], back.at[t]) for t in range(mine)
    ]
    arrivals[0].start()
    sums_ref[...] = sums_in[...]
    back_ref[...] = jnp.zeros_like(back_ref)
    for c in range(width):
        arrivals[c].wait()
        for copy in arrivals[c + 1 : c + 2] if c + 1 < width else returns:
            copy.start()
        standardized(lambda rows: given[c, rows, :], into(geno, c), wide_values, samples)
    for copy in returns:
        copy.wait()

    def add(c, y, inside=None):
        weights = band_weights(rows_of(turned, y), columns_of(geno, c), inside)
        sums_ref[:, cols_at(y)] += along_columns(given[c, samples:, :], weights)
        back_ref[:, c * TILE : (c + 1) * TILE] += along_rows(
            annot_ref[:, cols_at(n * mine + y)], weights
        )

    diagonal = (1 - 2 * n) * tile_offset() <= 0
    for c in range(width):
        add(c, c + (1 - n) * width, diagonal)
        for y in range(mine):
            first, second = y < c + width, c < y < width
            if first or second:

                @pl.when(True if first and second else (n == 0 if first else n == 1))
                def _(c=c, y=y):
                    add(c, y)


def rim_sums(n, arrived, turned, annot, sums):
    mine, chunks, _, _ = turned.shape
    samples = chunks * LANES
    width = mine // 2
    return pl.pallas_call(
        rim_kernel,
        out_shape=(
            jax.ShapeDtypeStruct(sums.shape, jnp.float32),
            jax.ShapeDtypeStruct((sums.shape[0], width * TILE), jnp.float32),
        ),
        in_specs=[in_smem, in_place, in_place, in_vmem, in_vmem],
        out_specs=(in_vmem, in_vmem),
        scratch_shapes=[
            pltpu.VMEM((width, arrived.shape[0], TILE), jnp.bfloat16),
            pltpu.VMEM((2 * width, samples, LANES), jnp.bfloat16),
            pltpu.VMEM(turned.shape, jnp.bfloat16),
            pltpu.VMEM((samples, TILE), jnp.float32),
            pltpu.SemaphoreType.DMA((width,)),
            pltpu.SemaphoreType.DMA((mine,)),
        ],
        cost_estimate=pl.CostEstimate(
            flops=2 * samples * width * TILE * mine * TILE,
            bytes_accessed=2 * samples * TILE * (mine + width),
            transcendentals=0,
        ),
        name="rim_sums",
    )(n, arrived, turned, annot, sums)


def eye(size):
    shape = (size, size)
    return lax.broadcasted_iota(jnp.int32, shape, 0) == lax.broadcasted_iota(jnp.int32, shape, 1)


def upright(row):
    size = row.shape[1]
    return jnp.sum(jnp.where(eye(size), jnp.broadcast_to(row, (size, size)), 0.0), axis=1, keepdims=True)


def lying(column):
    size = column.shape[0]
    return jnp.sum(
        jnp.where(eye(size), jnp.broadcast_to(column, (size, size)), 0.0), axis=0, keepdims=True
    )


def moments_kernel(total_variants, n_ref, w_ref, counts_ref, sums_ref, back_ref, scores_ref, payload_ref, whole):
    annots = counts_ref.shape[1]
    block = sums_ref.shape[1]
    width = back_ref.shape[1]
    n = n_ref[0]
    slot = 2 * w_ref[0] + n
    whole[...] = sums_ref[...]
    whole[:, pl.ds(pl.multiple_of(n * (block - width), width), width)] += back_ref[...]
    shares = upright(counts_ref[...]) / total_variants
    high = (1.0 - shares).astype(jnp.bfloat16).astype(jnp.float32)
    low = (0.0 - shares).astype(jnp.bfloat16).astype(jnp.float32)
    members = whole[:annots, :]
    scores = high * members + low * (whole[annots : annots + 1, :] - members)
    scores_ref[:annots, :] = scores
    row = lax.broadcasted_iota(jnp.int32, (2 * PAD, block), 0)
    scores_ref[annots:, :] = jnp.where(row == 0, 1.0, 0.0)
    mean = jnp.sum(scores, axis=1, keepdims=True) / block
    deviation = scores - mean
    payload_ref[:annots, :] = lax.dot_general(
        deviation,
        deviation,
        (((1,), (1,)), ((), ())),
        precision=highest_precision,
        preferred_element_type=jnp.float32,
    )
    slots = payload_ref.shape[0] - annots
    at = lax.broadcasted_iota(jnp.int32, (slots, annots), 0)
    payload_ref[annots:, :] = jnp.where(at == slot, lying(mean), 0.0)


def moments_of(total_variants, slots, n, w, counts, sums, back):
    annots = counts.shape[1]
    block = sums.shape[1]
    return pl.pallas_call(
        functools.partial(moments_kernel, total_variants),
        out_shape=(
            jax.ShapeDtypeStruct((annots + 2 * PAD, block), jnp.float32),
            jax.ShapeDtypeStruct((annots + slots, annots), jnp.float32),
        ),
        in_specs=[in_smem] * 2 + [in_vmem] * 3,
        out_specs=(in_vmem, in_vmem),
        scratch_shapes=[pltpu.VMEM(sums.shape, jnp.float32)],
        compiler_params=pltpu.CompilerParams(vmem_limit_bytes=VMEM_LIMIT),
        cost_estimate=pl.CostEstimate(
            flops=12 * annots * annots * block, bytes_accessed=12 * annots * block, transcendentals=0
        ),
        name="moments",
    )(n, w, counts, sums, back)


def inverse_kernel(divisor, payload_ref, inverse_ref, moments_ref):
    size = payload_ref.shape[1]
    slots = payload_ref.shape[0] - size
    means = payload_ref[size:, :]
    mean = jnp.sum(means, axis=0, keepdims=True) / slots
    between = means - mean
    covariance = (
        payload_ref[:size, :]
        + lax.dot_general(
            between,
            between,
            (((0,), (0,)), ((), ())),
            precision=highest_precision,
            preferred_element_type=jnp.float32,
        )
        * (divisor // slots)
    ) / divisor
    row = lax.broadcasted_iota(jnp.int32, (size, size), 0)
    lane = lax.broadcasted_iota(jnp.int32, (size, size), 1)
    diagonal = jnp.where(row == lane, covariance, 0.0)
    across = 1.0 / jnp.sqrt(jnp.sum(diagonal, axis=0, keepdims=True) + EPS)
    down = 1.0 / jnp.sqrt(jnp.sum(diagonal, axis=1, keepdims=True) + EPS)
    mean_down = jnp.sum(jnp.where(row == lane, jnp.broadcast_to(mean, (size, size)), 0.0), axis=1, keepdims=True)
    moments_ref[...] = jnp.where(lane == 0, mean_down, down)
    gram = covariance * down * across
    groups = [gram[PAD * g : PAD * (g + 1), :] for g in range(size // PAD)]
    lane_of = lax.broadcasted_iota(jnp.int32, (1, size), 1)
    row_of = lax.broadcasted_iota(jnp.int32, (PAD, size), 0)

    def pair_inverse(a, b, c):
        scale = 1.0 / (a * c - b * b)
        return c * scale, -b * scale, a * scale

    for k in range(0, size, PIVOTS):
        g, i = divmod(k, PAD)
        spread = [
            [jnp.broadcast_to(old[:, k + j : k + j + 1], (PAD, size)) for j in range(PIVOTS)]
            for old in groups
        ]
        m = [[spread[g][c][i + r : i + r + 1, :] for c in range(PIVOTS)] for r in range(PIVOTS)]
        rows = [
            groups[g][i + j : i + j + 1, :] - jnp.where(lane_of == k + j, 1.0, 0.0)
            for j in range(PIVOTS)
        ]
        a, b, c = pair_inverse(m[0][0], m[0][1], m[1][1])
        u = a * rows[0] + b * rows[1], b * rows[0] + c * rows[1]
        v = [(a * m[0][j] + b * m[1][j], b * m[0][j] + c * m[1][j]) for j in (2, 3)]
        rest = [rows[j] - m[0][j] * u[0] - m[1][j] * u[1] for j in (2, 3)]
        d, e, f = pair_inverse(
            m[2][2] - m[0][2] * v[0][0] - m[1][2] * v[0][1],
            m[2][3] - m[0][2] * v[1][0] - m[1][2] * v[1][1],
            m[3][3] - m[0][3] * v[1][0] - m[1][3] * v[1][1],
        )
        third = d * rest[0] + e * rest[1]
        fourth = e * rest[0] + f * rest[1]
        solved = [
            u[0] - v[0][0] * third - v[1][0] * fourth,
            u[1] - v[0][1] * third - v[1][1] * fourth,
            third,
            fourth,
        ]
        solved = [jnp.broadcast_to(value, (PAD, size)) for value in solved]
        for h, old in enumerate(groups):
            for j in range(PIVOTS):
                old = old - spread[h][j] * solved[j]
                if h == g:
                    old = old + jnp.where(row_of == i + j, solved[j], 0.0)
            groups[h] = old
    swept = jnp.concatenate(groups, axis=0)
    inverse = jnp.where(row == lane, 2.0, 0.0) - swept
    inverse_ref[...] = inverse * down * across / divisor


def gram_inverse(divisor, payload):
    size = payload.shape[1]
    square = jax.ShapeDtypeStruct((size, size), jnp.float32)
    return pl.pallas_call(
        functools.partial(inverse_kernel, divisor),
        out_shape=(square, square),
        in_specs=[in_vmem],
        out_specs=(in_vmem, in_vmem),
        compiler_params=pltpu.CompilerParams(vmem_limit_bytes=VMEM_LIMIT),
        cost_estimate=pl.CostEstimate(flops=20_000_000_000, bytes_accessed=4 * size * size, transcendentals=0),
        name="gram_inverse",
    )(payload)


def halves(value):
    upper = value.astype(jnp.bfloat16)
    return upper, (value - upper.astype(jnp.float32)).astype(jnp.bfloat16)


def fit_kernel(divisor, n_ref, inverse_ref, moments_ref, proj_ref, scores_ref, other_ref, own_ref, fitted_ref):
    annots = own_ref.shape[0]
    block = scores_ref.shape[1]
    n = n_ref[0]
    mean = moments_ref[:, 0:1]
    sums = proj_ref[annots : annots + 1, :]
    coefficient = jnp.dot(
        inverse_ref[...],
        proj_ref[:annots, :] - mean * sums,
        precision=highest_precision,
        preferred_element_type=jnp.float32,
    )
    upper, lower = halves(coefficient)
    right = jnp.concatenate([upper, upper, lower], axis=0)

    def fit(values, place):
        upper, lower = halves(values)
        fitted = lax.dot_general(
            jnp.concatenate([upper, lower, upper], axis=0),
            right,
            (((0,), (0,)), ((), ())),
            preferred_element_type=jnp.float32,
        )
        rows = pl.ds(pl.multiple_of(place * block, block), block)
        fitted_ref[rows, :] = sums / divisor + fitted

    centred = scores_ref[:annots, :] - mean
    own_ref[...] = centred * moments_ref[:, 1:2]
    fit(centred, n)
    fit(other_ref[...] - mean, 1 - n)


def fitted_values(divisor, n, inverse, moments, projection, scores, scores_other):
    annots, block = scores_other.shape
    traits = projection.shape[1]
    return pl.pallas_call(
        functools.partial(fit_kernel, divisor),
        out_shape=(
            jax.ShapeDtypeStruct((annots, block), jnp.float32),
            jax.ShapeDtypeStruct((2 * block, traits), jnp.float32),
        ),
        in_specs=[in_smem] + [in_vmem] * 5,
        out_specs=(in_vmem, in_vmem),
        compiler_params=pltpu.CompilerParams(vmem_limit_bytes=VMEM_LIMIT),
        cost_estimate=pl.CostEstimate(
            flops=4 * annots * block * traits, bytes_accessed=8 * block * traits, transcendentals=0
        ),
        name="fitted_values",
    )(n, inverse, moments, projection, scores, scores_other)


def flipped(value, axis, bit):
    length = lax.axis_size(axis)
    return lax.ppermute(value, axis, [(i, i ^ bit) for i in range(length)])


def wide_bits():
    length = lax.axis_size("wide")
    bits = []
    bit = 1
    while bit < length:
        bits.append(bit)
        bit *= 2
    return bits


def wide_sum(value):
    for bit in wide_bits():
        value = value + flipped(value, "wide", bit)
    return value


def split(value):
    half = value.shape[0] // 2
    low = lax.axis_index("wide") % 2
    kept = lax.dynamic_slice_in_dim(value, low * half, half, 0)
    given = lax.dynamic_slice_in_dim(value, (1 - low) * half, half, 0)
    return kept + flipped(given, "wide", 1)


def long_sum(value):
    for bit in wide_bits()[1:]:
        value = value + flipped(value, "wide", bit)
    return value


def joined(kept):
    low = lax.axis_index("wide") % 2
    other = flipped(kept, "wide", 1)
    return jnp.where(
        low == 0, jnp.concatenate([kept, other], 0), jnp.concatenate([other, kept], 0)
    )


def whole_step(dosage, annotations, test_statistic_table):
    _, strip = dosage.shape
    annots = annotations.shape[0]
    wide = lax.axis_size("wide")
    total_variants = wide * strip
    w = lax.axis_index("wide")
    n = lax.axis_index("narrow")
    block = strip // 2
    n_array = jnp.reshape(n, (1,)).astype(jnp.int32)

    rim_pairs = []
    back_pairs = []
    for i in range(wide - 1):
        rim_pairs += [(2 * i, 2 * i + 2), (2 * i + 3, 2 * i + 1)]
        back_pairs += [(2 * i + 1, 2 * i + 2), (2 * i + 2, 2 * i + 1)]
    chi = test_statistic_table
    outgoing, annot, counts, chi_given = prepared(n_array, dosage, annotations, chi)
    arrived = lax.ppermute(outgoing, both, rim_pairs)
    chi_other = flipped(chi_given, "narrow", 1)
    counts = wide_sum(counts)
    sums, turned = own_sums(n_array, dosage, annot)
    tiles = block // TILE
    sums = other_sums(tuple(range(tiles // 2)), n_array, dosage, annot, turned, sums)
    sums, back = rim_sums(n_array, arrived, turned, annot, sums)
    back = lax.ppermute(back, both, back_pairs)
    sums = other_sums(tuple(range(tiles // 2, tiles)), n_array, dosage, annot, turned, sums)

    w_array = jnp.reshape(w, (1,)).astype(jnp.int32)
    extended, payload = moments_of(
        total_variants, 2 * wide, n_array, w_array, counts, sums, back
    )
    scores = extended[:annots]
    payload = split(payload)
    payload = payload + flipped(payload, "narrow", 1)
    payload = joined(long_sum(payload))

    chi_own = lax.dynamic_slice_in_dim(chi, n * block, block, 0)
    halves_of = [
        jnp.dot(
            extended, values, precision=lax.Precision.HIGH, preferred_element_type=jnp.float32
        )
        for values in (chi_other, chi_own)
    ]
    projection = split(jnp.concatenate(halves_of, axis=1))
    traits = chi.shape[1]
    projection = projection[:, traits:] + flipped(projection[:, :traits], "narrow", 1)
    projection = joined(long_sum(projection))
    scores_other = flipped(scores, "narrow", 1)

    inverse, moments = gram_inverse(total_variants, payload)
    return fitted_values(
        total_variants, n_array, inverse, moments, projection, extended, scores_other
    )


def solution(mesh):
    in_specs = (P(None, "wide"), P(None, "wide"), P("wide", "narrow"))
    out_specs = (P(None, both), P("wide", "narrow"))
    return jax.shard_map(whole_step, mesh=mesh, in_specs=in_specs, out_specs=out_specs, check_vma=False)
```

```python
import functools

import jax
import jax.numpy as jnp
from jax import lax
from jax.experimental import pallas as pl
from jax.experimental.pallas import tpu as pltpu
from jax.sharding import PartitionSpec as P


EPS = 1e-05
TILE = 256
LANES = 128
ROWS = 256
PAD = 8
PIVOTS = 4
VMEM_LIMIT = 16 * 1024 * 1024

highest_precision = lax.Precision.HIGHEST
both = ("wide", "narrow")
in_vmem = pl.BlockSpec(memory_space=pltpu.VMEM)
in_place = pl.BlockSpec(memory_space=pl.ANY)
in_smem = pl.BlockSpec(memory_space=pltpu.SMEM)


def cols_at(c):
    return pl.ds(pl.multiple_of(c * TILE, TILE), TILE)


def standardized(read, write, wide_values, samples):
    steps = samples // ROWS
    empty = jnp.zeros((4 * PAD, TILE), jnp.float32)
    pivot = read(pl.ds(0, 2 * PAD)).astype(jnp.float32)[:1, :]

    def folded(values):
        return jnp.sum(values.reshape(-1, 4 * PAD, TILE), axis=0)

    def rows_at(r):
        return pl.ds(pl.multiple_of(r * ROWS, ROWS), ROWS)

    def total(r, carry):
        values = read(rows_at(r)).astype(jnp.float32) - pivot
        wide_values[rows_at(r), :] = values
        return carry[0] + folded(values), carry[1] + folded(values * values)

    first, second = (
        jnp.sum(value, axis=0, keepdims=True) / samples
        for value in lax.fori_loop(0, steps, total, (empty, empty))
    )
    variance = jnp.maximum(second - first * first, 0.0)
    scale = 1.0 / jnp.sqrt(variance + EPS)

    def store(r, carry):
        write(rows_at(r), ((wide_values[rows_at(r), :] - first) * scale).astype(jnp.bfloat16))
        return carry

    lax.fori_loop(0, steps, store, 0)


def into(geno, tile):
    def write(rows, value):
        geno[2 * tile, rows, :] = value[:, :LANES]
        geno[2 * tile + 1, rows, :] = value[:, LANES:]

    return write


def columns_of(geno, tile):
    return jnp.concatenate([geno[2 * tile], geno[2 * tile + 1]], axis=1)


def rows_of(turned, tile):
    return jnp.concatenate([turned[tile, k] for k in range(turned.shape[1])], axis=1)


def band_weights(rows, columns, inside=None):
    samples = rows.shape[1]
    products = jnp.dot(rows, columns, preferred_element_type=jnp.float32)
    unit = 1.0 / (samples - 2)
    weights = products * products * ((1.0 + unit) / (samples * samples)) - unit
    if inside is not None:
        weights = jnp.where(inside, weights, 0.0)
    return weights.astype(jnp.bfloat16)


def along_rows(annot, weights):
    return jnp.dot(annot, weights, preferred_element_type=jnp.float32)


def along_columns(annot, weights):
    return lax.dot_general(
        annot, weights, (((1,), (1,)), ((), ())), preferred_element_type=jnp.float32
    )


def tile_offset():
    shape = (TILE, TILE)
    return lax.broadcasted_iota(jnp.int32, shape, 0) - lax.broadcasted_iota(jnp.int32, shape, 1)


def sizes(dosage):
    samples, strip = dosage.shape
    return samples, strip, strip // (2 * TILE)


def prepare_kernel(
    n_ref, dosage_ref, annot_ref, chi_ref, out_ref, annot_out_ref, counts_ref, chi_out_ref, given_annot, came
):
    samples, strip = dosage_ref.shape
    annots = annot_ref.shape[0]
    block = strip // 2
    width = out_ref.shape[1]
    n = n_ref[0]
    column = pl.ds(pl.multiple_of((1 - n) * (strip - width), width), width)
    rows = pl.ds(pl.multiple_of((1 - n) * block, block), block)
    copies = [
        pltpu.make_async_copy(annot_ref, given_annot, came.at[0]),
        pltpu.make_async_copy(dosage_ref.at[:, column], out_ref.at[:samples, :], came.at[1]),
        pltpu.make_async_copy(chi_ref.at[rows, :], chi_out_ref, came.at[2]),
    ]
    for copy in copies:
        copy.start()
    row = lax.broadcasted_iota(jnp.int32, (PAD, strip), 0)
    annot_out_ref[annots:, :] = jnp.where(row == 0, 1.0, 0.0).astype(jnp.bfloat16)
    copies[0].wait()
    members = given_annot[...].astype(jnp.float32)
    annot_out_ref[:annots, :] = members.astype(jnp.bfloat16)
    counts = jnp.sum(members, axis=1, keepdims=True)
    counts_ref[...] = lying(counts)
    out_ref[samples:, :] = annot_out_ref[:, column]
    for copy in copies[1:]:
        copy.wait()


def prepared(n, dosage, annotations, chi):
    samples, strip, _ = sizes(dosage)
    annots = annotations.shape[0]
    rows = annots + PAD
    width = strip // 4
    return pl.pallas_call(
        prepare_kernel,
        out_shape=(
            jax.ShapeDtypeStruct((samples + rows, width), jnp.bfloat16),
            jax.ShapeDtypeStruct((rows, strip), jnp.bfloat16),
            jax.ShapeDtypeStruct((1, annots), jnp.float32),
            jax.ShapeDtypeStruct((strip // 2, chi.shape[1]), jnp.float32),
        ),
        in_specs=[in_smem, in_place, in_place, in_place],
        out_specs=(in_vmem,) * 4,
        scratch_shapes=[pltpu.VMEM(annotations.shape, jnp.int32), pltpu.SemaphoreType.DMA((3,))],
        cost_estimate=pl.CostEstimate(
            flops=0, bytes_accessed=4 * samples * width + 8 * strip * annots, transcendentals=0
        ),
        name="prepare",
    )(n, dosage, annotations, chi)


def own_kernel(n_ref, dosage_ref, annot_ref, sums_ref, turned_ref, geno, wide_values):
    samples, strip = dosage_ref.shape
    mine = strip // (2 * TILE)
    n = n_ref[0]
    sums_ref[...] = jnp.zeros_like(sums_ref)
    for t in range(mine):
        standardized(
            lambda rows: dosage_ref[rows, cols_at(n * mine + t)], into(geno, t), wide_values, samples
        )
        for k in range(samples // LANES):
            for part in range(2):
                turned_ref[t, k, part * LANES : (part + 1) * LANES, :] = geno[
                    2 * t + part, k * LANES : (k + 1) * LANES, :
                ].T
    for y in range(mine):
        for x in range(y + 1):
            weights = band_weights(rows_of(turned_ref, x), columns_of(geno, y))
            sums_ref[:, y * TILE : (y + 1) * TILE] += along_rows(
                annot_ref[:, cols_at(n * mine + x)], weights
            )
            if x < y:
                sums_ref[:, x * TILE : (x + 1) * TILE] += along_columns(
                    annot_ref[:, cols_at(n * mine + y)], weights
                )


def other_kernel(
    slots, n_ref, dosage_ref, annot_ref, turned_ref, sums_in, sums_ref, geno, wide_values
):
    samples, strip = dosage_ref.shape
    mine = strip // (2 * TILE)
    n = n_ref[0]

    def nearest(s):
        return (1 - n) * s + n * (mine - 1 - s)

    sums_ref[...] = sums_in[...]
    for s in slots:
        standardized(
            lambda rows: dosage_ref[rows, cols_at((1 - n) * mine + nearest(s))],
            into(geno, s),
            wide_values,
            samples,
        )
    inside = (1 - 2 * n) * tile_offset() >= 0
    for s in slots:
        for h in range(s, mine):
            weights = band_weights(
                rows_of(turned_ref, nearest(h)), columns_of(geno, s), inside if h == s else None
            )
            sums_ref[:, cols_at(nearest(h))] += along_columns(
                annot_ref[:, cols_at((1 - n) * mine + nearest(s))], weights
            )


def own_sums(n, dosage, annot):
    samples, strip, mine = sizes(dosage)
    chunks = samples // LANES
    turned = (mine, chunks, TILE, LANES)
    return pl.pallas_call(
        own_kernel,
        out_shape=(
            jax.ShapeDtypeStruct((annot.shape[0], strip // 2), jnp.float32),
            jax.ShapeDtypeStruct(turned, jnp.bfloat16),
        ),
        in_specs=[in_smem, in_vmem, in_vmem],
        out_specs=(in_vmem, in_vmem),
        scratch_shapes=strip_scratch(dosage),
        cost_estimate=strip_cost(dosage),
        compiler_params=pltpu.CompilerParams(vmem_limit_bytes=VMEM_LIMIT),
        name="own_sums",
    )(n, dosage, annot)


def other_sums(slots, n, dosage, annot, turned, sums):
    return pl.pallas_call(
        functools.partial(other_kernel, slots),
        out_shape=jax.ShapeDtypeStruct(sums.shape, jnp.float32),
        in_specs=[in_smem] + [in_vmem] * 4,
        out_specs=in_vmem,
        scratch_shapes=strip_scratch(dosage),
        cost_estimate=strip_cost(dosage),
        compiler_params=pltpu.CompilerParams(vmem_limit_bytes=VMEM_LIMIT),
        name="other_sums",
    )(n, dosage, annot, turned, sums)


def strip_scratch(dosage):
    samples, _, mine = sizes(dosage)
    return [
        pltpu.VMEM((2 * mine, samples, LANES), jnp.bfloat16),
        pltpu.VMEM((samples, TILE), jnp.float32),
    ]


def strip_cost(dosage):
    samples, strip, _ = sizes(dosage)
    return pl.CostEstimate(
        flops=samples * strip * strip // 2, bytes_accessed=2 * samples * strip, transcendentals=0
    )


def rim_kernel(
    n_ref, arrived_ref, turned_ref, annot_ref, sums_in, sums_ref, back_ref, geno, wide_values
):
    mine = turned_ref.shape[0]
    samples = geno.shape[1]
    width = mine // 2
    n = n_ref[0]
    sums_ref[...] = sums_in[...]
    back_ref[...] = jnp.zeros_like(back_ref)
    for c in range(width):
        columns = slice(c * TILE, (c + 1) * TILE)
        standardized(lambda rows: arrived_ref[rows, columns], into(geno, c), wide_values, samples)

    def add(c, y, inside=None):
        columns = slice(c * TILE, (c + 1) * TILE)
        weights = band_weights(rows_of(turned_ref, y), columns_of(geno, c), inside)
        sums_ref[:, cols_at(y)] += along_columns(arrived_ref[samples:, columns], weights)
        back_ref[:, columns] += along_rows(annot_ref[:, cols_at(n * mine + y)], weights)

    diagonal = (1 - 2 * n) * tile_offset() <= 0
    for c in range(width):
        add(c, c + (1 - n) * width, diagonal)
        for y in range(mine):
            first, second = y < c + width, c < y < width
            if first or second:

                @pl.when(True if first and second else (n == 0 if first else n == 1))
                def _(c=c, y=y):
                    add(c, y)


def rim_sums(n, arrived, turned, annot, sums):
    mine, chunks, _, _ = turned.shape
    samples = chunks * LANES
    width = mine // 2
    return pl.pallas_call(
        rim_kernel,
        out_shape=(
            jax.ShapeDtypeStruct(sums.shape, jnp.float32),
            jax.ShapeDtypeStruct((sums.shape[0], width * TILE), jnp.float32),
        ),
        in_specs=[in_smem] + [in_vmem] * 4,
        out_specs=(in_vmem, in_vmem),
        scratch_shapes=[
            pltpu.VMEM((2 * width, samples, LANES), jnp.bfloat16),
            pltpu.VMEM((samples, TILE), jnp.float32),
        ],
        compiler_params=pltpu.CompilerParams(vmem_limit_bytes=VMEM_LIMIT),
        cost_estimate=pl.CostEstimate(
            flops=2 * samples * width * TILE * mine * TILE,
            bytes_accessed=2 * samples * TILE * (mine + width),
            transcendentals=0,
        ),
        name="rim_sums",
    )(n, arrived, turned, annot, sums)


def eye(size):
    shape = (size, size)
    return lax.broadcasted_iota(jnp.int32, shape, 0) == lax.broadcasted_iota(jnp.int32, shape, 1)


def upright(row):
    size = row.shape[1]
    return jnp.sum(jnp.where(eye(size), jnp.broadcast_to(row, (size, size)), 0.0), axis=1, keepdims=True)


def lying(column):
    size = column.shape[0]
    return jnp.sum(
        jnp.where(eye(size), jnp.broadcast_to(column, (size, size)), 0.0), axis=0, keepdims=True
    )


def moments_kernel(total_variants, n_ref, w_ref, counts_ref, sums_ref, back_ref, scores_ref, payload_ref, whole):
    annots = counts_ref.shape[1]
    block = sums_ref.shape[1]
    width = back_ref.shape[1]
    n = n_ref[0]
    slot = 2 * w_ref[0] + n
    whole[...] = sums_ref[...]
    whole[:, pl.ds(pl.multiple_of(n * (block - width), width), width)] += back_ref[...]
    shares = upright(counts_ref[...]) / total_variants
    high = (1.0 - shares).astype(jnp.bfloat16).astype(jnp.float32)
    low = (0.0 - shares).astype(jnp.bfloat16).astype(jnp.float32)
    members = whole[:annots, :]
    scores = high * members + low * (whole[annots : annots + 1, :] - members)
    scores_ref[:annots, :] = scores
    row = lax.broadcasted_iota(jnp.int32, (2 * PAD, block), 0)
    scores_ref[annots:, :] = jnp.where(row == 0, 1.0, 0.0)
    mean = jnp.sum(scores, axis=1, keepdims=True) / block
    deviation = scores - mean
    payload_ref[:annots, :] = lax.dot_general(
        deviation,
        deviation,
        (((1,), (1,)), ((), ())),
        precision=highest_precision,
        preferred_element_type=jnp.float32,
    )
    slots = payload_ref.shape[0] - annots
    at = lax.broadcasted_iota(jnp.int32, (slots, annots), 0)
    payload_ref[annots:, :] = jnp.where(at == slot, lying(mean), 0.0)


def moments_of(total_variants, slots, n, w, counts, sums, back):
    annots = counts.shape[1]
    block = sums.shape[1]
    return pl.pallas_call(
        functools.partial(moments_kernel, total_variants),
        out_shape=(
            jax.ShapeDtypeStruct((annots + 2 * PAD, block), jnp.float32),
            jax.ShapeDtypeStruct((annots + slots, annots), jnp.float32),
        ),
        in_specs=[in_smem] * 2 + [in_vmem] * 3,
        out_specs=(in_vmem, in_vmem),
        scratch_shapes=[pltpu.VMEM(sums.shape, jnp.float32)],
        compiler_params=pltpu.CompilerParams(vmem_limit_bytes=VMEM_LIMIT),
        cost_estimate=pl.CostEstimate(
            flops=12 * annots * annots * block, bytes_accessed=12 * annots * block, transcendentals=0
        ),
        name="moments",
    )(n, w, counts, sums, back)


def inverse_kernel(divisor, payload_ref, inverse_ref, moments_ref):
    size = payload_ref.shape[1]
    slots = payload_ref.shape[0] - size
    means = payload_ref[size:, :]
    mean = jnp.sum(means, axis=0, keepdims=True) / slots
    between = means - mean
    covariance = (
        payload_ref[:size, :]
        + lax.dot_general(
            between,
            between,
            (((0,), (0,)), ((), ())),
            precision=highest_precision,
            preferred_element_type=jnp.float32,
        )
        * (divisor // slots)
    ) / divisor
    row = lax.broadcasted_iota(jnp.int32, (size, size), 0)
    lane = lax.broadcasted_iota(jnp.int32, (size, size), 1)
    diagonal = jnp.where(row == lane, covariance, 0.0)
    across = 1.0 / jnp.sqrt(jnp.sum(diagonal, axis=0, keepdims=True) + EPS)
    down = 1.0 / jnp.sqrt(jnp.sum(diagonal, axis=1, keepdims=True) + EPS)
    mean_down = jnp.sum(jnp.where(row == lane, jnp.broadcast_to(mean, (size, size)), 0.0), axis=1, keepdims=True)
    moments_ref[...] = jnp.where(lane == 0, mean_down, down)
    gram = covariance * down * across
    groups = [gram[PAD * g : PAD * (g + 1), :] for g in range(size // PAD)]
    lane_of = lax.broadcasted_iota(jnp.int32, (1, size), 1)
    row_of = lax.broadcasted_iota(jnp.int32, (PAD, size), 0)

    def pair_inverse(a, b, c):
        scale = 1.0 / (a * c - b * b)
        return c * scale, -b * scale, a * scale

    for k in range(0, size, PIVOTS):
        g, i = divmod(k, PAD)
        spread = [
            [jnp.broadcast_to(old[:, k + j : k + j + 1], (PAD, size)) for j in range(PIVOTS)]
            for old in groups
        ]
        m = [[spread[g][c][i + r : i + r + 1, :] for c in range(PIVOTS)] for r in range(PIVOTS)]
        rows = [
            groups[g][i + j : i + j + 1, :] - jnp.where(lane_of == k + j, 1.0, 0.0)
            for j in range(PIVOTS)
        ]
        a, b, c = pair_inverse(m[0][0], m[0][1], m[1][1])
        u = a * rows[0] + b * rows[1], b * rows[0] + c * rows[1]
        v = [(a * m[0][j] + b * m[1][j], b * m[0][j] + c * m[1][j]) for j in (2, 3)]
        rest = [rows[j] - m[0][j] * u[0] - m[1][j] * u[1] for j in (2, 3)]
        d, e, f = pair_inverse(
            m[2][2] - m[0][2] * v[0][0] - m[1][2] * v[0][1],
            m[2][3] - m[0][2] * v[1][0] - m[1][2] * v[1][1],
            m[3][3] - m[0][3] * v[1][0] - m[1][3] * v[1][1],
        )
        third = d * rest[0] + e * rest[1]
        fourth = e * rest[0] + f * rest[1]
        solved = [
            u[0] - v[0][0] * third - v[1][0] * fourth,
            u[1] - v[0][1] * third - v[1][1] * fourth,
            third,
            fourth,
        ]
        solved = [jnp.broadcast_to(value, (PAD, size)) for value in solved]
        for h, old in enumerate(groups):
            for j in range(PIVOTS):
                old = old - spread[h][j] * solved[j]
                if h == g:
                    old = old + jnp.where(row_of == i + j, solved[j], 0.0)
            groups[h] = old
    swept = jnp.concatenate(groups, axis=0)
    inverse = jnp.where(row == lane, 2.0, 0.0) - swept
    inverse_ref[...] = inverse * down * across / divisor


def gram_inverse(divisor, payload):
    size = payload.shape[1]
    square = jax.ShapeDtypeStruct((size, size), jnp.float32)
    return pl.pallas_call(
        functools.partial(inverse_kernel, divisor),
        out_shape=(square, square),
        in_specs=[in_vmem],
        out_specs=(in_vmem, in_vmem),
        compiler_params=pltpu.CompilerParams(vmem_limit_bytes=VMEM_LIMIT),
        cost_estimate=pl.CostEstimate(flops=20_000_000_000, bytes_accessed=4 * size * size, transcendentals=0),
        name="gram_inverse",
    )(payload)


def halves(value):
    upper = value.astype(jnp.bfloat16)
    return upper, (value - upper.astype(jnp.float32)).astype(jnp.bfloat16)


def fit_kernel(divisor, n_ref, inverse_ref, moments_ref, proj_ref, scores_ref, other_ref, own_ref, fitted_ref):
    annots = own_ref.shape[0]
    block = scores_ref.shape[1]
    n = n_ref[0]
    mean = moments_ref[:, 0:1]
    sums = proj_ref[annots : annots + 1, :]
    coefficient = jnp.dot(
        inverse_ref[...],
        proj_ref[:annots, :] - mean * sums,
        precision=highest_precision,
        preferred_element_type=jnp.float32,
    )
    upper, lower = halves(coefficient)
    right = jnp.concatenate([upper, upper, lower], axis=0)

    def fit(values, place):
        upper, lower = halves(values)
        fitted = lax.dot_general(
            jnp.concatenate([upper, lower, upper], axis=0),
            right,
            (((0,), (0,)), ((), ())),
            preferred_element_type=jnp.float32,
        )
        rows = pl.ds(pl.multiple_of(place * block, block), block)
        fitted_ref[rows, :] = sums / divisor + fitted

    centred = scores_ref[:annots, :] - mean
    own_ref[...] = centred * moments_ref[:, 1:2]
    fit(centred, n)
    fit(other_ref[...] - mean, 1 - n)


def fitted_values(divisor, n, inverse, moments, projection, scores, scores_other):
    annots, block = scores_other.shape
    traits = projection.shape[1]
    return pl.pallas_call(
        functools.partial(fit_kernel, divisor),
        out_shape=(
            jax.ShapeDtypeStruct((annots, block), jnp.float32),
            jax.ShapeDtypeStruct((2 * block, traits), jnp.float32),
        ),
        in_specs=[in_smem] + [in_vmem] * 5,
        out_specs=(in_vmem, in_vmem),
        compiler_params=pltpu.CompilerParams(vmem_limit_bytes=VMEM_LIMIT),
        cost_estimate=pl.CostEstimate(
            flops=4 * annots * block * traits, bytes_accessed=8 * block * traits, transcendentals=0
        ),
        name="fitted_values",
    )(n, inverse, moments, projection, scores, scores_other)


def flipped(value, axis, bit):
    length = lax.axis_size(axis)
    return lax.ppermute(value, axis, [(i, i ^ bit) for i in range(length)])


def wide_bits():
    length = lax.axis_size("wide")
    bits = []
    bit = 1
    while bit < length:
        bits.append(bit)
        bit *= 2
    return bits


def added_kernel(first_ref, second_ref, out_ref):
    out_ref[...] = first_ref[...] + second_ref[...]


def added(first, second):
    return pl.pallas_call(
        added_kernel,
        out_shape=jax.ShapeDtypeStruct(first.shape, first.dtype),
        in_specs=[in_vmem, in_vmem],
        out_specs=in_vmem,
        compiler_params=pltpu.CompilerParams(vmem_limit_bytes=VMEM_LIMIT // 4),
        name="added",
    )(first, second)


def wide_sum(value):
    for bit in wide_bits():
        value = added(value, flipped(value, "wide", bit))
    return value


def split(value):
    half = value.shape[0] // 2
    low = lax.axis_index("wide") % 2
    kept = lax.dynamic_slice_in_dim(value, low * half, half, 0)
    given = lax.dynamic_slice_in_dim(value, (1 - low) * half, half, 0)
    return kept + flipped(given, "wide", 1)


def long_sum(value):
    for bit in wide_bits()[1:]:
        value = value + flipped(value, "wide", bit)
    return value


def joined(kept):
    low = lax.axis_index("wide") % 2
    other = flipped(kept, "wide", 1)
    return jnp.where(
        low == 0, jnp.concatenate([kept, other], 0), jnp.concatenate([other, kept], 0)
    )


def whole_step(dosage, annotations, test_statistic_table):
    _, strip = dosage.shape
    annots = annotations.shape[0]
    wide = lax.axis_size("wide")
    total_variants = wide * strip
    w = lax.axis_index("wide")
    n = lax.axis_index("narrow")
    block = strip // 2
    n_array = jnp.reshape(n, (1,)).astype(jnp.int32)

    rim_pairs = []
    back_pairs = []
    for i in range(wide - 1):
        rim_pairs += [(2 * i, 2 * i + 2), (2 * i + 3, 2 * i + 1)]
        back_pairs += [(2 * i + 1, 2 * i + 2), (2 * i + 2, 2 * i + 1)]
    chi = test_statistic_table
    outgoing, annot, counts, chi_given = prepared(n_array, dosage, annotations, chi)
    arrived = lax.ppermute(outgoing, both, rim_pairs)
    chi_other = flipped(chi_given, "narrow", 1)
    counts = wide_sum(counts)
    sums, turned = own_sums(n_array, dosage, annot)
    tiles = block // TILE
    sums = other_sums(tuple(range(tiles // 2)), n_array, dosage, annot, turned, sums)
    sums, back = rim_sums(n_array, arrived, turned, annot, sums)
    back = lax.ppermute(back, both, back_pairs)
    sums = other_sums(tuple(range(tiles // 2, tiles)), n_array, dosage, annot, turned, sums)

    w_array = jnp.reshape(w, (1,)).astype(jnp.int32)
    extended, payload = moments_of(
        total_variants, 2 * wide, n_array, w_array, counts, sums, back
    )
    scores = extended[:annots]
    payload = split(payload)
    payload = payload + flipped(payload, "narrow", 1)
    payload = joined(long_sum(payload))

    chi_own = lax.dynamic_slice_in_dim(chi, n * block, block, 0)
    halves_of = [
        jnp.dot(
            extended, values, precision=lax.Precision.HIGH, preferred_element_type=jnp.float32
        )
        for values in (chi_other, chi_own)
    ]
    projection = split(jnp.concatenate(halves_of, axis=1))
    traits = chi.shape[1]
    projection = projection[:, traits:] + flipped(projection[:, :traits], "narrow", 1)
    projection = joined(long_sum(projection))
    scores_other = flipped(scores, "narrow", 1)

    inverse, moments = gram_inverse(total_variants, payload)
    return fitted_values(
        total_variants, n_array, inverse, moments, projection, extended, scores_other
    )


def solution(mesh):
    in_specs = (P(None, "wide"), P(None, "wide"), P("wide", "narrow"))
    out_specs = (P(None, both), P("wide", "narrow"))
    return jax.shard_map(whole_step, mesh=mesh, in_specs=in_specs, out_specs=out_specs, check_vma=False)
```

```python
import functools

import jax
import jax.numpy as jnp
from jax import lax
from jax.experimental import pallas as pl
from jax.experimental.pallas import tpu as pltpu
from jax.sharding import PartitionSpec as P


EPS = 1e-05
TILE = 256
LANES = 128
ROWS = 256
PAD = 8
PIVOTS = 4
VMEM_LIMIT = 16 * 1024 * 1024

highest_precision = lax.Precision.HIGHEST
both = ("wide", "narrow")
in_vmem = pl.BlockSpec(memory_space=pltpu.VMEM)
in_place = pl.BlockSpec(memory_space=pl.ANY)
in_smem = pl.BlockSpec(memory_space=pltpu.SMEM)


def cols_at(c):
    return pl.ds(pl.multiple_of(c * TILE, TILE), TILE)


def standardized(read, write, wide_values, samples):
    steps = samples // ROWS
    empty = jnp.zeros((4 * PAD, TILE), jnp.float32)
    pivot = read(pl.ds(0, 2 * PAD)).astype(jnp.float32)[:1, :]

    def folded(values):
        return jnp.sum(values.reshape(-1, 4 * PAD, TILE), axis=0)

    def rows_at(r):
        return pl.ds(pl.multiple_of(r * ROWS, ROWS), ROWS)

    def total(r, carry):
        values = read(rows_at(r)).astype(jnp.float32) - pivot
        wide_values[rows_at(r), :] = values
        return carry[0] + folded(values), carry[1] + folded(values * values)

    first, second = (
        jnp.sum(value, axis=0, keepdims=True) / samples
        for value in lax.fori_loop(0, steps, total, (empty, empty))
    )
    variance = jnp.maximum(second - first * first, 0.0)
    scale = 1.0 / jnp.sqrt(variance + EPS)

    def store(r, carry):
        write(rows_at(r), ((wide_values[rows_at(r), :] - first) * scale).astype(jnp.bfloat16))
        return carry

    lax.fori_loop(0, steps, store, 0)


def into(geno, tile):
    def write(rows, value):
        geno[2 * tile, rows, :] = value[:, :LANES]
        geno[2 * tile + 1, rows, :] = value[:, LANES:]

    return write


def columns_of(geno, tile):
    return jnp.concatenate([geno[2 * tile], geno[2 * tile + 1]], axis=1)


def rows_of(turned, tile):
    return jnp.concatenate([turned[tile, k] for k in range(turned.shape[1])], axis=1)


def band_weights(rows, columns, inside=None):
    samples = rows.shape[1]
    products = jnp.dot(rows, columns, preferred_element_type=jnp.float32)
    unit = 1.0 / (samples - 2)
    weights = products * products * ((1.0 + unit) / (samples * samples)) - unit
    if inside is not None:
        weights = jnp.where(inside, weights, 0.0)
    return weights.astype(jnp.bfloat16)


def along_rows(annot, weights):
    return jnp.dot(annot, weights, preferred_element_type=jnp.float32)


def along_columns(annot, weights):
    return lax.dot_general(
        annot, weights, (((1,), (1,)), ((), ())), preferred_element_type=jnp.float32
    )


def tile_offset():
    shape = (TILE, TILE)
    return lax.broadcasted_iota(jnp.int32, shape, 0) - lax.broadcasted_iota(jnp.int32, shape, 1)


def sizes(dosage):
    samples, strip = dosage.shape
    return samples, strip, strip // (2 * TILE)


def outgoing_kernel(n_ref, dosage_ref, annot_ref, first_ref, second_ref, given_annot, came):
    samples, strip = dosage_ref.shape
    annots = annot_ref.shape[0]
    n = n_ref[0]
    outs = (first_ref, second_ref)
    copies = []
    for order, out_ref in enumerate(outs):
        column = cols_at((1 - n) * (strip // TILE - 1 - order) + n * order)
        copies += [
            pltpu.make_async_copy(
                dosage_ref.at[:, column], out_ref.at[:samples, :], came.at[2 * order]
            ),
            pltpu.make_async_copy(
                annot_ref.at[:, column], given_annot.at[order], came.at[2 * order + 1]
            ),
        ]
    for copy in copies:
        copy.start()
    row = lax.broadcasted_iota(jnp.int32, (PAD, TILE), 0)
    for order, out_ref in enumerate(outs):
        out_ref[samples + annots :, :] = jnp.where(row == 0, 1.0, 0.0).astype(jnp.bfloat16)
        copies[2 * order + 1].wait()
        out_ref[samples : samples + annots, :] = (
            given_annot[order].astype(jnp.float32).astype(jnp.bfloat16)
        )
    for order in range(2):
        copies[2 * order].wait()


def outgoing_columns(n, dosage, annotations):
    samples = dosage.shape[0]
    annots = annotations.shape[0]
    out = jax.ShapeDtypeStruct((samples + annots + PAD, TILE), jnp.bfloat16)
    return pl.pallas_call(
        outgoing_kernel,
        out_shape=(out, out),
        in_specs=[in_smem, in_place, in_place],
        out_specs=(in_vmem, in_vmem),
        scratch_shapes=[pltpu.VMEM((2, annots, TILE), jnp.int32), pltpu.SemaphoreType.DMA((4,))],
        cost_estimate=pl.CostEstimate(
            flops=0, bytes_accessed=8 * samples * TILE, transcendentals=0
        ),
        name="outgoing",
    )(n, dosage, annotations)


def prepare_kernel(n_ref, annot_ref, chi_ref, annot_out_ref, counts_ref, chi_out_ref, came):
    annots, strip = annot_ref.shape
    block = strip // 2
    n = n_ref[0]
    rows = pl.ds(pl.multiple_of((1 - n) * block, block), block)
    copy = pltpu.make_async_copy(chi_ref.at[rows, :], chi_out_ref, came)
    copy.start()
    row = lax.broadcasted_iota(jnp.int32, (PAD, strip), 0)
    annot_out_ref[annots:, :] = jnp.where(row == 0, 1.0, 0.0).astype(jnp.bfloat16)
    members = annot_ref[...].astype(jnp.float32)
    annot_out_ref[:annots, :] = members.astype(jnp.bfloat16)
    counts_ref[...] = lying(jnp.sum(members, axis=1, keepdims=True))
    copy.wait()


def prepared(n, annotations, chi):
    annots, strip = annotations.shape
    return pl.pallas_call(
        prepare_kernel,
        out_shape=(
            jax.ShapeDtypeStruct((annots + PAD, strip), jnp.bfloat16),
            jax.ShapeDtypeStruct((1, annots), jnp.float32),
            jax.ShapeDtypeStruct((strip // 2, chi.shape[1]), jnp.float32),
        ),
        in_specs=[in_smem, in_vmem, in_place],
        out_specs=(in_vmem,) * 3,
        scratch_shapes=[pltpu.SemaphoreType.DMA],
        compiler_params=pltpu.CompilerParams(vmem_limit_bytes=VMEM_LIMIT),
        cost_estimate=pl.CostEstimate(
            flops=0, bytes_accessed=16 * strip * annots, transcendentals=0
        ),
        name="prepare",
    )(n, annotations, chi)


def own_kernel(n_ref, dosage_ref, annot_ref, sums_ref, turned_ref, geno, wide_values):
    samples, strip = dosage_ref.shape
    mine = strip // (2 * TILE)
    n = n_ref[0]
    sums_ref[...] = jnp.zeros_like(sums_ref)
    for t in range(mine):
        standardized(
            lambda rows: dosage_ref[rows, cols_at(n * mine + t)], into(geno, t), wide_values, samples
        )
        for k in range(samples // LANES):
            for part in range(2):
                turned_ref[t, k, part * LANES : (part + 1) * LANES, :] = geno[
                    2 * t + part, k * LANES : (k + 1) * LANES, :
                ].T
    for y in range(mine):
        for x in range(y + 1):
            weights = band_weights(rows_of(turned_ref, x), columns_of(geno, y))
            sums_ref[:, y * TILE : (y + 1) * TILE] += along_rows(
                annot_ref[:, cols_at(n * mine + x)], weights
            )
            if x < y:
                sums_ref[:, x * TILE : (x + 1) * TILE] += along_columns(
                    annot_ref[:, cols_at(n * mine + y)], weights
                )


def other_kernel(
    slots, n_ref, dosage_ref, annot_ref, turned_ref, sums_in, sums_ref, geno, wide_values
):
    samples, strip = dosage_ref.shape
    mine = strip // (2 * TILE)
    n = n_ref[0]

    def nearest(s):
        return (1 - n) * s + n * (mine - 1 - s)

    sums_ref[...] = sums_in[...]
    for s in slots:
        standardized(
            lambda rows: dosage_ref[rows, cols_at((1 - n) * mine + nearest(s))],
            into(geno, s),
            wide_values,
            samples,
        )
    inside = (1 - 2 * n) * tile_offset() >= 0
    for s in slots:
        for h in range(s, mine):
            weights = band_weights(
                rows_of(turned_ref, nearest(h)), columns_of(geno, s), inside if h == s else None
            )
            sums_ref[:, cols_at(nearest(h))] += along_columns(
                annot_ref[:, cols_at((1 - n) * mine + nearest(s))], weights
            )


def own_sums(n, dosage, annot):
    samples, strip, mine = sizes(dosage)
    chunks = samples // LANES
    turned = (mine, chunks, TILE, LANES)
    return pl.pallas_call(
        own_kernel,
        out_shape=(
            jax.ShapeDtypeStruct((annot.shape[0], strip // 2), jnp.float32),
            jax.ShapeDtypeStruct(turned, jnp.bfloat16),
        ),
        in_specs=[in_smem, in_vmem, in_vmem],
        out_specs=(in_vmem, in_vmem),
        scratch_shapes=strip_scratch(dosage),
        cost_estimate=strip_cost(dosage),
        compiler_params=pltpu.CompilerParams(vmem_limit_bytes=VMEM_LIMIT),
        name="own_sums",
    )(n, dosage, annot)


def other_sums(slots, n, dosage, annot, turned, sums):
    return pl.pallas_call(
        functools.partial(other_kernel, slots),
        out_shape=jax.ShapeDtypeStruct(sums.shape, jnp.float32),
        in_specs=[in_smem] + [in_vmem] * 4,
        out_specs=in_vmem,
        scratch_shapes=strip_scratch(dosage),
        cost_estimate=strip_cost(dosage),
        compiler_params=pltpu.CompilerParams(vmem_limit_bytes=VMEM_LIMIT),
        name="other_sums",
    )(n, dosage, annot, turned, sums)


def strip_scratch(dosage):
    samples, _, mine = sizes(dosage)
    return [
        pltpu.VMEM((2 * mine, samples, LANES), jnp.bfloat16),
        pltpu.VMEM((samples, TILE), jnp.float32),
    ]


def strip_cost(dosage):
    samples, strip, _ = sizes(dosage)
    return pl.CostEstimate(
        flops=samples * strip * strip // 2, bytes_accessed=2 * samples * strip, transcendentals=0
    )


def rim_kernel(
    order, n_ref, arrived_ref, turned_ref, annot_ref, sums_in, sums_ref, back_ref, geno, wide_values
):
    mine = turned_ref.shape[0]
    samples = geno.shape[1]
    n = n_ref[0]
    sums_ref[...] = sums_in[...]
    back_ref[...] = jnp.zeros_like(back_ref)
    standardized(lambda rows: arrived_ref[rows, :], into(geno, 0), wide_values, samples)

    def add(y, inside=None):
        weights = band_weights(rows_of(turned_ref, y), columns_of(geno, 0), inside)
        sums_ref[:, cols_at(y)] += along_columns(arrived_ref[samples:, :], weights)
        back_ref[...] += along_rows(annot_ref[:, cols_at(n * mine + y)], weights)

    low, high = order, mine - 1 - order
    add((1 - n) * high + n * low, (1 - 2 * n) * tile_offset() <= 0)
    for y in range(mine):
        first, second = y < high, low < y < mine // 2
        if first or second:

            @pl.when(True if first and second else (n == 0 if first else n == 1))
            def _(y=y):
                add(y)


def rim_sums(order, n, arrived, turned, annot, sums):
    mine, chunks, _, _ = turned.shape
    samples = chunks * LANES
    return pl.pallas_call(
        functools.partial(rim_kernel, order),
        out_shape=(
            jax.ShapeDtypeStruct(sums.shape, jnp.float32),
            jax.ShapeDtypeStruct((sums.shape[0], TILE), jnp.float32),
        ),
        in_specs=[in_smem] + [in_vmem] * 4,
        out_specs=(in_vmem, in_vmem),
        scratch_shapes=[
            pltpu.VMEM((2, samples, LANES), jnp.bfloat16),
            pltpu.VMEM((samples, TILE), jnp.float32),
        ],
        compiler_params=pltpu.CompilerParams(vmem_limit_bytes=VMEM_LIMIT),
        cost_estimate=pl.CostEstimate(
            flops=2 * samples * TILE * mine * TILE,
            bytes_accessed=2 * samples * TILE * (mine + 1),
            transcendentals=0,
        ),
        name="rim_sums",
    )(n, arrived, turned, annot, sums)


def eye(size):
    shape = (size, size)
    return lax.broadcasted_iota(jnp.int32, shape, 0) == lax.broadcasted_iota(jnp.int32, shape, 1)


def upright(row):
    size = row.shape[1]
    return jnp.sum(jnp.where(eye(size), jnp.broadcast_to(row, (size, size)), 0.0), axis=1, keepdims=True)


def lying(column):
    size = column.shape[0]
    return jnp.sum(
        jnp.where(eye(size), jnp.broadcast_to(column, (size, size)), 0.0), axis=0, keepdims=True
    )


def moments_kernel(total_variants, n_ref, w_ref, counts_ref, sums_ref, first_ref, second_ref, scores_ref, payload_ref, whole):
    annots = counts_ref.shape[1]
    block = sums_ref.shape[1]
    mine = block // TILE
    n = n_ref[0]
    slot = 2 * w_ref[0] + n
    whole[...] = sums_ref[...]
    for order, back_ref in enumerate((first_ref, second_ref)):
        whole[:, cols_at((1 - n) * order + n * (mine - 1 - order))] += back_ref[...]
    shares = upright(counts_ref[...]) / total_variants
    high = (1.0 - shares).astype(jnp.bfloat16).astype(jnp.float32)
    low = (0.0 - shares).astype(jnp.bfloat16).astype(jnp.float32)
    members = whole[:annots, :]
    scores = high * members + low * (whole[annots : annots + 1, :] - members)
    scores_ref[:annots, :] = scores
    row = lax.broadcasted_iota(jnp.int32, (2 * PAD, block), 0)
    scores_ref[annots:, :] = jnp.where(row == 0, 1.0, 0.0)
    mean = jnp.sum(scores, axis=1, keepdims=True) / block
    deviation = scores - mean
    payload_ref[:annots, :] = lax.dot_general(
        deviation,
        deviation,
        (((1,), (1,)), ((), ())),
        precision=highest_precision,
        preferred_element_type=jnp.float32,
    )
    slots = payload_ref.shape[0] - annots
    at = lax.broadcasted_iota(jnp.int32, (slots, annots), 0)
    payload_ref[annots:, :] = jnp.where(at == slot, lying(mean), 0.0)


def moments_of(total_variants, slots, n, w, counts, sums, back):
    annots = counts.shape[1]
    block = sums.shape[1]
    return pl.pallas_call(
        functools.partial(moments_kernel, total_variants),
        out_shape=(
            jax.ShapeDtypeStruct((annots + 2 * PAD, block), jnp.float32),
            jax.ShapeDtypeStruct((annots + slots, annots), jnp.float32),
        ),
        in_specs=[in_smem] * 2 + [in_vmem] * 4,
        out_specs=(in_vmem, in_vmem),
        scratch_shapes=[pltpu.VMEM(sums.shape, jnp.float32)],
        compiler_params=pltpu.CompilerParams(vmem_limit_bytes=VMEM_LIMIT),
        cost_estimate=pl.CostEstimate(
            flops=12 * annots * annots * block, bytes_accessed=12 * annots * block, transcendentals=0
        ),
        name="moments",
    )(n, w, counts, sums, *back)


def inverse_kernel(divisor, payload_ref, inverse_ref, moments_ref):
    size = payload_ref.shape[1]
    slots = payload_ref.shape[0] - size
    means = payload_ref[size:, :]
    mean = jnp.sum(means, axis=0, keepdims=True) / slots
    between = means - mean
    covariance = (
        payload_ref[:size, :]
        + lax.dot_general(
            between,
            between,
            (((0,), (0,)), ((), ())),
            precision=highest_precision,
            preferred_element_type=jnp.float32,
        )
        * (divisor // slots)
    ) / divisor
    row = lax.broadcasted_iota(jnp.int32, (size, size), 0)
    lane = lax.broadcasted_iota(jnp.int32, (size, size), 1)
    diagonal = jnp.where(row == lane, covariance, 0.0)
    across = 1.0 / jnp.sqrt(jnp.sum(diagonal, axis=0, keepdims=True) + EPS)
    down = 1.0 / jnp.sqrt(jnp.sum(diagonal, axis=1, keepdims=True) + EPS)
    mean_down = jnp.sum(jnp.where(row == lane, jnp.broadcast_to(mean, (size, size)), 0.0), axis=1, keepdims=True)
    moments_ref[...] = jnp.where(lane == 0, mean_down, down)
    gram = covariance * down * across
    groups = [gram[PAD * g : PAD * (g + 1), :] for g in range(size // PAD)]
    lane_of = lax.broadcasted_iota(jnp.int32, (1, size), 1)
    row_of = lax.broadcasted_iota(jnp.int32, (PAD, size), 0)

    def pair_inverse(a, b, c):
        scale = 1.0 / (a * c - b * b)
        return c * scale, -b * scale, a * scale

    for k in range(0, size, PIVOTS):
        g, i = divmod(k, PAD)
        spread = [
            [jnp.broadcast_to(old[:, k + j : k + j + 1], (PAD, size)) for j in range(PIVOTS)]
            for old in groups
        ]
        m = [[spread[g][c][i + r : i + r + 1, :] for c in range(PIVOTS)] for r in range(PIVOTS)]
        rows = [
            groups[g][i + j : i + j + 1, :] - jnp.where(lane_of == k + j, 1.0, 0.0)
            for j in range(PIVOTS)
        ]
        a, b, c = pair_inverse(m[0][0], m[0][1], m[1][1])
        u = a * rows[0] + b * rows[1], b * rows[0] + c * rows[1]
        v = [(a * m[0][j] + b * m[1][j], b * m[0][j] + c * m[1][j]) for j in (2, 3)]
        rest = [rows[j] - m[0][j] * u[0] - m[1][j] * u[1] for j in (2, 3)]
        d, e, f = pair_inverse(
            m[2][2] - m[0][2] * v[0][0] - m[1][2] * v[0][1],
            m[2][3] - m[0][2] * v[1][0] - m[1][2] * v[1][1],
            m[3][3] - m[0][3] * v[1][0] - m[1][3] * v[1][1],
        )
        third = d * rest[0] + e * rest[1]
        fourth = e * rest[0] + f * rest[1]
        solved = [
            u[0] - v[0][0] * third - v[1][0] * fourth,
            u[1] - v[0][1] * third - v[1][1] * fourth,
            third,
            fourth,
        ]
        solved = [jnp.broadcast_to(value, (PAD, size)) for value in solved]
        for h, old in enumerate(groups):
            for j in range(PIVOTS):
                old = old - spread[h][j] * solved[j]
                if h == g:
                    old = old + jnp.where(row_of == i + j, solved[j], 0.0)
            groups[h] = old
    swept = jnp.concatenate(groups, axis=0)
    inverse = jnp.where(row == lane, 2.0, 0.0) - swept
    inverse_ref[...] = inverse * down * across / divisor


def gram_inverse(divisor, payload):
    size = payload.shape[1]
    square = jax.ShapeDtypeStruct((size, size), jnp.float32)
    return pl.pallas_call(
        functools.partial(inverse_kernel, divisor),
        out_shape=(square, square),
        in_specs=[in_vmem],
        out_specs=(in_vmem, in_vmem),
        compiler_params=pltpu.CompilerParams(vmem_limit_bytes=VMEM_LIMIT),
        cost_estimate=pl.CostEstimate(flops=20_000_000_000, bytes_accessed=4 * size * size, transcendentals=0),
        name="gram_inverse",
    )(payload)


def halves(value):
    upper = value.astype(jnp.bfloat16)
    return upper, (value - upper.astype(jnp.float32)).astype(jnp.bfloat16)


def fit_kernel(divisor, n_ref, inverse_ref, moments_ref, proj_ref, scores_ref, other_ref, own_ref, fitted_ref):
    annots = own_ref.shape[0]
    block = scores_ref.shape[1]
    n = n_ref[0]
    mean = moments_ref[:, 0:1]
    sums = proj_ref[annots : annots + 1, :]
    coefficient = jnp.dot(
        inverse_ref[...],
        proj_ref[:annots, :] - mean * sums,
        precision=highest_precision,
        preferred_element_type=jnp.float32,
    )
    upper, lower = halves(coefficient)
    right = jnp.concatenate([upper, upper, lower], axis=0)

    def fit(values, place):
        upper, lower = halves(values)
        fitted = lax.dot_general(
            jnp.concatenate([upper, lower, upper], axis=0),
            right,
            (((0,), (0,)), ((), ())),
            preferred_element_type=jnp.float32,
        )
        rows = pl.ds(pl.multiple_of(place * block, block), block)
        fitted_ref[rows, :] = sums / divisor + fitted

    centred = scores_ref[:annots, :] - mean
    own_ref[...] = centred * moments_ref[:, 1:2]
    fit(centred, n)
    fit(other_ref[...] - mean, 1 - n)


def fitted_values(divisor, n, inverse, moments, projection, scores, scores_other):
    annots, block = scores_other.shape
    traits = projection.shape[1]
    return pl.pallas_call(
        functools.partial(fit_kernel, divisor),
        out_shape=(
            jax.ShapeDtypeStruct((annots, block), jnp.float32),
            jax.ShapeDtypeStruct((2 * block, traits), jnp.float32),
        ),
        in_specs=[in_smem] + [in_vmem] * 5,
        out_specs=(in_vmem, in_vmem),
        compiler_params=pltpu.CompilerParams(vmem_limit_bytes=VMEM_LIMIT),
        cost_estimate=pl.CostEstimate(
            flops=4 * annots * block * traits, bytes_accessed=8 * block * traits, transcendentals=0
        ),
        name="fitted_values",
    )(n, inverse, moments, projection, scores, scores_other)


def flipped(value, axis, bit):
    length = lax.axis_size(axis)
    return lax.ppermute(value, axis, [(i, i ^ bit) for i in range(length)])


def wide_bits():
    length = lax.axis_size("wide")
    bits = []
    bit = 1
    while bit < length:
        bits.append(bit)
        bit *= 2
    return bits


def added_kernel(first_ref, second_ref, out_ref):
    out_ref[...] = first_ref[...] + second_ref[...]


def added(first, second):
    return pl.pallas_call(
        added_kernel,
        out_shape=jax.ShapeDtypeStruct(first.shape, first.dtype),
        in_specs=[in_vmem, in_vmem],
        out_specs=in_vmem,
        compiler_params=pltpu.CompilerParams(vmem_limit_bytes=VMEM_LIMIT // 4),
        name="added",
    )(first, second)


def wide_sum(value):
    bits = wide_bits()
    for bit in bits[:1] + bits[2:] + bits[1:2]:
        value = added(value, flipped(value, "wide", bit))
    return value


def split(value):
    half = value.shape[0] // 2
    low = lax.axis_index("wide") % 2
    kept = lax.dynamic_slice_in_dim(value, low * half, half, 0)
    given = lax.dynamic_slice_in_dim(value, (1 - low) * half, half, 0)
    return kept + flipped(given, "wide", 1)


def long_sum(value):
    for bit in wide_bits()[1:]:
        value = value + flipped(value, "wide", bit)
    return value


def joined(kept):
    low = lax.axis_index("wide") % 2
    other = flipped(kept, "wide", 1)
    return jnp.where(
        low == 0, jnp.concatenate([kept, other], 0), jnp.concatenate([other, kept], 0)
    )


def whole_step(dosage, annotations, test_statistic_table):
    _, strip = dosage.shape
    annots = annotations.shape[0]
    wide = lax.axis_size("wide")
    total_variants = wide * strip
    w = lax.axis_index("wide")
    n = lax.axis_index("narrow")
    block = strip // 2
    n_array = jnp.reshape(n, (1,)).astype(jnp.int32)

    rim_pairs = []
    back_pairs = []
    for i in range(wide - 1):
        rim_pairs += [(2 * i, 2 * i + 2), (2 * i + 3, 2 * i + 1)]
        back_pairs += [(2 * i + 1, 2 * i + 2), (2 * i + 2, 2 * i + 1)]
    chi = test_statistic_table
    arrived = []
    for outgoing in outgoing_columns(n_array, dosage, annotations):
        arrived.append(lax.ppermute(outgoing, both, rim_pairs))
    annot, counts, chi_given = prepared(n_array, annotations, chi)
    chi_other = flipped(chi_given, "narrow", 1)
    counts = wide_sum(counts)
    sums, turned = own_sums(n_array, dosage, annot)
    tiles = block // TILE
    pieces = tuple(range(tiles // 2)), tuple(range(tiles // 2, tiles))
    back = []
    for order in range(2):
        sums, part = rim_sums(order, n_array, arrived[order], turned, annot, sums)
        back.append(lax.ppermute(part, both, back_pairs))
        sums = other_sums(pieces[order], n_array, dosage, annot, turned, sums)

    w_array = jnp.reshape(w, (1,)).astype(jnp.int32)
    extended, payload = moments_of(
        total_variants, 2 * wide, n_array, w_array, counts, sums, back
    )
    scores = extended[:annots]
    payload = split(payload)
    payload = payload + flipped(payload, "narrow", 1)
    payload = joined(long_sum(payload))

    chi_own = lax.dynamic_slice_in_dim(chi, n * block, block, 0)
    halves_of = [
        jnp.dot(
            extended, values, precision=lax.Precision.HIGH, preferred_element_type=jnp.float32
        )
        for values in (chi_other, chi_own)
    ]
    projection = split(jnp.concatenate(halves_of, axis=1))
    traits = chi.shape[1]
    projection = projection[:, traits:] + flipped(projection[:, :traits], "narrow", 1)
    projection = joined(long_sum(projection))
    scores_other = flipped(scores, "narrow", 1)

    inverse, moments = gram_inverse(total_variants, payload)
    return fitted_values(
        total_variants, n_array, inverse, moments, projection, extended, scores_other
    )


def solution(mesh):
    in_specs = (P(None, "wide"), P(None, "wide"), P("wide", "narrow"))
    out_specs = (P(None, both), P("wide", "narrow"))
    return jax.shard_map(whole_step, mesh=mesh, in_specs=in_specs, out_specs=out_specs, check_vma=False)
```

```python
import functools

import jax
import jax.numpy as jnp
from jax import lax
from jax.experimental import pallas as pl
from jax.experimental.pallas import tpu as pltpu
from jax.sharding import PartitionSpec as P


EPS = 1e-05
TILE = 256
LANES = 128
ROWS = 64
PAD = 8
PIVOTS = 4
VMEM_LIMIT = 16 * 1024 * 1024

highest_precision = lax.Precision.HIGHEST
both = ("wide", "narrow")
in_vmem = pl.BlockSpec(memory_space=pltpu.VMEM)
in_place = pl.BlockSpec(memory_space=pl.ANY)
in_smem = pl.BlockSpec(memory_space=pltpu.SMEM)


def cols_at(c):
    return pl.ds(pl.multiple_of(c * TILE, TILE), TILE)


def standardized(read, write, wide_values, samples):
    steps = samples // ROWS
    pivot = read(pl.ds(0, 2 * PAD)).astype(jnp.float32)[:1, :]

    def folded(values):
        return jnp.sum(values.reshape(-1, 4 * PAD, TILE), axis=0)

    first = second = jnp.zeros((4 * PAD, TILE), jnp.float32)
    for r in range(steps):
        rows = pl.ds(r * ROWS, ROWS)
        values = read(rows).astype(jnp.float32) - pivot
        wide_values[rows, :] = values
        first, second = first + folded(values), second + folded(values * values)
    first, second = (
        jnp.sum(value, axis=0, keepdims=True) / samples for value in (first, second)
    )
    variance = jnp.maximum(second - first * first, 0.0)
    scale = 1.0 / jnp.sqrt(variance + EPS)
    for r in range(steps):
        rows = pl.ds(r * ROWS, ROWS)
        write(rows, ((wide_values[rows, :] - first) * scale).astype(jnp.bfloat16))


def into(geno, tile):
    def write(rows, value):
        geno[2 * tile, rows, :] = value[:, :LANES]
        geno[2 * tile + 1, rows, :] = value[:, LANES:]

    return write


def columns_of(geno, tile):
    return jnp.concatenate([geno[2 * tile], geno[2 * tile + 1]], axis=1)


def rows_of(turned, tile):
    return jnp.concatenate([turned[tile, k] for k in range(turned.shape[1])], axis=1)


def band_weights(rows, columns, inside=None):
    samples = rows.shape[1]
    products = jnp.dot(rows, columns, preferred_element_type=jnp.float32)
    unit = 1.0 / (samples - 2)
    weights = products * products * ((1.0 + unit) / (samples * samples)) - unit
    if inside is not None:
        weights = jnp.where(inside, weights, 0.0)
    return weights.astype(jnp.bfloat16)


def along_rows(annot, weights):
    return jnp.dot(annot, weights, preferred_element_type=jnp.float32)


def along_columns(annot, weights):
    return lax.dot_general(
        annot, weights, (((1,), (1,)), ((), ())), preferred_element_type=jnp.float32
    )


def tile_offset():
    shape = (TILE, TILE)
    return lax.broadcasted_iota(jnp.int32, shape, 0) - lax.broadcasted_iota(jnp.int32, shape, 1)


def sizes(dosage):
    samples, strip = dosage.shape
    return samples, strip, strip // (2 * TILE)


def outgoing_kernel(n_ref, dosage_ref, annot_ref, first_ref, second_ref, given_annot, came):
    samples, strip = dosage_ref.shape
    annots = annot_ref.shape[0]
    n = n_ref[0]
    outs = (first_ref, second_ref)
    copies = []
    for order, out_ref in enumerate(outs):
        column = cols_at((1 - n) * (strip // TILE - 1 - order) + n * order)
        copies += [
            pltpu.make_async_copy(
                dosage_ref.at[:, column], out_ref.at[:samples, :], came.at[2 * order]
            ),
            pltpu.make_async_copy(
                annot_ref.at[:, column], given_annot.at[order], came.at[2 * order + 1]
            ),
        ]
    for copy in copies:
        copy.start()
    row = lax.broadcasted_iota(jnp.int32, (PAD, TILE), 0)
    for order, out_ref in enumerate(outs):
        out_ref[samples + annots :, :] = jnp.where(row == 0, 1.0, 0.0).astype(jnp.bfloat16)
        copies[2 * order + 1].wait()
        out_ref[samples : samples + annots, :] = (
            given_annot[order].astype(jnp.float32).astype(jnp.bfloat16)
        )
    for order in range(2):
        copies[2 * order].wait()


def outgoing_columns(n, dosage, annotations):
    samples = dosage.shape[0]
    annots = annotations.shape[0]
    out = jax.ShapeDtypeStruct((samples + annots + PAD, TILE), jnp.bfloat16)
    return pl.pallas_call(
        outgoing_kernel,
        out_shape=(out, out),
        in_specs=[in_smem, in_place, in_place],
        out_specs=(in_vmem, in_vmem),
        scratch_shapes=[pltpu.VMEM((2, annots, TILE), jnp.int32), pltpu.SemaphoreType.DMA((4,))],
        cost_estimate=pl.CostEstimate(
            flops=0, bytes_accessed=8 * samples * TILE, transcendentals=0
        ),
        name="outgoing",
    )(n, dosage, annotations)


def prepare_kernel(n_ref, annot_ref, chi_ref, annot_out_ref, counts_ref, chi_out_ref, came):
    annots, strip = annot_ref.shape
    block = strip // 2
    n = n_ref[0]
    rows = pl.ds(pl.multiple_of((1 - n) * block, block), block)
    copy = pltpu.make_async_copy(chi_ref.at[rows, :], chi_out_ref, came)
    copy.start()
    row = lax.broadcasted_iota(jnp.int32, (PAD, strip), 0)
    annot_out_ref[annots:, :] = jnp.where(row == 0, 1.0, 0.0).astype(jnp.bfloat16)
    members = annot_ref[...].astype(jnp.float32)
    annot_out_ref[:annots, :] = members.astype(jnp.bfloat16)
    counts_ref[...] = lying(jnp.sum(members, axis=1, keepdims=True))
    copy.wait()


def prepared(n, annotations, chi):
    annots, strip = annotations.shape
    return pl.pallas_call(
        prepare_kernel,
        out_shape=(
            jax.ShapeDtypeStruct((annots + PAD, strip), jnp.bfloat16),
            jax.ShapeDtypeStruct((1, annots), jnp.float32),
            jax.ShapeDtypeStruct((strip // 2, chi.shape[1]), jnp.float32),
        ),
        in_specs=[in_smem, in_vmem, in_place],
        out_specs=(in_vmem,) * 3,
        scratch_shapes=[pltpu.SemaphoreType.DMA],
        compiler_params=pltpu.CompilerParams(vmem_limit_bytes=VMEM_LIMIT),
        cost_estimate=pl.CostEstimate(
            flops=0, bytes_accessed=16 * strip * annots, transcendentals=0
        ),
        name="prepare",
    )(n, annotations, chi)


def own_kernel(n_ref, dosage_ref, annot_ref, sums_ref, turned_ref, geno, wide_values):
    samples, strip = dosage_ref.shape
    mine = strip // (2 * TILE)
    n = n_ref[0]
    sums_ref[...] = jnp.zeros_like(sums_ref)

    def standardize(t):
        standardized(
            lambda rows: dosage_ref[rows, cols_at(n * mine + t)],
            into(geno, t),
            wide_values.at[t % 2],
            samples,
        )
        for k in range(samples // LANES):
            for part in range(2):
                turned_ref[t, k, part * LANES : (part + 1) * LANES, :] = geno[
                    2 * t + part, k * LANES : (k + 1) * LANES, :
                ].T

    standardize(0)
    for y in range(mine):
        if y + 1 < mine:
            standardize(y + 1)
        for x in range(y + 1):
            weights = band_weights(rows_of(turned_ref, x), columns_of(geno, y))
            sums_ref[:, y * TILE : (y + 1) * TILE] += along_rows(
                annot_ref[:, cols_at(n * mine + x)], weights
            )
            if x < y:
                sums_ref[:, x * TILE : (x + 1) * TILE] += along_columns(
                    annot_ref[:, cols_at(n * mine + y)], weights
                )


def other_kernel(
    slots, n_ref, dosage_ref, annot_ref, turned_ref, sums_in, sums_ref, geno, wide_values
):
    samples, strip = dosage_ref.shape
    mine = strip // (2 * TILE)
    n = n_ref[0]

    def nearest(s):
        return (1 - n) * s + n * (mine - 1 - s)

    sums_ref[...] = sums_in[...]
    inside = (1 - 2 * n) * tile_offset() >= 0

    def standardize(s):
        standardized(
            lambda rows: dosage_ref[rows, cols_at((1 - n) * mine + nearest(s))],
            into(geno, s),
            wide_values.at[s % 2],
            samples,
        )

    standardize(slots[0])
    for s in slots:
        if s + 1 in slots:
            standardize(s + 1)
        for h in range(s, mine):
            weights = band_weights(
                rows_of(turned_ref, nearest(h)), columns_of(geno, s), inside if h == s else None
            )
            sums_ref[:, cols_at(nearest(h))] += along_columns(
                annot_ref[:, cols_at((1 - n) * mine + nearest(s))], weights
            )


def own_sums(n, dosage, annot):
    samples, strip, mine = sizes(dosage)
    chunks = samples // LANES
    turned = (mine, chunks, TILE, LANES)
    return pl.pallas_call(
        own_kernel,
        out_shape=(
            jax.ShapeDtypeStruct((annot.shape[0], strip // 2), jnp.float32),
            jax.ShapeDtypeStruct(turned, jnp.bfloat16),
        ),
        in_specs=[in_smem, in_vmem, in_vmem],
        out_specs=(in_vmem, in_vmem),
        scratch_shapes=strip_scratch(dosage),
        cost_estimate=strip_cost(dosage),
        compiler_params=pltpu.CompilerParams(vmem_limit_bytes=VMEM_LIMIT),
        name="own_sums",
    )(n, dosage, annot)


def other_sums(slots, n, dosage, annot, turned, sums):
    return pl.pallas_call(
        functools.partial(other_kernel, slots),
        out_shape=jax.ShapeDtypeStruct(sums.shape, jnp.float32),
        in_specs=[in_smem] + [in_vmem] * 4,
        out_specs=in_vmem,
        scratch_shapes=strip_scratch(dosage),
        cost_estimate=strip_cost(dosage),
        compiler_params=pltpu.CompilerParams(vmem_limit_bytes=VMEM_LIMIT),
        name="other_sums",
    )(n, dosage, annot, turned, sums)


def strip_scratch(dosage):
    samples, _, mine = sizes(dosage)
    return [
        pltpu.VMEM((2 * mine, samples, LANES), jnp.bfloat16),
        pltpu.VMEM((2, samples, TILE), jnp.float32),
    ]


def strip_cost(dosage):
    samples, strip, _ = sizes(dosage)
    return pl.CostEstimate(
        flops=samples * strip * strip // 2, bytes_accessed=2 * samples * strip, transcendentals=0
    )


def rim_kernel(
    order, n_ref, arrived_ref, turned_ref, annot_ref, sums_in, sums_ref, back_ref, geno, wide_values
):
    mine = turned_ref.shape[0]
    samples = geno.shape[1]
    n = n_ref[0]
    sums_ref[...] = sums_in[...]
    back_ref[...] = jnp.zeros_like(back_ref)
    standardized(lambda rows: arrived_ref[rows, :], into(geno, 0), wide_values, samples)

    def add(y, inside=None):
        weights = band_weights(rows_of(turned_ref, y), columns_of(geno, 0), inside)
        sums_ref[:, cols_at(y)] += along_columns(arrived_ref[samples:, :], weights)
        back_ref[...] += along_rows(annot_ref[:, cols_at(n * mine + y)], weights)

    low, high = order, mine - 1 - order
    add((1 - n) * high + n * low, (1 - 2 * n) * tile_offset() <= 0)
    width, last = mine // 2, mine - mine // 4
    for y in range(mine):
        first = y < high and (y >= width or high >= last)
        second = low < y < last
        if first or second:

            @pl.when(True if first and second else (n == 0 if first else n == 1))
            def _(y=y):
                add(y)


def rim_sums(order, n, arrived, turned, annot, sums):
    mine, chunks, _, _ = turned.shape
    samples = chunks * LANES
    return pl.pallas_call(
        functools.partial(rim_kernel, order),
        out_shape=(
            jax.ShapeDtypeStruct(sums.shape, jnp.float32),
            jax.ShapeDtypeStruct((sums.shape[0], TILE), jnp.float32),
        ),
        in_specs=[in_smem] + [in_vmem] * 4,
        out_specs=(in_vmem, in_vmem),
        scratch_shapes=[
            pltpu.VMEM((2, samples, LANES), jnp.bfloat16),
            pltpu.VMEM((samples, TILE), jnp.float32),
        ],
        compiler_params=pltpu.CompilerParams(vmem_limit_bytes=VMEM_LIMIT),
        cost_estimate=pl.CostEstimate(
            flops=2 * samples * TILE * mine * TILE,
            bytes_accessed=2 * samples * TILE * (mine + 1),
            transcendentals=0,
        ),
        name="rim_sums",
    )(n, arrived, turned, annot, sums)


def eye(size):
    shape = (size, size)
    return lax.broadcasted_iota(jnp.int32, shape, 0) == lax.broadcasted_iota(jnp.int32, shape, 1)


def upright(row):
    size = row.shape[1]
    return jnp.sum(jnp.where(eye(size), jnp.broadcast_to(row, (size, size)), 0.0), axis=1, keepdims=True)


def lying(column):
    size = column.shape[0]
    return jnp.sum(
        jnp.where(eye(size), jnp.broadcast_to(column, (size, size)), 0.0), axis=0, keepdims=True
    )


def moments_kernel(total_variants, n_ref, w_ref, counts_ref, sums_ref, first_ref, second_ref, scores_ref, payload_ref, whole):
    annots = counts_ref.shape[1]
    block = sums_ref.shape[1]
    mine = block // TILE
    n = n_ref[0]
    slot = 2 * w_ref[0] + n
    whole[...] = sums_ref[...]
    for order, back_ref in enumerate((first_ref, second_ref)):
        whole[:, cols_at((1 - n) * order + n * (mine - 1 - order))] += back_ref[...]
    shares = upright(counts_ref[...]) / total_variants
    high = (1.0 - shares).astype(jnp.bfloat16).astype(jnp.float32)
    low = (0.0 - shares).astype(jnp.bfloat16).astype(jnp.float32)
    members = whole[:annots, :]
    scores = high * members + low * (whole[annots : annots + 1, :] - members)
    scores_ref[:annots, :] = scores
    row = lax.broadcasted_iota(jnp.int32, (2 * PAD, block), 0)
    scores_ref[annots:, :] = jnp.where(row == 0, 1.0, 0.0)
    mean = jnp.sum(scores, axis=1, keepdims=True) / block
    deviation = scores - mean
    payload_ref[:annots, :] = lax.dot_general(
        deviation,
        deviation,
        (((1,), (1,)), ((), ())),
        precision=highest_precision,
        preferred_element_type=jnp.float32,
    )
    slots = payload_ref.shape[0] - annots
    at = lax.broadcasted_iota(jnp.int32, (slots, annots), 0)
    payload_ref[annots:, :] = jnp.where(at == slot, lying(mean), 0.0)


def moments_of(total_variants, slots, n, w, counts, sums, back):
    annots = counts.shape[1]
    block = sums.shape[1]
    return pl.pallas_call(
        functools.partial(moments_kernel, total_variants),
        out_shape=(
            jax.ShapeDtypeStruct((annots + 2 * PAD, block), jnp.float32),
            jax.ShapeDtypeStruct((annots + slots, annots), jnp.float32),
        ),
        in_specs=[in_smem] * 2 + [in_vmem] * 4,
        out_specs=(in_vmem, in_vmem),
        scratch_shapes=[pltpu.VMEM(sums.shape, jnp.float32)],
        compiler_params=pltpu.CompilerParams(vmem_limit_bytes=VMEM_LIMIT),
        cost_estimate=pl.CostEstimate(
            flops=12 * annots * annots * block, bytes_accessed=12 * annots * block, transcendentals=0
        ),
        name="moments",
    )(n, w, counts, sums, *back)


def inverse_kernel(divisor, payload_ref, inverse_ref, moments_ref):
    size = payload_ref.shape[1]
    slots = payload_ref.shape[0] - size
    means = payload_ref[size:, :]
    mean = jnp.sum(means, axis=0, keepdims=True) / slots
    between = means - mean
    covariance = (
        payload_ref[:size, :]
        + lax.dot_general(
            between,
            between,
            (((0,), (0,)), ((), ())),
            precision=highest_precision,
            preferred_element_type=jnp.float32,
        )
        * (divisor // slots)
    ) / divisor
    row = lax.broadcasted_iota(jnp.int32, (size, size), 0)
    lane = lax.broadcasted_iota(jnp.int32, (size, size), 1)
    diagonal = jnp.where(row == lane, covariance, 0.0)
    across = 1.0 / jnp.sqrt(jnp.sum(diagonal, axis=0, keepdims=True) + EPS)
    down = 1.0 / jnp.sqrt(jnp.sum(diagonal, axis=1, keepdims=True) + EPS)
    mean_down = jnp.sum(jnp.where(row == lane, jnp.broadcast_to(mean, (size, size)), 0.0), axis=1, keepdims=True)
    moments_ref[...] = jnp.where(lane == 0, mean_down, down)
    gram = covariance * down * across
    groups = [gram[PAD * g : PAD * (g + 1), :] for g in range(size // PAD)]
    lane_of = lax.broadcasted_iota(jnp.int32, (1, size), 1)
    row_of = lax.broadcasted_iota(jnp.int32, (PAD, size), 0)

    def pair_inverse(a, b, c):
        scale = 1.0 / (a * c - b * b)
        return c * scale, -b * scale, a * scale

    for k in range(0, size, PIVOTS):
        g, i = divmod(k, PAD)
        spread = [
            [jnp.broadcast_to(old[:, k + j : k + j + 1], (PAD, size)) for j in range(PIVOTS)]
            for old in groups
        ]
        m = [[spread[g][c][i + r : i + r + 1, :] for c in range(PIVOTS)] for r in range(PIVOTS)]
        rows = [
            groups[g][i + j : i + j + 1, :] - jnp.where(lane_of == k + j, 1.0, 0.0)
            for j in range(PIVOTS)
        ]
        a, b, c = pair_inverse(m[0][0], m[0][1], m[1][1])
        u = a * rows[0] + b * rows[1], b * rows[0] + c * rows[1]
        v = [(a * m[0][j] + b * m[1][j], b * m[0][j] + c * m[1][j]) for j in (2, 3)]
        rest = [rows[j] - m[0][j] * u[0] - m[1][j] * u[1] for j in (2, 3)]
        d, e, f = pair_inverse(
            m[2][2] - m[0][2] * v[0][0] - m[1][2] * v[0][1],
            m[2][3] - m[0][2] * v[1][0] - m[1][2] * v[1][1],
            m[3][3] - m[0][3] * v[1][0] - m[1][3] * v[1][1],
        )
        third = d * rest[0] + e * rest[1]
        fourth = e * rest[0] + f * rest[1]
        solved = [
            u[0] - v[0][0] * third - v[1][0] * fourth,
            u[1] - v[0][1] * third - v[1][1] * fourth,
            third,
            fourth,
        ]
        solved = [jnp.broadcast_to(value, (PAD, size)) for value in solved]
        for h, old in enumerate(groups):
            for j in range(PIVOTS):
                old = old - spread[h][j] * solved[j]
                if h == g:
                    old = old + jnp.where(row_of == i + j, solved[j], 0.0)
            groups[h] = old
    swept = jnp.concatenate(groups, axis=0)
    inverse = jnp.where(row == lane, 2.0, 0.0) - swept
    inverse_ref[...] = inverse * down * across / divisor


def gram_inverse(divisor, payload):
    size = payload.shape[1]
    square = jax.ShapeDtypeStruct((size, size), jnp.float32)
    return pl.pallas_call(
        functools.partial(inverse_kernel, divisor),
        out_shape=(square, square),
        in_specs=[in_vmem],
        out_specs=(in_vmem, in_vmem),
        compiler_params=pltpu.CompilerParams(vmem_limit_bytes=VMEM_LIMIT),
        cost_estimate=pl.CostEstimate(flops=20_000_000_000, bytes_accessed=4 * size * size, transcendentals=0),
        name="gram_inverse",
    )(payload)


def halves(value):
    upper = value.astype(jnp.bfloat16)
    return upper, (value - upper.astype(jnp.float32)).astype(jnp.bfloat16)


def fit_kernel(
    divisor, n_ref, inverse_ref, moments_ref, proj_ref, scores_ref, other_ref, own_ref, fitted_ref,
    own, fitted, went,
):
    annots, block = own.shape
    n = n_ref[0]
    mean = moments_ref[:, 0:1]
    centred = scores_ref[:annots, :] - mean
    own[...] = centred * moments_ref[:, 1:2]
    copies = [pltpu.make_async_copy(own, own_ref, went.at[0])]
    copies[0].start()
    sums = proj_ref[annots : annots + 1, :]
    coefficient = jnp.dot(
        inverse_ref[...],
        proj_ref[:annots, :] - mean * sums,
        precision=highest_precision,
        preferred_element_type=jnp.float32,
    )
    upper, lower = halves(coefficient)
    right = jnp.concatenate([upper, upper, lower], axis=0)
    for half, values in enumerate((centred, other_ref[...] - mean)):
        upper, lower = halves(values)
        left = jnp.concatenate([upper, lower, upper], axis=0)
        place = (1 - half) * n + half * (1 - n)
        for c in range(block // TILE):
            rows = pl.ds(half * block + c * TILE, TILE)
            fitted[rows, :] = sums / divisor + lax.dot_general(
                left[:, c * TILE : (c + 1) * TILE],
                right,
                (((0,), (0,)), ((), ())),
                preferred_element_type=jnp.float32,
            )
            target = pl.ds(pl.multiple_of(place * block + c * TILE, TILE), TILE)
            copies.append(
                pltpu.make_async_copy(
                    fitted.at[rows, :], fitted_ref.at[target, :], went.at[len(copies)]
                )
            )
            copies[-1].start()
    for copy in copies:
        copy.wait()


def fitted_values(divisor, n, inverse, moments, projection, scores, scores_other):
    annots, block = scores_other.shape
    traits = projection.shape[1]
    return pl.pallas_call(
        functools.partial(fit_kernel, divisor),
        out_shape=(
            jax.ShapeDtypeStruct((annots, block), jnp.float32),
            jax.ShapeDtypeStruct((2 * block, traits), jnp.float32),
        ),
        in_specs=[in_smem] + [in_vmem] * 5,
        out_specs=(in_place, in_place),
        scratch_shapes=[
            pltpu.VMEM((annots, block), jnp.float32),
            pltpu.VMEM((2 * block, traits), jnp.float32),
            pltpu.SemaphoreType.DMA((1 + 2 * (block // TILE),)),
        ],
        compiler_params=pltpu.CompilerParams(vmem_limit_bytes=VMEM_LIMIT),
        cost_estimate=pl.CostEstimate(
            flops=4 * annots * block * traits, bytes_accessed=8 * block * traits, transcendentals=0
        ),
        name="fitted_values",
    )(n, inverse, moments, projection, scores, scores_other)


def flipped(value, axis, bit):
    length = lax.axis_size(axis)
    return lax.ppermute(value, axis, [(i, i ^ bit) for i in range(length)])


def wide_bits():
    length = lax.axis_size("wide")
    bits = []
    bit = 1
    while bit < length:
        bits.append(bit)
        bit *= 2
    return bits


def added_kernel(first_ref, second_ref, out_ref):
    out_ref[...] = first_ref[...] + second_ref[...]


def added(first, second):
    return pl.pallas_call(
        added_kernel,
        out_shape=jax.ShapeDtypeStruct(first.shape, first.dtype),
        in_specs=[in_vmem, in_vmem],
        out_specs=in_vmem,
        compiler_params=pltpu.CompilerParams(vmem_limit_bytes=VMEM_LIMIT // 4),
        name="added",
    )(first, second)


def wide_sum(value):
    bits = wide_bits()
    for bit in bits[:1] + bits[2:] + bits[1:2]:
        value = added(value, flipped(value, "wide", bit))
    return value


def split(value):
    half = value.shape[0] // 2
    low = lax.axis_index("wide") % 2
    kept = lax.dynamic_slice_in_dim(value, low * half, half, 0)
    given = lax.dynamic_slice_in_dim(value, (1 - low) * half, half, 0)
    return kept + flipped(given, "wide", 1)


def long_sum(value):
    for bit in wide_bits()[1:]:
        value = value + flipped(value, "wide", bit)
    return value


def joined(kept):
    low = lax.axis_index("wide") % 2
    other = flipped(kept, "wide", 1)
    return jnp.where(low == 0, jnp.concatenate([kept, other], 0), jnp.concatenate([other, kept], 0))


def whole_step(dosage, annotations, test_statistic_table):
    _, strip = dosage.shape
    annots = annotations.shape[0]
    wide = lax.axis_size("wide")
    total_variants = wide * strip
    w = lax.axis_index("wide")
    n = lax.axis_index("narrow")
    block = strip // 2
    n_array = jnp.reshape(n, (1,)).astype(jnp.int32)

    rim_pairs = []
    back_pairs = []
    for i in range(wide - 1):
        rim_pairs += [(2 * i, 2 * i + 2), (2 * i + 3, 2 * i + 1)]
        back_pairs += [(2 * i + 1, 2 * i + 2), (2 * i + 2, 2 * i + 1)]
    chi = test_statistic_table
    arrived = []
    for outgoing in outgoing_columns(n_array, dosage, annotations):
        arrived.append(lax.ppermute(outgoing, both, rim_pairs))
    annot, counts, chi_given = prepared(n_array, annotations, chi)
    chi_other = flipped(chi_given, "narrow", 1)
    counts = wide_sum(counts)
    sums, turned = own_sums(n_array, dosage, annot)
    tiles = block // TILE
    pieces = tuple(range(tiles // 2)), tuple(range(tiles // 2, tiles))
    back = []
    for order in range(2):
        sums, part = rim_sums(order, n_array, arrived[order], turned, annot, sums)
        back.append(lax.ppermute(part, both, back_pairs))
        sums = other_sums(pieces[order], n_array, dosage, annot, turned, sums)

    w_array = jnp.reshape(w, (1,)).astype(jnp.int32)
    extended, payload = moments_of(total_variants, 2 * wide, n_array, w_array, counts, sums, back)
    scores = extended[:annots]
    payload = split(payload)
    payload = payload + flipped(payload, "narrow", 1)
    payload = joined(long_sum(payload))

    chi_own = lax.dynamic_slice_in_dim(chi, n * block, block, 0)
    halves_of = [
        jnp.dot(extended, values, precision=lax.Precision.HIGH, preferred_element_type=jnp.float32)
        for values in (chi_other, chi_own)
    ]
    projection = split(jnp.concatenate(halves_of, axis=1))
    traits = chi.shape[1]
    projection = projection[:, traits:] + flipped(projection[:, :traits], "narrow", 1)
    projection = joined(long_sum(projection))
    scores_other = flipped(scores, "narrow", 1)

    inverse, moments = gram_inverse(total_variants, payload)
    return fitted_values(
        total_variants, n_array, inverse, moments, projection, extended, scores_other
    )


def solution(mesh):
    in_specs = (P(None, "wide"), P(None, "wide"), P("wide", "narrow"))
    out_specs = (P(None, both), P("wide", "narrow"))
    return jax.shard_map(whole_step, mesh=mesh, in_specs=in_specs, out_specs=out_specs, check_vma=False)
```

```python
import functools

import jax
import jax.numpy as jnp
from jax import lax
from jax.experimental import pallas as pl
from jax.experimental.pallas import tpu as pltpu
from jax.sharding import PartitionSpec as P


EPS = 1e-05
TILE = 256
LANES = 128
ROWS = 64
PAD = 8
PIVOTS = 4
VMEM_LIMIT = 16 * 1024 * 1024

highest_precision = lax.Precision.HIGHEST
both = ("wide", "narrow")
in_vmem = pl.BlockSpec(memory_space=pltpu.VMEM)
in_place = pl.BlockSpec(memory_space=pl.ANY)
in_smem = pl.BlockSpec(memory_space=pltpu.SMEM)


def cols_at(c):
    return pl.ds(pl.multiple_of(c * TILE, TILE), TILE)


def standardized(read, write, wide_values, samples):
    steps = samples // ROWS
    pivot = read(pl.ds(0, 2 * PAD)).astype(jnp.float32)[:1, :]

    def folded(values):
        return jnp.sum(values.reshape(-1, 4 * PAD, TILE), axis=0)

    first = second = jnp.zeros((4 * PAD, TILE), jnp.float32)
    for r in range(steps):
        rows = pl.ds(r * ROWS, ROWS)
        values = read(rows).astype(jnp.float32) - pivot
        wide_values[rows, :] = values
        first, second = first + folded(values), second + folded(values * values)
    first, second = (
        jnp.sum(value, axis=0, keepdims=True) / samples for value in (first, second)
    )
    variance = jnp.maximum(second - first * first, 0.0)
    scale = 1.0 / jnp.sqrt(variance + EPS)
    for r in range(steps):
        rows = pl.ds(r * ROWS, ROWS)
        write(rows, ((wide_values[rows, :] - first) * scale).astype(jnp.bfloat16))


def into(geno, tile):
    def write(rows, value):
        geno[2 * tile, rows, :] = value[:, :LANES]
        geno[2 * tile + 1, rows, :] = value[:, LANES:]

    return write


def columns_of(geno, tile):
    return jnp.concatenate([geno[2 * tile], geno[2 * tile + 1]], axis=1)


def rows_of(turned, tile):
    return jnp.concatenate([turned[tile, k] for k in range(turned.shape[1])], axis=1)


def band_weights(rows, columns, inside=None):
    samples = rows.shape[1]
    products = jnp.dot(rows, columns, preferred_element_type=jnp.float32)
    unit = 1.0 / (samples - 2)
    weights = products * products * ((1.0 + unit) / (samples * samples)) - unit
    if inside is not None:
        weights = jnp.where(inside, weights, 0.0)
    return weights.astype(jnp.bfloat16)


def along_rows(annot, weights):
    return jnp.dot(annot, weights, preferred_element_type=jnp.float32)


def along_columns(annot, weights):
    return lax.dot_general(
        annot, weights, (((1,), (1,)), ((), ())), preferred_element_type=jnp.float32
    )


def tile_offset():
    shape = (TILE, TILE)
    return lax.broadcasted_iota(jnp.int32, shape, 0) - lax.broadcasted_iota(jnp.int32, shape, 1)


def sizes(dosage):
    samples, strip = dosage.shape
    return samples, strip, strip // (2 * TILE)


def outgoing_kernel(n_ref, dosage_ref, annot_ref, first_ref, second_ref, given_annot, came):
    samples, strip = dosage_ref.shape
    annots = annot_ref.shape[0]
    n = n_ref[0]
    outs = (first_ref, second_ref)
    copies = []
    for order, out_ref in enumerate(outs):
        column = cols_at((1 - n) * (strip // TILE - 1 - order) + n * order)
        copies += [
            pltpu.make_async_copy(
                dosage_ref.at[:, column], out_ref.at[:samples, :], came.at[2 * order]
            ),
            pltpu.make_async_copy(
                annot_ref.at[:, column], given_annot.at[order], came.at[2 * order + 1]
            ),
        ]
    for copy in copies:
        copy.start()
    row = lax.broadcasted_iota(jnp.int32, (PAD, TILE), 0)
    for order, out_ref in enumerate(outs):
        out_ref[samples + annots :, :] = jnp.where(row == 0, 1.0, 0.0).astype(jnp.bfloat16)
        copies[2 * order + 1].wait()
        out_ref[samples : samples + annots, :] = (
            given_annot[order].astype(jnp.float32).astype(jnp.bfloat16)
        )
    for order in range(2):
        copies[2 * order].wait()


def outgoing_columns(n, dosage, annotations):
    samples = dosage.shape[0]
    annots = annotations.shape[0]
    out = jax.ShapeDtypeStruct((samples + annots + PAD, TILE), jnp.bfloat16)
    return pl.pallas_call(
        outgoing_kernel,
        out_shape=(out, out),
        in_specs=[in_smem, in_place, in_place],
        out_specs=(in_vmem, in_vmem),
        scratch_shapes=[pltpu.VMEM((2, annots, TILE), jnp.int32), pltpu.SemaphoreType.DMA((4,))],
        cost_estimate=pl.CostEstimate(
            flops=0, bytes_accessed=8 * samples * TILE, transcendentals=0
        ),
        name="outgoing",
    )(n, dosage, annotations)


def prepare_kernel(n_ref, annot_ref, chi_ref, annot_out_ref, counts_ref, chi_out_ref, came):
    annots, strip = annot_ref.shape
    block = strip // 2
    n = n_ref[0]
    rows = pl.ds(pl.multiple_of((1 - n) * block, block), block)
    copy = pltpu.make_async_copy(chi_ref.at[rows, :], chi_out_ref, came)
    copy.start()
    row = lax.broadcasted_iota(jnp.int32, (PAD, strip), 0)
    annot_out_ref[annots:, :] = jnp.where(row == 0, 1.0, 0.0).astype(jnp.bfloat16)
    members = annot_ref[...].astype(jnp.float32)
    annot_out_ref[:annots, :] = members.astype(jnp.bfloat16)
    counts_ref[...] = lying(jnp.sum(members, axis=1, keepdims=True))
    copy.wait()


def prepared(n, annotations, chi):
    annots, strip = annotations.shape
    return pl.pallas_call(
        prepare_kernel,
        out_shape=(
            jax.ShapeDtypeStruct((annots + PAD, strip), jnp.bfloat16),
            jax.ShapeDtypeStruct((1, annots), jnp.float32),
            jax.ShapeDtypeStruct((strip // 2, chi.shape[1]), jnp.float32),
        ),
        in_specs=[in_smem, in_vmem, in_place],
        out_specs=(in_vmem,) * 3,
        scratch_shapes=[pltpu.SemaphoreType.DMA],
        compiler_params=pltpu.CompilerParams(vmem_limit_bytes=VMEM_LIMIT),
        cost_estimate=pl.CostEstimate(
            flops=0, bytes_accessed=16 * strip * annots, transcendentals=0
        ),
        name="prepare",
    )(n, annotations, chi)


def own_kernel(n_ref, dosage_ref, annot_ref, sums_ref, turned_ref, geno, wide_values):
    samples, strip = dosage_ref.shape
    mine = strip // (2 * TILE)
    n = n_ref[0]
    sums_ref[...] = jnp.zeros_like(sums_ref)

    def standardize(t):
        standardized(
            lambda rows: dosage_ref[rows, cols_at(n * mine + t)],
            into(geno, t),
            wide_values.at[t % 2],
            samples,
        )
        for k in range(samples // LANES):
            for part in range(2):
                turned_ref[t, k, part * LANES : (part + 1) * LANES, :] = geno[
                    2 * t + part, k * LANES : (k + 1) * LANES, :
                ].T

    standardize(0)
    for y in range(mine):
        if y + 1 < mine:
            standardize(y + 1)
        for x in range(y + 1):
            weights = band_weights(rows_of(turned_ref, x), columns_of(geno, y))
            sums_ref[:, y * TILE : (y + 1) * TILE] += along_rows(
                annot_ref[:, cols_at(n * mine + x)], weights
            )
            if x < y:
                sums_ref[:, x * TILE : (x + 1) * TILE] += along_columns(
                    annot_ref[:, cols_at(n * mine + y)], weights
                )


def other_kernel(
    slots, n_ref, dosage_ref, annot_ref, turned_ref, sums_in, sums_ref, geno, wide_values
):
    samples, strip = dosage_ref.shape
    mine = strip // (2 * TILE)
    n = n_ref[0]

    def nearest(s):
        return (1 - n) * s + n * (mine - 1 - s)

    sums_ref[...] = sums_in[...]
    inside = (1 - 2 * n) * tile_offset() >= 0

    def standardize(s):
        standardized(
            lambda rows: dosage_ref[rows, cols_at((1 - n) * mine + nearest(s))],
            into(geno, s),
            wide_values.at[s % 2],
            samples,
        )

    standardize(slots[0])
    for s in slots:
        if s + 1 in slots:
            standardize(s + 1)
        for h in range(s, mine):
            weights = band_weights(
                rows_of(turned_ref, nearest(h)), columns_of(geno, s), inside if h == s else None
            )
            sums_ref[:, cols_at(nearest(h))] += along_columns(
                annot_ref[:, cols_at((1 - n) * mine + nearest(s))], weights
            )


def own_sums(n, dosage, annot):
    samples, strip, mine = sizes(dosage)
    chunks = samples // LANES
    turned = (mine, chunks, TILE, LANES)
    return pl.pallas_call(
        own_kernel,
        out_shape=(
            jax.ShapeDtypeStruct((annot.shape[0], strip // 2), jnp.float32),
            jax.ShapeDtypeStruct(turned, jnp.bfloat16),
        ),
        in_specs=[in_smem, in_vmem, in_vmem],
        out_specs=(in_vmem, in_vmem),
        scratch_shapes=strip_scratch(dosage),
        cost_estimate=strip_cost(dosage),
        compiler_params=pltpu.CompilerParams(vmem_limit_bytes=VMEM_LIMIT),
        name="own_sums",
    )(n, dosage, annot)


def other_sums(slots, n, dosage, annot, turned, sums):
    return pl.pallas_call(
        functools.partial(other_kernel, slots),
        out_shape=jax.ShapeDtypeStruct(sums.shape, jnp.float32),
        in_specs=[in_smem] + [in_vmem] * 4,
        out_specs=in_vmem,
        scratch_shapes=strip_scratch(dosage),
        cost_estimate=strip_cost(dosage),
        compiler_params=pltpu.CompilerParams(vmem_limit_bytes=VMEM_LIMIT),
        name="other_sums",
    )(n, dosage, annot, turned, sums)


def strip_scratch(dosage):
    samples, _, mine = sizes(dosage)
    return [
        pltpu.VMEM((2 * mine, samples, LANES), jnp.bfloat16),
        pltpu.VMEM((2, samples, TILE), jnp.float32),
    ]


def strip_cost(dosage):
    samples, strip, _ = sizes(dosage)
    return pl.CostEstimate(
        flops=samples * strip * strip // 2, bytes_accessed=2 * samples * strip, transcendentals=0
    )


def rim_kernel(
    order, n_ref, arrived_ref, turned_ref, annot_ref, sums_in, *refs
):
    *earlier, sums_ref, back_ref, geno, wide_values = refs
    columns = slice(order * TILE, (order + 1) * TILE)
    mine = turned_ref.shape[0]
    samples = geno.shape[1]
    n = n_ref[0]
    sums_ref[...] = sums_in[...]
    back_ref[...] = jnp.zeros_like(back_ref)
    for ref in earlier:
        back_ref[:, : ref.shape[1]] = ref[...]
    standardized(lambda rows: arrived_ref[rows, :], into(geno, 0), wide_values, samples)

    def add(y, inside=None):
        weights = band_weights(rows_of(turned_ref, y), columns_of(geno, 0), inside)
        sums_ref[:, cols_at(y)] += along_columns(arrived_ref[samples:, :], weights)
        back_ref[:, columns] += along_rows(annot_ref[:, cols_at(n * mine + y)], weights)

    low, high = order, mine - 1 - order
    add((1 - n) * high + n * low, (1 - 2 * n) * tile_offset() <= 0)
    width, last = mine // 2, mine - mine // 4
    for y in range(mine):
        first = y < high and (y >= width or high >= last)
        second = low < y < last
        if first or second:

            @pl.when(True if first and second else (n == 0 if first else n == 1))
            def _(y=y):
                add(y)


def rim_sums(order, n, arrived, turned, annot, sums, *earlier):
    mine, chunks, _, _ = turned.shape
    samples = chunks * LANES
    return pl.pallas_call(
        functools.partial(rim_kernel, order),
        out_shape=(
            jax.ShapeDtypeStruct(sums.shape, jnp.float32),
            jax.ShapeDtypeStruct((sums.shape[0], (order + 1) * TILE), jnp.float32),
        ),
        in_specs=[in_smem] + [in_vmem] * (4 + len(earlier)),
        out_specs=(in_vmem, in_vmem),
        scratch_shapes=[
            pltpu.VMEM((2, samples, LANES), jnp.bfloat16),
            pltpu.VMEM((samples, TILE), jnp.float32),
        ],
        compiler_params=pltpu.CompilerParams(vmem_limit_bytes=VMEM_LIMIT),
        cost_estimate=pl.CostEstimate(
            flops=2 * samples * TILE * mine * TILE,
            bytes_accessed=2 * samples * TILE * (mine + 1),
            transcendentals=0,
        ),
        name="rim_sums",
    )(n, arrived, turned, annot, sums, *earlier)


def eye(size):
    shape = (size, size)
    return lax.broadcasted_iota(jnp.int32, shape, 0) == lax.broadcasted_iota(jnp.int32, shape, 1)


def upright(row):
    size = row.shape[1]
    return jnp.sum(jnp.where(eye(size), jnp.broadcast_to(row, (size, size)), 0.0), axis=1, keepdims=True)


def lying(column):
    size = column.shape[0]
    return jnp.sum(
        jnp.where(eye(size), jnp.broadcast_to(column, (size, size)), 0.0), axis=0, keepdims=True
    )


def moments_kernel(total_variants, n_ref, w_ref, counts_ref, sums_ref, back_ref, scores_ref, payload_ref, whole):
    annots = counts_ref.shape[1]
    block = sums_ref.shape[1]
    mine = block // TILE
    n = n_ref[0]
    slot = 2 * w_ref[0] + n
    whole[...] = sums_ref[...]
    for order in range(back_ref.shape[1] // TILE):
        whole[:, cols_at((1 - n) * order + n * (mine - 1 - order))] += back_ref[
            :, order * TILE : (order + 1) * TILE
        ]
    shares = upright(counts_ref[...]) / total_variants
    high = (1.0 - shares).astype(jnp.bfloat16).astype(jnp.float32)
    low = (0.0 - shares).astype(jnp.bfloat16).astype(jnp.float32)
    members = whole[:annots, :]
    scores = high * members + low * (whole[annots : annots + 1, :] - members)
    scores_ref[:annots, :] = scores
    row = lax.broadcasted_iota(jnp.int32, (2 * PAD, block), 0)
    scores_ref[annots:, :] = jnp.where(row == 0, 1.0, 0.0)
    mean = jnp.sum(scores, axis=1, keepdims=True) / block
    deviation = scores - mean
    payload_ref[:annots, :] = lax.dot_general(
        deviation,
        deviation,
        (((1,), (1,)), ((), ())),
        precision=highest_precision,
        preferred_element_type=jnp.float32,
    )
    slots = payload_ref.shape[0] - annots
    at = lax.broadcasted_iota(jnp.int32, (slots, annots), 0)
    payload_ref[annots:, :] = jnp.where(at == slot, lying(mean), 0.0)


def moments_of(total_variants, slots, n, w, counts, sums, back):
    annots = counts.shape[1]
    block = sums.shape[1]
    return pl.pallas_call(
        functools.partial(moments_kernel, total_variants),
        out_shape=(
            jax.ShapeDtypeStruct((annots + 2 * PAD, block), jnp.float32),
            jax.ShapeDtypeStruct((annots + slots, annots), jnp.float32),
        ),
        in_specs=[in_smem] * 2 + [in_vmem] * 3,
        out_specs=(in_vmem, in_vmem),
        scratch_shapes=[pltpu.VMEM(sums.shape, jnp.float32)],
        compiler_params=pltpu.CompilerParams(vmem_limit_bytes=VMEM_LIMIT),
        cost_estimate=pl.CostEstimate(
            flops=12 * annots * annots * block, bytes_accessed=12 * annots * block, transcendentals=0
        ),
        name="moments",
    )(n, w, counts, sums, back)


def inverse_kernel(divisor, payload_ref, inverse_ref, moments_ref):
    size = payload_ref.shape[1]
    slots = payload_ref.shape[0] - size
    means = payload_ref[size:, :]
    mean = jnp.sum(means, axis=0, keepdims=True) / slots
    between = means - mean
    covariance = (
        payload_ref[:size, :]
        + lax.dot_general(
            between,
            between,
            (((0,), (0,)), ((), ())),
            precision=highest_precision,
            preferred_element_type=jnp.float32,
        )
        * (divisor // slots)
    ) / divisor
    row = lax.broadcasted_iota(jnp.int32, (size, size), 0)
    lane = lax.broadcasted_iota(jnp.int32, (size, size), 1)
    diagonal = jnp.where(row == lane, covariance, 0.0)
    across = 1.0 / jnp.sqrt(jnp.sum(diagonal, axis=0, keepdims=True) + EPS)
    down = 1.0 / jnp.sqrt(jnp.sum(diagonal, axis=1, keepdims=True) + EPS)
    mean_down = jnp.sum(jnp.where(row == lane, jnp.broadcast_to(mean, (size, size)), 0.0), axis=1, keepdims=True)
    moments_ref[...] = jnp.where(lane == 0, mean_down, down)
    gram = covariance * down * across
    groups = [gram[PAD * g : PAD * (g + 1), :] for g in range(size // PAD)]
    lane_of = lax.broadcasted_iota(jnp.int32, (1, size), 1)
    row_of = lax.broadcasted_iota(jnp.int32, (PAD, size), 0)

    def pair_inverse(a, b, c):
        scale = 1.0 / (a * c - b * b)
        return c * scale, -b * scale, a * scale

    for k in range(0, size, PIVOTS):
        g, i = divmod(k, PAD)
        spread = [
            [jnp.broadcast_to(old[:, k + j : k + j + 1], (PAD, size)) for j in range(PIVOTS)]
            for old in groups
        ]
        m = [[spread[g][c][i + r : i + r + 1, :] for c in range(PIVOTS)] for r in range(PIVOTS)]
        rows = [
            groups[g][i + j : i + j + 1, :] - jnp.where(lane_of == k + j, 1.0, 0.0)
            for j in range(PIVOTS)
        ]
        a, b, c = pair_inverse(m[0][0], m[0][1], m[1][1])
        u = a * rows[0] + b * rows[1], b * rows[0] + c * rows[1]
        v = [(a * m[0][j] + b * m[1][j], b * m[0][j] + c * m[1][j]) for j in (2, 3)]
        rest = [rows[j] - m[0][j] * u[0] - m[1][j] * u[1] for j in (2, 3)]
        d, e, f = pair_inverse(
            m[2][2] - m[0][2] * v[0][0] - m[1][2] * v[0][1],
            m[2][3] - m[0][2] * v[1][0] - m[1][2] * v[1][1],
            m[3][3] - m[0][3] * v[1][0] - m[1][3] * v[1][1],
        )
        third = d * rest[0] + e * rest[1]
        fourth = e * rest[0] + f * rest[1]
        solved = [
            u[0] - v[0][0] * third - v[1][0] * fourth,
            u[1] - v[0][1] * third - v[1][1] * fourth,
            third,
            fourth,
        ]
        solved = [jnp.broadcast_to(value, (PAD, size)) for value in solved]
        for h, old in enumerate(groups):
            for j in range(PIVOTS):
                old = old - spread[h][j] * solved[j]
                if h == g:
                    old = old + jnp.where(row_of == i + j, solved[j], 0.0)
            groups[h] = old
    swept = jnp.concatenate(groups, axis=0)
    inverse = jnp.where(row == lane, 2.0, 0.0) - swept
    inverse_ref[...] = inverse * down * across / divisor


def gram_inverse(divisor, payload):
    size = payload.shape[1]
    square = jax.ShapeDtypeStruct((size, size), jnp.float32)
    return pl.pallas_call(
        functools.partial(inverse_kernel, divisor),
        out_shape=(square, square),
        in_specs=[in_vmem],
        out_specs=(in_vmem, in_vmem),
        compiler_params=pltpu.CompilerParams(vmem_limit_bytes=VMEM_LIMIT),
        cost_estimate=pl.CostEstimate(flops=20_000_000_000, bytes_accessed=4 * size * size, transcendentals=0),
        name="gram_inverse",
    )(payload)


def halves(value):
    upper = value.astype(jnp.bfloat16)
    return upper, (value - upper.astype(jnp.float32)).astype(jnp.bfloat16)


def fit_kernel(
    divisor, n_ref, inverse_ref, moments_ref, proj_ref, scores_ref, other_ref, own_ref, fitted_ref,
    own, fitted, went,
):
    annots, block = own.shape
    n = n_ref[0]
    mean = moments_ref[:, 0:1]
    centred = scores_ref[:annots, :] - mean
    own[...] = centred * moments_ref[:, 1:2]
    copies = [pltpu.make_async_copy(own, own_ref, went.at[0])]
    copies[0].start()
    sums = proj_ref[annots : annots + 1, :]
    coefficient = jnp.dot(
        inverse_ref[...],
        proj_ref[:annots, :] - mean * sums,
        precision=highest_precision,
        preferred_element_type=jnp.float32,
    )
    upper, lower = halves(coefficient)
    right = jnp.concatenate([upper, upper, lower], axis=0)
    for half, values in enumerate((centred, other_ref[...] - mean)):
        upper, lower = halves(values)
        left = jnp.concatenate([upper, lower, upper], axis=0)
        place = (1 - half) * n + half * (1 - n)
        for c in range(block // TILE):
            rows = pl.ds(half * block + c * TILE, TILE)
            fitted[rows, :] = sums / divisor + lax.dot_general(
                left[:, c * TILE : (c + 1) * TILE],
                right,
                (((0,), (0,)), ((), ())),
                preferred_element_type=jnp.float32,
            )
            target = pl.ds(pl.multiple_of(place * block + c * TILE, TILE), TILE)
            copies.append(
                pltpu.make_async_copy(
                    fitted.at[rows, :], fitted_ref.at[target, :], went.at[len(copies)]
                )
            )
            copies[-1].start()
    for copy in copies:
        copy.wait()


def fitted_values(divisor, n, inverse, moments, projection, scores, scores_other):
    annots, block = scores_other.shape
    traits = projection.shape[1]
    return pl.pallas_call(
        functools.partial(fit_kernel, divisor),
        out_shape=(
            jax.ShapeDtypeStruct((annots, block), jnp.float32),
            jax.ShapeDtypeStruct((2 * block, traits), jnp.float32),
        ),
        in_specs=[in_smem] + [in_vmem] * 5,
        out_specs=(in_place, in_place),
        scratch_shapes=[
            pltpu.VMEM((annots, block), jnp.float32),
            pltpu.VMEM((2 * block, traits), jnp.float32),
            pltpu.SemaphoreType.DMA((1 + 2 * (block // TILE),)),
        ],
        compiler_params=pltpu.CompilerParams(vmem_limit_bytes=VMEM_LIMIT),
        cost_estimate=pl.CostEstimate(
            flops=4 * annots * block * traits, bytes_accessed=8 * block * traits, transcendentals=0
        ),
        name="fitted_values",
    )(n, inverse, moments, projection, scores, scores_other)


def flipped(value, axis, bit):
    length = lax.axis_size(axis)
    return lax.ppermute(value, axis, [(i, i ^ bit) for i in range(length)])


def wide_bits():
    length = lax.axis_size("wide")
    bits = []
    bit = 1
    while bit < length:
        bits.append(bit)
        bit *= 2
    return bits


def added_kernel(first_ref, second_ref, out_ref):
    out_ref[...] = first_ref[...] + second_ref[...]


def added(first, second):
    return pl.pallas_call(
        added_kernel,
        out_shape=jax.ShapeDtypeStruct(first.shape, first.dtype),
        in_specs=[in_vmem, in_vmem],
        out_specs=in_vmem,
        compiler_params=pltpu.CompilerParams(vmem_limit_bytes=VMEM_LIMIT // 4),
        name="added",
    )(first, second)


def wide_sum(value):
    bits = wide_bits()
    for bit in bits[:1] + bits[2:] + bits[1:2]:
        value = added(value, flipped(value, "wide", bit))
    return value


def split(value):
    half = value.shape[0] // 2
    low = lax.axis_index("wide") % 2
    kept = lax.dynamic_slice_in_dim(value, low * half, half, 0)
    given = lax.dynamic_slice_in_dim(value, (1 - low) * half, half, 0)
    return kept + flipped(given, "wide", 1)


def long_sum(value):
    for bit in wide_bits()[1:]:
        value = value + flipped(value, "wide", bit)
    return value


def joined(kept):
    low = lax.axis_index("wide") % 2
    other = flipped(kept, "wide", 1)
    return jnp.where(low == 0, jnp.concatenate([kept, other], 0), jnp.concatenate([other, kept], 0))


def whole_step(dosage, annotations, test_statistic_table):
    _, strip = dosage.shape
    annots = annotations.shape[0]
    wide = lax.axis_size("wide")
    total_variants = wide * strip
    w = lax.axis_index("wide")
    n = lax.axis_index("narrow")
    block = strip // 2
    n_array = jnp.reshape(n, (1,)).astype(jnp.int32)

    rim_pairs = []
    back_pairs = []
    for i in range(wide - 1):
        rim_pairs += [(2 * i, 2 * i + 2), (2 * i + 3, 2 * i + 1)]
        back_pairs += [(2 * i + 1, 2 * i + 2), (2 * i + 2, 2 * i + 1)]
    chi = test_statistic_table
    arrived = []
    for outgoing in outgoing_columns(n_array, dosage, annotations):
        arrived.append(lax.ppermute(outgoing, both, rim_pairs))
    annot, counts, chi_given = prepared(n_array, annotations, chi)
    chi_other = flipped(chi_given, "narrow", 1)
    counts = wide_sum(counts)
    sums, turned = own_sums(n_array, dosage, annot)
    tiles = block // TILE
    pieces = tuple(range(tiles // 4)), tuple(range(tiles // 4, tiles))
    back = []
    for order in range(2):
        sums, part = rim_sums(order, n_array, arrived[order], turned, annot, sums, *back)
        back.append(part)
        sums = other_sums(pieces[order], n_array, dosage, annot, turned, sums)
    back = lax.ppermute(part, both, back_pairs)

    w_array = jnp.reshape(w, (1,)).astype(jnp.int32)
    extended, payload = moments_of(total_variants, 2 * wide, n_array, w_array, counts, sums, back)
    scores = extended[:annots]
    payload = split(payload)
    payload = payload + flipped(payload, "narrow", 1)
    payload = joined(long_sum(payload))

    chi_own = lax.dynamic_slice_in_dim(chi, n * block, block, 0)
    halves_of = [
        jnp.dot(extended, values, precision=lax.Precision.HIGH, preferred_element_type=jnp.float32)
        for values in (chi_other, chi_own)
    ]
    projection = split(jnp.concatenate(halves_of, axis=1))
    traits = chi.shape[1]
    projection = projection[:, traits:] + flipped(projection[:, :traits], "narrow", 1)
    projection = joined(long_sum(projection))
    scores_other = flipped(scores, "narrow", 1)

    inverse, moments = gram_inverse(total_variants, payload)
    return fitted_values(
        total_variants, n_array, inverse, moments, projection, extended, scores_other
    )


def solution(mesh):
    in_specs = (P(None, "wide"), P(None, "wide"), P("wide", "narrow"))
    out_specs = (P(None, both), P("wide", "narrow"))
    return jax.shard_map(whole_step, mesh=mesh, in_specs=in_specs, out_specs=out_specs, check_vma=False)
```
